128 devices in a mesh: branch: 2 (over y_lo), rows: 64 (over x, y_hi, z, core).
Axes of the slice: x: 4, y: 4 (y_hi: 2, y_lo: 2; y = y_hi * 2 + y_lo), z: 4, core: 2. Of those that a mesh axis runs over, the one named last changes fastest.
Arguments:
- homolog_features: bfloat16 [128, 1024, 256], P(('branch', 'rows')), may hold values from -6 to 6
- pairwise_input: bfloat16 [1024, 1024, 128], P('rows', 'branch'), may hold values from -6 to 6
- transition_expand_matrix: bfloat16 [256, 1024], replicated, may hold values from -0.375 to 0.375
- transition_contract_matrix: bfloat16 [1024, 256], replicated, may hold values from -0.1875 to 0.1875
- factor_pair_matrices: bfloat16 [256, 64], replicated, may hold values from -0.375 to 0.375
- outer_output_weight: bfloat16 [1024, 128], replicated, may hold values from -0.75 to 0.75
- triangle_projection_weight: bfloat16 [128, 640], replicated, may hold values from -0.5 to 0.5
- triangle_output_weight: bfloat16 [128, 128], replicated, may hold values from -1 to 1
- pairwise_up_weight: bfloat16 [128, 512], replicated, may hold values from -0.5 to 0.5
- pairwise_down_weight: bfloat16 [512, 128], replicated, may hold values from -0.25 to 0.25
Outputs:
- refreshed_homolog_features: bfloat16 [128, 1024, 256], P(('branch', 'rows'))
- pairwise_output: bfloat16 [1024, 1024, 128], P('rows', 'branch')
The draws below stay inside these ranges and needn't reach their ends.
All inputs are finite; a program needn't handle non-finite values.
Results may differ from the reference program's by a relative error of at most 0.0085.
Values may be sent and summed in bfloat16 or wider, within the bound.
A program may use at most 128 MiB of HBM per device.

```python
import jax
import jax.numpy as jnp
from jax import lax

FEATURE_DEPTH = 256
EXPANDED_DEPTH = 1024
FACTOR_DEPTH = 32
PAIR = 128
PAIR_HID = 512
ROW_DEV = 16
AMINO_TOTAL = 1024
HOMOLOG_TOTAL = 128
N_ROWS = 64


def block_levels(key, shape, shards, low, top_value):
    def one(axis_at, blocks):
        draws = jax.random.uniform(jax.random.fold_in(jax.random.fold_in(key, 6), axis_at), (blocks,), jnp.float32, low / len(shards), top_value / len(shards))
        return jnp.repeat(jnp.exp(draws), shape[axis_at] // blocks).reshape((-1,) + (1,) * (len(shape) - axis_at - 1))

    factor_of = one(*shards[0])
    for cut in shards[1:]:
        factor_of = factor_of * one(*cut)
    return factor_of


def normal_values(key, shape, deviation, bound, shards=(), held_as=jnp.bfloat16):
    drawn = jax.random.normal(key, shape, jnp.float32) * deviation
    if len(shards) > 0:
        drawn = block_levels(key, shape, shards, -0.22, 0.18) * drawn
    return jnp.clip(drawn, min=-bound, max=bound).astype(held_as)


def setup_inputs(seed: int = 0) -> dict:
    key_list = jax.random.split(jax.random.key(seed), 11)
    return {
        "homolog_features": normal_values(key_list[0], (HOMOLOG_TOTAL, AMINO_TOTAL, FEATURE_DEPTH), 1.0, 6.0, ((0, 128),)),
        "pairwise_input": normal_values(key_list[1], (AMINO_TOTAL, AMINO_TOTAL, PAIR), 1.0, 6.0, ((0, 64), (1, 2))),
        "transition_expand_matrix": normal_values(key_list[2], (FEATURE_DEPTH, EXPANDED_DEPTH), FEATURE_DEPTH ** -0.5, 0.375),
        "transition_contract_matrix": normal_values(key_list[3], (EXPANDED_DEPTH, FEATURE_DEPTH), EXPANDED_DEPTH ** -0.5, 0.1875),
        "factor_pair_matrices": normal_values(key_list[4], (FEATURE_DEPTH, 2 * FACTOR_DEPTH), FEATURE_DEPTH ** -0.5, 0.375),
        "outer_output_weight": normal_values(key_list[5], (FACTOR_DEPTH * FACTOR_DEPTH, PAIR), (2 * FACTOR_DEPTH) ** -0.5, 0.75),
        "triangle_projection_weight": normal_values(key_list[6], (PAIR, 5 * PAIR), PAIR ** -0.5, 0.5),
        "triangle_output_weight": normal_values(key_list[7], (PAIR, PAIR), (PAIR // 4) ** -0.5, 1.0),
        "pairwise_up_weight": normal_values(key_list[8], (PAIR, PAIR_HID), PAIR ** -0.5, 0.5),
        "pairwise_down_weight": normal_values(key_list[9], (PAIR_HID, PAIR), PAIR_HID ** -0.5, 0.25),
    }


def standardize_features(values, dimension):
    average = lax.optimization_barrier(jnp.mean(values, axis=dimension, keepdims=True))
    centered = values - average
    variance = lax.optimization_barrier(jnp.mean(centered * centered, axis=dimension, keepdims=True))
    return centered * lax.rsqrt(variance + 1e-05)

def rounded(values):
    return lax.optimization_barrier(values.astype(jnp.bfloat16)).astype(jnp.float32)

def reference(homolog_features, pairwise_input, transition_expand_matrix, transition_contract_matrix, factor_pair_matrices, outer_output_weight, triangle_projection_weight, triangle_output_weight, pairwise_up_weight, pairwise_down_weight):
    homolog_real_matrix = homolog_features.astype(jnp.float32)
    standardized_homologs = standardize_features(homolog_real_matrix, -1).astype(jnp.bfloat16).reshape(HOMOLOG_TOTAL * AMINO_TOTAL, FEATURE_DEPTH)
    expanded_activations = jax.nn.relu(jnp.dot(standardized_homologs, transition_expand_matrix, preferred_element_type=jnp.float32)).astype(jnp.bfloat16)
    refreshed_homolog_features = (homolog_real_matrix + jnp.dot(expanded_activations, transition_contract_matrix, preferred_element_type=jnp.float32).reshape(HOMOLOG_TOTAL, AMINO_TOTAL, FEATURE_DEPTH)).astype(jnp.bfloat16)
    standardized_for_factors = standardize_features(refreshed_homolog_features.astype(jnp.float32), -1).astype(jnp.bfloat16).reshape(HOMOLOG_TOTAL * AMINO_TOTAL, FEATURE_DEPTH)
    projected = jnp.dot(standardized_for_factors, factor_pair_matrices, preferred_element_type=jnp.float32).reshape(HOMOLOG_TOTAL, AMINO_TOTAL, 2 * FACTOR_DEPTH)
    left_side = projected[..., :FACTOR_DEPTH].astype(jnp.bfloat16)
    right_side = projected[..., FACTOR_DEPTH:].astype(jnp.bfloat16)
    right_flat = right_side.reshape(HOMOLOG_TOTAL, AMINO_TOTAL * FACTOR_DEPTH)
    outer_weight = outer_output_weight.astype(jnp.float32).reshape(FACTOR_DEPTH, FACTOR_DEPTH, PAIR)
    left_tiles = jnp.moveaxis(left_side.reshape(HOMOLOG_TOTAL, N_ROWS, ROW_DEV * FACTOR_DEPTH), 1, 0)
    pair_tiles = pairwise_input.reshape(N_ROWS, ROW_DEV, AMINO_TOTAL, PAIR)
    tri_weight = triangle_projection_weight.astype(jnp.float32)

    def tri_inputs(pair_tile):
        pair_norm = rounded(standardize_features(pair_tile.astype(jnp.float32), -1))
        proj_tile = jnp.einsum('ikd,de->eik', pair_norm, tri_weight[:, :4 * PAIR])
        left_tri = (jax.nn.sigmoid(proj_tile[PAIR:2 * PAIR]) * proj_tile[:PAIR]).astype(jnp.bfloat16)
        right_tri = (jax.nn.sigmoid(proj_tile[3 * PAIR:]) * proj_tile[2 * PAIR:3 * PAIR]).astype(jnp.bfloat16)
        return (left_tri, right_tri)
    left_stack, right_stack = lax.map(tri_inputs, pair_tiles)
    left_chan = jnp.moveaxis(left_stack, 1, 0).reshape(PAIR, AMINO_TOTAL, AMINO_TOTAL)
    right_chan = jnp.moveaxis(right_stack, 1, 0).reshape(PAIR, AMINO_TOTAL, AMINO_TOTAL)

    def channel_product(operands):
        left_one, right_one = operands
        return jnp.dot(left_one, right_one.T, preferred_element_type=jnp.float32).astype(jnp.bfloat16)
    product = lax.map(channel_product, (left_chan, right_chan))
    product_tiles = jnp.moveaxis(product.reshape(PAIR, N_ROWS, ROW_DEV, AMINO_TOTAL), 1, 0)

    def tile_output(operands):
        pair_tile, product_tile, left_tile = operands
        pair_float = pair_tile.astype(jnp.float32)
        pair_norm = rounded(standardize_features(pair_float, -1))
        gate_vals = jax.nn.sigmoid(jnp.einsum('ijd,de->ije', pair_norm, tri_weight[:, 4 * PAIR:]))
        prod_norm = rounded(standardize_features(product_tile.astype(jnp.float32), 0))
        tri_update = jnp.einsum('cij,ce->ije', prod_norm, triangle_output_weight.astype(jnp.float32))
        pair_mid = pair_float + gate_vals * tri_update
        mid_norm = rounded(standardize_features(pair_mid, -1))
        pair_hidden = rounded(jax.nn.relu(jnp.einsum('ijd,dh->ijh', mid_norm, pairwise_up_weight.astype(jnp.float32))))
        pair_mid = pair_mid + jnp.einsum('ijh,hd->ijd', pair_hidden, pairwise_down_weight.astype(jnp.float32))
        outer_vals = jnp.dot(left_tile.T, right_flat, preferred_element_type=jnp.float32)
        outer_vals = rounded(outer_vals / HOMOLOG_TOTAL).reshape(ROW_DEV, FACTOR_DEPTH, AMINO_TOTAL, FACTOR_DEPTH)
        outer_update = jnp.einsum('icjd,cde->ije', outer_vals, outer_weight)
        return (pair_mid + outer_update).astype(jnp.bfloat16)
    pairwise_output = lax.map(tile_output, (pair_tiles, product_tiles, left_tiles)).reshape(AMINO_TOTAL, AMINO_TOTAL, PAIR)
    return (refreshed_homolog_features, pairwise_output)
```

```python
import jax
import jax.numpy as jnp
from jax import lax
from jax.sharding import PartitionSpec as P


def standardize_features(values, dimension):
    average = jnp.mean(values, axis=dimension, keepdims=True)
    centered = values - average
    variance = jnp.mean(centered * centered, axis=dimension, keepdims=True)
    return centered * lax.rsqrt(variance + 1e-05)


def alignment_branch(
    homolog_features, transition_expand_matrix, transition_contract_matrix, factor_pair_matrices
):
    local_rows, sequence_length, channel_width = homolog_features.shape
    homolog_real_matrix = homolog_features.astype(jnp.float32)
    standardized_homologs = (
        standardize_features(homolog_real_matrix, -1)
        .astype(jnp.bfloat16)
        .reshape(local_rows * sequence_length, channel_width)
    )
    expanded_activations = jax.nn.relu(
        jnp.dot(standardized_homologs, transition_expand_matrix, preferred_element_type=jnp.float32)
    ).astype(jnp.bfloat16)
    refreshed_homolog_features = (
        homolog_real_matrix
        + jnp.dot(
            expanded_activations, transition_contract_matrix, preferred_element_type=jnp.float32
        ).reshape(homolog_features.shape)
    ).astype(jnp.bfloat16)
    standardized_for_factors = (
        standardize_features(refreshed_homolog_features.astype(jnp.float32), -1)
        .astype(jnp.bfloat16)
        .reshape(local_rows * sequence_length, channel_width)
    )
    projected = jnp.dot(
        standardized_for_factors, factor_pair_matrices, preferred_element_type=jnp.float32
    ).reshape(local_rows, sequence_length, -1)
    channels = projected.shape[-1] // 2
    left_side = projected[..., :channels].astype(jnp.bfloat16)
    right_side = jnp.swapaxes(projected[..., channels:].astype(jnp.bfloat16), 1, 2)
    left_pair = lax.all_gather(left_side, "branch", axis=0, tiled=True)
    left_gathered = lax.all_to_all(left_pair, "rows", split_axis=1, concat_axis=0, tiled=True)
    right_pair = lax.all_to_all(right_side, "branch", split_axis=2, concat_axis=0, tiled=True)
    right_gathered = lax.all_gather(right_pair, "rows", axis=0, tiled=True)
    return (refreshed_homolog_features, left_gathered, right_gathered)


def send_whole(tri_left, tri_right):
    both = ("branch", "rows")
    return (
        lax.all_to_all(tri_left, both, split_axis=0, concat_axis=0, tiled=True),
        lax.all_to_all(tri_right, both, split_axis=0, concat_axis=0, tiled=True),
    )


def send_back(product):
    return lax.all_to_all(product, ("branch", "rows"), split_axis=0, concat_axis=0, tiled=True)


def pair_branch(
    pairwise_input,
    triangle_projection_weight,
    triangle_output_weight,
    pairwise_up_weight,
    pairwise_down_weight,
):
    tile_rows, columns, chans = pairwise_input.shape
    pair_float = pairwise_input.astype(jnp.float32)
    pair_norm = standardize_features(pair_float, -1).astype(jnp.bfloat16)
    norm_flat = pair_norm.reshape(tile_rows * columns, chans)
    proj_flat = lax.dot_general(
        triangle_projection_weight,
        norm_flat,
        (((0,), (1,)), ((), ())),
        preferred_element_type=jnp.float32,
    )
    proj_tile = proj_flat[: 4 * chans].reshape(4 * chans, tile_rows, columns)
    gate_vals = jax.nn.sigmoid(proj_flat[4 * chans :])
    tri_left = (jax.nn.sigmoid(proj_tile[chans : 2 * chans]) * proj_tile[:chans]).astype(
        jnp.bfloat16
    )
    tri_right = (jax.nn.sigmoid(proj_tile[3 * chans :]) * proj_tile[2 * chans : 3 * chans]).astype(
        jnp.bfloat16
    )
    left_chan, right_chan = send_whole(tri_left, tri_right)
    halves = lax.axis_size("branch")
    left_src = left_chan.reshape(halves, -1, columns)
    right_src = right_chan.reshape(halves, halves, -1, columns)
    product = jnp.einsum(
        "bik,bhjk->hij", left_src, right_src, preferred_element_type=jnp.float32
    ).astype(jnp.bfloat16)
    product_tile = send_back(product.reshape(-1, tile_rows, columns))
    prod_norm = (
        standardize_features(product_tile.astype(jnp.float32), 0)
        .astype(jnp.bfloat16)
        .reshape(chans, tile_rows * columns)
    )
    tri_update = lax.dot_general(
        triangle_output_weight,
        prod_norm,
        (((0,), (0,)), ((), ())),
        preferred_element_type=jnp.float32,
    )
    gated_update = jnp.transpose(gate_vals * tri_update).reshape(tile_rows, columns, chans)
    pair_mid = pair_float + gated_update
    mid_norm = standardize_features(pair_mid, -1).astype(jnp.bfloat16)
    pair_hidden = jax.nn.relu(
        jnp.einsum("ijd,dh->ijh", mid_norm, pairwise_up_weight, preferred_element_type=jnp.float32)
    ).astype(jnp.bfloat16)
    return pair_mid + jnp.einsum(
        "ijh,hd->ijd", pair_hidden, pairwise_down_weight, preferred_element_type=jnp.float32
    )


def outer_product(left_gathered, right_gathered, outer_output_weight):
    total_rows, tile_rows, channels = left_gathered.shape
    columns = right_gathered.shape[2]
    span_cols = 128
    left_flat = left_gathered.reshape(total_rows, tile_rows * channels)
    pieces = []
    for offset in range(0, columns, span_cols):
        right_piece = right_gathered[:, :, offset : offset + span_cols].reshape(
            total_rows, channels * span_cols
        )
        outer_vals = lax.dot_general(
            left_flat, right_piece, (((0,), (0,)), ((), ())), preferred_element_type=jnp.float32
        )
        outer_vals = (
            (outer_vals / total_rows)
            .astype(jnp.bfloat16)
            .reshape(tile_rows, channels * channels, span_cols)
        )
        pieces.append(
            lax.dot_general(
                outer_output_weight,
                outer_vals,
                (((0,), (1,)), ((), ())),
                preferred_element_type=jnp.float32,
            )
        )
    outer_eij = jnp.concatenate(pieces, axis=2)
    return jnp.transpose(outer_eij, (1, 2, 0))


def on_device(
    homolog_features,
    pairwise_input,
    transition_expand_matrix,
    transition_contract_matrix,
    factor_pair_matrices,
    outer_output_weight,
    triangle_projection_weight,
    triangle_output_weight,
    pairwise_up_weight,
    pairwise_down_weight,
):
    refreshed_homolog_features, left_gathered, right_gathered = alignment_branch(
        homolog_features, transition_expand_matrix, transition_contract_matrix, factor_pair_matrices
    )
    pair_mid = pair_branch(
        pairwise_input,
        triangle_projection_weight,
        triangle_output_weight,
        pairwise_up_weight,
        pairwise_down_weight,
    )
    outer_update = outer_product(left_gathered, right_gathered, outer_output_weight)
    pairwise_output = (pair_mid + outer_update).astype(jnp.bfloat16)
    return (refreshed_homolog_features, pairwise_output)


def solution(mesh):
    return jax.shard_map(
        on_device,
        mesh=mesh,
        in_specs=(
            P(("branch", "rows"), None, None),
            P("rows", "branch", None),
            P(),
            P(),
            P(),
            P(),
            P(),
            P(),
            P(),
            P(),
        ),
        out_specs=(P(("branch", "rows"), None, None), P("rows", "branch", None)),
        check_vma=False,
    )
```

```python
import jax
import jax.numpy as jnp
from jax import lax
from jax.sharding import PartitionSpec as P


def standardize_features(values, dimension):
    average = jnp.mean(values, axis=dimension, keepdims=True)
    centered = values - average
    variance = jnp.mean(centered * centered, axis=dimension, keepdims=True)
    return centered * lax.rsqrt(variance + 1e-05)


def alignment_branch(
    homolog_features, transition_expand_matrix, transition_contract_matrix, factor_pair_matrices
):
    local_rows, sequence_length, channel_width = homolog_features.shape
    homolog_real_matrix = homolog_features.astype(jnp.float32)
    standardized_homologs = (
        standardize_features(homolog_real_matrix, -1)
        .astype(jnp.bfloat16)
        .reshape(local_rows * sequence_length, channel_width)
    )
    expanded_activations = jax.nn.relu(
        jnp.dot(standardized_homologs, transition_expand_matrix, preferred_element_type=jnp.float32)
    ).astype(jnp.bfloat16)
    refreshed_homolog_features = (
        homolog_real_matrix
        + jnp.dot(
            expanded_activations, transition_contract_matrix, preferred_element_type=jnp.float32
        ).reshape(homolog_features.shape)
    ).astype(jnp.bfloat16)
    standardized_for_factors = (
        standardize_features(refreshed_homolog_features.astype(jnp.float32), -1)
        .astype(jnp.bfloat16)
        .reshape(local_rows * sequence_length, channel_width)
    )
    projected = jnp.dot(
        standardized_for_factors, factor_pair_matrices, preferred_element_type=jnp.float32
    ).reshape(local_rows, sequence_length, -1)
    channels = projected.shape[-1] // 2
    left_side = projected[..., :channels].astype(jnp.bfloat16)
    right_side = jnp.swapaxes(projected[..., channels:].astype(jnp.bfloat16), 1, 2)
    left_pair = lax.all_gather(left_side, "branch", axis=0, tiled=True)
    left_gathered = lax.all_to_all(left_pair, "rows", split_axis=1, concat_axis=0, tiled=True)
    right_pair = lax.all_to_all(right_side, "branch", split_axis=2, concat_axis=0, tiled=True)
    right_gathered = lax.all_gather(right_pair, "rows", axis=0, tiled=True)
    return (refreshed_homolog_features, left_gathered, right_gathered)


def send_whole(tri_left, tri_right):
    both = ("branch", "rows")
    return (
        lax.all_to_all(tri_left, both, split_axis=0, concat_axis=0, tiled=True),
        lax.all_to_all(tri_right, both, split_axis=0, concat_axis=0, tiled=True),
    )


def send_back(product):
    return lax.all_to_all(product, ("branch", "rows"), split_axis=0, concat_axis=0, tiled=True)


def pair_front(pairwise_input, triangle_projection_weight):
    tile_rows, columns, chans = pairwise_input.shape
    pair_float = pairwise_input.astype(jnp.float32)
    pair_norm = standardize_features(pair_float, -1).astype(jnp.bfloat16)
    norm_flat = pair_norm.reshape(tile_rows * columns, chans)
    proj_flat = lax.dot_general(
        triangle_projection_weight,
        norm_flat,
        (((0,), (1,)), ((), ())),
        preferred_element_type=jnp.float32,
    )
    proj_tile = proj_flat[: 4 * chans].reshape(4 * chans, tile_rows, columns)
    gate_vals = jax.nn.sigmoid(proj_flat[4 * chans :])
    tri_left = (jax.nn.sigmoid(proj_tile[chans : 2 * chans]) * proj_tile[:chans]).astype(
        jnp.bfloat16
    )
    tri_right = (jax.nn.sigmoid(proj_tile[3 * chans :]) * proj_tile[2 * chans : 3 * chans]).astype(
        jnp.bfloat16
    )
    return pair_float, gate_vals, tri_left, tri_right


def triangle_product(left_chan, right_chan):
    halves = lax.axis_size("branch")
    columns = left_chan.shape[-1]
    tile_rows = left_chan.shape[1]
    left_src = left_chan.reshape(halves, -1, columns)
    right_src = right_chan.reshape(halves, halves, -1, columns)
    product = jnp.einsum(
        "bik,bhjk->hij", left_src, right_src, preferred_element_type=jnp.float32
    ).astype(jnp.bfloat16)
    return product.reshape(-1, tile_rows, columns)


def pair_back(
    pair_float,
    gate_vals,
    product_tile,
    triangle_output_weight,
    pairwise_up_weight,
    pairwise_down_weight,
):
    tile_rows, columns, chans = pair_float.shape
    prod_norm = (
        standardize_features(product_tile.astype(jnp.float32), 0)
        .astype(jnp.bfloat16)
        .reshape(chans, tile_rows * columns)
    )
    tri_update = lax.dot_general(
        triangle_output_weight,
        prod_norm,
        (((0,), (0,)), ((), ())),
        preferred_element_type=jnp.float32,
    )
    gated_update = jnp.transpose(gate_vals * tri_update).reshape(tile_rows, columns, chans)
    pair_mid = pair_float + gated_update
    mid_norm = standardize_features(pair_mid, -1).astype(jnp.bfloat16)
    pair_hidden = jax.nn.relu(
        jnp.einsum("ijd,dh->ijh", mid_norm, pairwise_up_weight, preferred_element_type=jnp.float32)
    ).astype(jnp.bfloat16)
    return pair_mid + jnp.einsum(
        "ijh,hd->ijd", pair_hidden, pairwise_down_weight, preferred_element_type=jnp.float32
    )


def outer_product(left_gathered, right_gathered, outer_output_weight):
    total_rows, tile_rows, channels = left_gathered.shape
    columns = right_gathered.shape[2]
    span_cols = 128
    left_flat = left_gathered.reshape(total_rows, tile_rows * channels)
    pieces = []
    for offset in range(0, columns, span_cols):
        right_piece = right_gathered[:, :, offset : offset + span_cols].reshape(
            total_rows, channels * span_cols
        )
        outer_vals = lax.dot_general(
            left_flat, right_piece, (((0,), (0,)), ((), ())), preferred_element_type=jnp.float32
        )
        outer_vals = (
            (outer_vals / total_rows)
            .astype(jnp.bfloat16)
            .reshape(tile_rows, channels * channels, span_cols)
        )
        pieces.append(
            lax.dot_general(
                outer_output_weight,
                outer_vals,
                (((0,), (1,)), ((), ())),
                preferred_element_type=jnp.float32,
            )
        )
    outer_eij = jnp.concatenate(pieces, axis=2)
    return jnp.transpose(outer_eij, (1, 2, 0))


def on_device(
    homolog_features,
    pairwise_input,
    transition_expand_matrix,
    transition_contract_matrix,
    factor_pair_matrices,
    outer_output_weight,
    triangle_projection_weight,
    triangle_output_weight,
    pairwise_up_weight,
    pairwise_down_weight,
):
    pair_float, gate_vals, tri_left, tri_right = pair_front(
        pairwise_input, triangle_projection_weight
    )
    left_chan, right_chan = send_whole(tri_left, tri_right)
    homolog_features, tri_right = lax.optimization_barrier((homolog_features, tri_right))
    refreshed_homolog_features, left_gathered, right_gathered = alignment_branch(
        homolog_features, transition_expand_matrix, transition_contract_matrix, factor_pair_matrices
    )
    outer_update = outer_product(left_gathered, right_gathered, outer_output_weight)
    left_chan, right_chan, outer_update = lax.optimization_barrier(
        (left_chan, right_chan, outer_update)
    )
    product_tile = send_back(triangle_product(left_chan, right_chan))
    pair_mid = pair_back(
        pair_float,
        gate_vals,
        product_tile,
        triangle_output_weight,
        pairwise_up_weight,
        pairwise_down_weight,
    )
    pairwise_output = (pair_mid + outer_update).astype(jnp.bfloat16)
    return (refreshed_homolog_features, pairwise_output)


def solution(mesh):
    return jax.shard_map(
        on_device,
        mesh=mesh,
        in_specs=(
            P(("branch", "rows"), None, None),
            P("rows", "branch", None),
            P(),
            P(),
            P(),
            P(),
            P(),
            P(),
            P(),
            P(),
        ),
        out_specs=(P(("branch", "rows"), None, None), P("rows", "branch", None)),
        check_vma=False,
    )
```

```python
import jax
import jax.numpy as jnp
from jax import lax
from jax.sharding import PartitionSpec as P


def standardize_features(values, dimension):
    average = jnp.mean(values, axis=dimension, keepdims=True)
    centered = values - average
    variance = jnp.mean(centered * centered, axis=dimension, keepdims=True)
    return centered * lax.rsqrt(variance + 1e-05)


def alignment_branch(
    homolog_features, transition_expand_matrix, transition_contract_matrix, factor_pair_matrices
):
    local_rows, sequence_length, channel_width = homolog_features.shape
    homolog_real_matrix = homolog_features.astype(jnp.float32)
    standardized_homologs = (
        standardize_features(homolog_real_matrix, -1)
        .astype(jnp.bfloat16)
        .reshape(local_rows * sequence_length, channel_width)
    )
    expanded_activations = jax.nn.relu(
        jnp.dot(standardized_homologs, transition_expand_matrix, preferred_element_type=jnp.float32)
    ).astype(jnp.bfloat16)
    refreshed_homolog_features = (
        homolog_real_matrix
        + jnp.dot(
            expanded_activations, transition_contract_matrix, preferred_element_type=jnp.float32
        ).reshape(homolog_features.shape)
    ).astype(jnp.bfloat16)
    standardized_for_factors = (
        standardize_features(refreshed_homolog_features.astype(jnp.float32), -1)
        .astype(jnp.bfloat16)
        .reshape(local_rows * sequence_length, channel_width)
    )
    projected = jnp.dot(
        standardized_for_factors, factor_pair_matrices, preferred_element_type=jnp.float32
    ).reshape(local_rows, sequence_length, -1)
    channels = projected.shape[-1] // 2
    left_side = projected[..., :channels].astype(jnp.bfloat16)
    right_side = jnp.swapaxes(projected[..., channels:].astype(jnp.bfloat16), 1, 2)
    return (refreshed_homolog_features, left_side, right_side)


def gather_sides(left_side, right_side):
    left_pair = lax.all_gather(left_side, "branch", axis=0, tiled=True)
    left_gathered = lax.all_to_all(left_pair, "rows", split_axis=1, concat_axis=0, tiled=True)
    right_pair = lax.all_to_all(right_side, "branch", split_axis=2, concat_axis=0, tiled=True)
    right_gathered = lax.all_gather(right_pair, "rows", axis=0, tiled=True)
    return left_gathered, right_gathered


def send_whole(tri_left, tri_right):
    both = ("branch", "rows")
    return (
        lax.all_to_all(tri_left, both, split_axis=0, concat_axis=0, tiled=True),
        lax.all_to_all(tri_right, both, split_axis=0, concat_axis=0, tiled=True),
    )


def send_back(product):
    return lax.all_to_all(product, ("branch", "rows"), split_axis=0, concat_axis=0, tiled=True)


def pair_front(pairwise_input, triangle_projection_weight):
    tile_rows, columns, chans = pairwise_input.shape
    pair_float = pairwise_input.astype(jnp.float32)
    pair_norm = standardize_features(pair_float, -1).astype(jnp.bfloat16)
    norm_flat = pair_norm.reshape(tile_rows * columns, chans)
    proj_flat = lax.dot_general(
        triangle_projection_weight,
        norm_flat,
        (((0,), (1,)), ((), ())),
        preferred_element_type=jnp.float32,
    )
    proj_tile = proj_flat[: 4 * chans].reshape(4 * chans, tile_rows, columns)
    gate_vals = jax.nn.sigmoid(proj_flat[4 * chans :])
    tri_left = (jax.nn.sigmoid(proj_tile[chans : 2 * chans]) * proj_tile[:chans]).astype(
        jnp.bfloat16
    )
    tri_right = (jax.nn.sigmoid(proj_tile[3 * chans :]) * proj_tile[2 * chans : 3 * chans]).astype(
        jnp.bfloat16
    )
    return pair_float, gate_vals, tri_left, tri_right


def triangle_product(left_chan, right_chan):
    halves = lax.axis_size("branch")
    columns = left_chan.shape[-1]
    tile_rows = left_chan.shape[1]
    left_src = left_chan.reshape(halves, -1, columns)
    right_src = right_chan.reshape(halves, halves, -1, columns)
    product = jnp.einsum(
        "bik,bhjk->hij", left_src, right_src, preferred_element_type=jnp.float32
    ).astype(jnp.bfloat16)
    return product.reshape(-1, tile_rows, columns)


def pair_back(
    pair_float,
    gate_vals,
    product_tile,
    triangle_output_weight,
    pairwise_up_weight,
    pairwise_down_weight,
):
    tile_rows, columns, chans = pair_float.shape
    prod_norm = (
        standardize_features(product_tile.astype(jnp.float32), 0)
        .astype(jnp.bfloat16)
        .reshape(chans, tile_rows * columns)
    )
    tri_update = lax.dot_general(
        triangle_output_weight,
        prod_norm,
        (((0,), (0,)), ((), ())),
        preferred_element_type=jnp.float32,
    )
    gated_update = jnp.transpose(gate_vals * tri_update).reshape(tile_rows, columns, chans)
    pair_mid = pair_float + gated_update
    mid_norm = standardize_features(pair_mid, -1).astype(jnp.bfloat16)
    pair_hidden = jax.nn.relu(
        jnp.einsum("ijd,dh->ijh", mid_norm, pairwise_up_weight, preferred_element_type=jnp.float32)
    ).astype(jnp.bfloat16)
    return pair_mid + jnp.einsum(
        "ijh,hd->ijd", pair_hidden, pairwise_down_weight, preferred_element_type=jnp.float32
    )


def outer_product(left_gathered, right_gathered, outer_output_weight, first, last):
    total_rows, tile_rows, channels = left_gathered.shape
    span_cols = 128
    left_flat = left_gathered.reshape(total_rows, tile_rows * channels)
    pieces = []
    for offset in range(first * span_cols, last * span_cols, span_cols):
        right_piece = right_gathered[:, :, offset : offset + span_cols].reshape(
            total_rows, channels * span_cols
        )
        outer_vals = lax.dot_general(
            left_flat, right_piece, (((0,), (0,)), ((), ())), preferred_element_type=jnp.float32
        )
        outer_vals = (
            (outer_vals / total_rows)
            .astype(jnp.bfloat16)
            .reshape(tile_rows, channels * channels, span_cols)
        )
        pieces.append(
            lax.dot_general(
                outer_output_weight,
                outer_vals,
                (((0,), (1,)), ((), ())),
                preferred_element_type=jnp.float32,
            )
        )
    return jnp.concatenate(pieces, axis=2)


def on_device(
    homolog_features,
    pairwise_input,
    transition_expand_matrix,
    transition_contract_matrix,
    factor_pair_matrices,
    outer_output_weight,
    triangle_projection_weight,
    triangle_output_weight,
    pairwise_up_weight,
    pairwise_down_weight,
):
    refreshed_homolog_features, left_side, right_side = alignment_branch(
        homolog_features, transition_expand_matrix, transition_contract_matrix, factor_pair_matrices
    )
    left_gathered, right_gathered = gather_sides(left_side, right_side)
    pairwise_input, right_side = lax.optimization_barrier((pairwise_input, right_side))
    pair_float, gate_vals, tri_left, tri_right = pair_front(
        pairwise_input, triangle_projection_weight
    )
    left_chan, right_chan = send_whole(tri_left, tri_right)
    left_gathered, right_gathered, tri_right = lax.optimization_barrier(
        (left_gathered, right_gathered, tri_right)
    )
    pieces = right_gathered.shape[2] // 128
    outer_first = outer_product(
        left_gathered, right_gathered, outer_output_weight, 0, pieces // 2
    )
    left_chan, right_chan, outer_first = lax.optimization_barrier(
        (left_chan, right_chan, outer_first)
    )
    product = triangle_product(left_chan, right_chan)
    product, left_gathered, right_gathered = lax.optimization_barrier(
        (product, left_gathered, right_gathered)
    )
    product_tile = send_back(product)
    outer_second = outer_product(
        left_gathered, right_gathered, outer_output_weight, pieces // 2, pieces
    )
    product_tile, outer_second = lax.optimization_barrier((product_tile, outer_second))
    outer_update = jnp.transpose(
        jnp.concatenate([outer_first, outer_second], axis=2), (1, 2, 0)
    )
    pair_mid = pair_back(
        pair_float,
        gate_vals,
        product_tile,
        triangle_output_weight,
        pairwise_up_weight,
        pairwise_down_weight,
    )
    pairwise_output = (pair_mid + outer_update).astype(jnp.bfloat16)
    return (refreshed_homolog_features, pairwise_output)


def solution(mesh):
    return jax.shard_map(
        on_device,
        mesh=mesh,
        in_specs=(
            P(("branch", "rows"), None, None),
            P("rows", "branch", None),
            P(),
            P(),
            P(),
            P(),
            P(),
            P(),
            P(),
            P(),
        ),
        out_specs=(P(("branch", "rows"), None, None), P("rows", "branch", None)),
        check_vma=False,
    )
```

```python
import jax
import jax.numpy as jnp
from jax import lax
from jax.sharding import PartitionSpec as P


def standardize_features(values, dimension):
    average = jnp.mean(values, axis=dimension, keepdims=True)
    centered = values - average
    variance = jnp.mean(centered * centered, axis=dimension, keepdims=True)
    return centered * lax.rsqrt(variance + 1e-05)


def alignment_branch(
    homolog_features, transition_expand_matrix, transition_contract_matrix, factor_pair_matrices
):
    local_rows, sequence_length, channel_width = homolog_features.shape
    homolog_real_matrix = homolog_features.astype(jnp.float32)
    standardized_homologs = (
        standardize_features(homolog_real_matrix, -1)
        .astype(jnp.bfloat16)
        .reshape(local_rows * sequence_length, channel_width)
    )
    expanded_activations = jax.nn.relu(
        jnp.dot(standardized_homologs, transition_expand_matrix, preferred_element_type=jnp.float32)
    ).astype(jnp.bfloat16)
    refreshed_homolog_features = (
        homolog_real_matrix
        + jnp.dot(
            expanded_activations, transition_contract_matrix, preferred_element_type=jnp.float32
        ).reshape(homolog_features.shape)
    ).astype(jnp.bfloat16)
    standardized_for_factors = (
        standardize_features(refreshed_homolog_features.astype(jnp.float32), -1)
        .astype(jnp.bfloat16)
        .reshape(local_rows * sequence_length, channel_width)
    )
    projected = jnp.dot(
        standardized_for_factors, factor_pair_matrices, preferred_element_type=jnp.float32
    ).reshape(local_rows, sequence_length, -1)
    channels = projected.shape[-1] // 2
    left_side = projected[..., :channels].astype(jnp.bfloat16)
    right_side = jnp.swapaxes(projected[..., channels:].astype(jnp.bfloat16), 1, 2)
    return (refreshed_homolog_features, left_side, right_side)


def branch_pair(mine, theirs):
    first = lax.axis_index("branch") == 0
    return jnp.where(first, jnp.concatenate([mine, theirs]), jnp.concatenate([theirs, mine]))


def gather_sides(left_side, right_side):
    swap = [(0, 1), (1, 0)]
    left_pair = branch_pair(left_side, lax.ppermute(left_side, "branch", swap))
    left_gathered = lax.all_to_all(left_pair, "rows", split_axis=1, concat_axis=0, tiled=True)
    half = right_side.shape[2] // 2
    me = lax.axis_index("branch")
    keep = lax.dynamic_slice_in_dim(right_side, me * half, half, axis=2)
    send = lax.dynamic_slice_in_dim(right_side, (1 - me) * half, half, axis=2)
    right_pair = branch_pair(keep, lax.ppermute(send, "branch", swap))
    right_gathered = lax.all_gather(right_pair, "rows", axis=0, tiled=True)
    return left_gathered, right_gathered


def send_whole(tri_left, tri_right):
    both = ("branch", "rows")
    moved = lax.all_to_all(
        jnp.stack([tri_left, tri_right], axis=1), both, split_axis=0, concat_axis=0, tiled=True
    )
    return moved[:, 0], moved[:, 1]


def send_back(product):
    return lax.all_to_all(product, ("branch", "rows"), split_axis=0, concat_axis=0, tiled=True)


def pair_front(pairwise_input, triangle_projection_weight):
    tile_rows, columns, chans = pairwise_input.shape
    pair_float = pairwise_input.astype(jnp.float32)
    pair_norm = standardize_features(pair_float, -1).astype(jnp.bfloat16)
    norm_flat = pair_norm.reshape(tile_rows * columns, chans)
    proj_flat = lax.dot_general(
        triangle_projection_weight,
        norm_flat,
        (((0,), (1,)), ((), ())),
        preferred_element_type=jnp.float32,
    )
    proj_tile = proj_flat[: 4 * chans].reshape(4 * chans, tile_rows, columns)
    gate_vals = jax.nn.sigmoid(proj_flat[4 * chans :])
    tri_left = (jax.nn.sigmoid(proj_tile[chans : 2 * chans]) * proj_tile[:chans]).astype(
        jnp.bfloat16
    )
    tri_right = (jax.nn.sigmoid(proj_tile[3 * chans :]) * proj_tile[2 * chans : 3 * chans]).astype(
        jnp.bfloat16
    )
    return pair_float, gate_vals, tri_left, tri_right


def triangle_product(left_chan, right_chan):
    halves = lax.axis_size("branch")
    columns = left_chan.shape[-1]
    tile_rows = left_chan.shape[1]
    left_src = left_chan.reshape(halves, -1, columns)
    right_src = right_chan.reshape(halves, halves, -1, columns)
    product = jnp.einsum(
        "bik,bhjk->hij", left_src, right_src, preferred_element_type=jnp.float32
    ).astype(jnp.bfloat16)
    return product.reshape(-1, tile_rows, columns)


def pair_back(
    pair_float,
    gate_vals,
    product_tile,
    triangle_output_weight,
    pairwise_up_weight,
    pairwise_down_weight,
):
    tile_rows, columns, chans = pair_float.shape
    prod_norm = (
        standardize_features(product_tile.astype(jnp.float32), 0)
        .astype(jnp.bfloat16)
        .reshape(chans, tile_rows * columns)
    )
    tri_update = lax.dot_general(
        triangle_output_weight,
        prod_norm,
        (((0,), (0,)), ((), ())),
        preferred_element_type=jnp.float32,
    )
    gated_update = jnp.transpose(gate_vals * tri_update).reshape(tile_rows, columns, chans)
    pair_mid = pair_float + gated_update
    mid_norm = standardize_features(pair_mid, -1).astype(jnp.bfloat16)
    pair_hidden = jax.nn.relu(
        jnp.einsum("ijd,dh->ijh", mid_norm, pairwise_up_weight, preferred_element_type=jnp.float32)
    ).astype(jnp.bfloat16)
    return pair_mid + jnp.einsum(
        "ijh,hd->ijd", pair_hidden, pairwise_down_weight, preferred_element_type=jnp.float32
    )


def outer_product(left_gathered, right_gathered, outer_output_weight, first, last):
    total_rows, tile_rows, channels = left_gathered.shape
    span_cols = 128
    left_flat = left_gathered.reshape(total_rows, tile_rows * channels)
    pieces = []
    for offset in range(first * span_cols, last * span_cols, span_cols):
        right_piece = right_gathered[:, :, offset : offset + span_cols].reshape(
            total_rows, channels * span_cols
        )
        outer_vals = lax.dot_general(
            left_flat, right_piece, (((0,), (0,)), ((), ())), preferred_element_type=jnp.float32
        )
        outer_vals = (
            (outer_vals / total_rows)
            .astype(jnp.bfloat16)
            .reshape(tile_rows, channels * channels, span_cols)
        )
        pieces.append(
            lax.dot_general(
                outer_output_weight,
                outer_vals,
                (((0,), (1,)), ((), ())),
                preferred_element_type=jnp.float32,
            )
        )
    return jnp.concatenate(pieces, axis=2)


def on_device(
    homolog_features,
    pairwise_input,
    transition_expand_matrix,
    transition_contract_matrix,
    factor_pair_matrices,
    outer_output_weight,
    triangle_projection_weight,
    triangle_output_weight,
    pairwise_up_weight,
    pairwise_down_weight,
):
    refreshed_homolog_features, left_side, right_side = alignment_branch(
        homolog_features, transition_expand_matrix, transition_contract_matrix, factor_pair_matrices
    )
    left_gathered, right_gathered = gather_sides(left_side, right_side)
    pairwise_input, right_side = lax.optimization_barrier((pairwise_input, right_side))
    pair_float, gate_vals, tri_left, tri_right = pair_front(
        pairwise_input, triangle_projection_weight
    )
    left_chan, right_chan = send_whole(tri_left, tri_right)
    left_gathered, right_gathered, tri_right = lax.optimization_barrier(
        (left_gathered, right_gathered, tri_right)
    )
    pieces = right_gathered.shape[2] // 128
    outer_first = outer_product(
        left_gathered, right_gathered, outer_output_weight, 0, pieces // 2
    )
    left_chan, right_chan, outer_first = lax.optimization_barrier(
        (left_chan, right_chan, outer_first)
    )
    product = triangle_product(left_chan, right_chan)
    product, left_gathered, right_gathered = lax.optimization_barrier(
        (product, left_gathered, right_gathered)
    )
    product_tile = send_back(product)
    outer_second = outer_product(
        left_gathered, right_gathered, outer_output_weight, pieces // 2, pieces
    )
    product_tile, outer_second = lax.optimization_barrier((product_tile, outer_second))
    outer_update = jnp.transpose(
        jnp.concatenate([outer_first, outer_second], axis=2), (1, 2, 0)
    )
    pair_mid = pair_back(
        pair_float,
        gate_vals,
        product_tile,
        triangle_output_weight,
        pairwise_up_weight,
        pairwise_down_weight,
    )
    pairwise_output = (pair_mid + outer_update).astype(jnp.bfloat16)
    return (refreshed_homolog_features, pairwise_output)


def solution(mesh):
    return jax.shard_map(
        on_device,
        mesh=mesh,
        in_specs=(
            P(("branch", "rows"), None, None),
            P("rows", "branch", None),
            P(),
            P(),
            P(),
            P(),
            P(),
            P(),
            P(),
            P(),
        ),
        out_specs=(P(("branch", "rows"), None, None), P("rows", "branch", None)),
        check_vma=False,
    )
```

```python
import jax
import jax.numpy as jnp
from jax import lax
from jax.experimental import pallas as pl
from jax.experimental.pallas import tpu as pltpu
from jax.sharding import PartitionSpec as P


def standardize_features(values, dimension):
    average = jnp.mean(values, axis=dimension, keepdims=True)
    centered = values - average
    variance = jnp.mean(centered * centered, axis=dimension, keepdims=True)
    return centered * lax.rsqrt(variance + 1e-05)


def alignment_branch(
    homolog_features, transition_expand_matrix, transition_contract_matrix, factor_pair_matrices
):
    local_rows, sequence_length, channel_width = homolog_features.shape
    homolog_real_matrix = homolog_features.astype(jnp.float32)
    standardized_homologs = (
        standardize_features(homolog_real_matrix, -1)
        .astype(jnp.bfloat16)
        .reshape(local_rows * sequence_length, channel_width)
    )
    expanded_activations = jax.nn.relu(
        jnp.dot(standardized_homologs, transition_expand_matrix, preferred_element_type=jnp.float32)
    ).astype(jnp.bfloat16)
    refreshed_homolog_features = (
        homolog_real_matrix
        + jnp.dot(
            expanded_activations, transition_contract_matrix, preferred_element_type=jnp.float32
        ).reshape(homolog_features.shape)
    ).astype(jnp.bfloat16)
    standardized_for_factors = (
        standardize_features(refreshed_homolog_features.astype(jnp.float32), -1)
        .astype(jnp.bfloat16)
        .reshape(local_rows * sequence_length, channel_width)
    )
    projected = jnp.dot(
        standardized_for_factors, factor_pair_matrices, preferred_element_type=jnp.float32
    ).reshape(local_rows, sequence_length, -1)
    channels = projected.shape[-1] // 2
    left_side = projected[..., :channels].astype(jnp.bfloat16)
    right_side = jnp.swapaxes(projected[..., channels:].astype(jnp.bfloat16), 1, 2)
    return (refreshed_homolog_features, left_side, right_side)


def gather_sides(left_side, right_side):
    left_pair = lax.all_gather(left_side, "branch", axis=0, tiled=True)
    left_gathered = lax.all_to_all(left_pair, "rows", split_axis=1, concat_axis=0, tiled=True)
    right_pair = lax.all_to_all(right_side, "branch", split_axis=2, concat_axis=0, tiled=True)
    right_gathered = lax.all_gather(jnp.swapaxes(right_pair, 0, 1), "rows", axis=1, tiled=True)
    return left_gathered, right_gathered


def send_whole(tri_left, tri_right):
    both = ("branch", "rows")
    return (
        lax.all_to_all(tri_left, both, split_axis=0, concat_axis=0, tiled=True),
        lax.all_to_all(tri_right, both, split_axis=0, concat_axis=0, tiled=True),
    )


def send_back(product):
    return lax.all_to_all(product, ("branch", "rows"), split_axis=0, concat_axis=0, tiled=True)


def pair_front(pairwise_input, triangle_projection_weight):
    tile_rows, columns, chans = pairwise_input.shape
    pair_float = pairwise_input.astype(jnp.float32)
    pair_norm = standardize_features(pair_float, -1).astype(jnp.bfloat16)
    norm_flat = pair_norm.reshape(tile_rows * columns, chans)
    proj_flat = lax.dot_general(
        triangle_projection_weight,
        norm_flat,
        (((0,), (1,)), ((), ())),
        preferred_element_type=jnp.float32,
    )
    proj_tile = proj_flat[: 4 * chans].reshape(4 * chans, tile_rows, columns)
    gate_vals = jax.nn.sigmoid(proj_flat[4 * chans :])
    tri_left = (jax.nn.sigmoid(proj_tile[chans : 2 * chans]) * proj_tile[:chans]).astype(
        jnp.bfloat16
    )
    tri_right = (jax.nn.sigmoid(proj_tile[3 * chans :]) * proj_tile[2 * chans : 3 * chans]).astype(
        jnp.bfloat16
    )
    return pair_float, gate_vals, tri_left, tri_right


def triangle_product(left_chan, right_chan):
    halves = lax.axis_size("branch")
    columns = left_chan.shape[-1]
    tile_rows = left_chan.shape[1]
    left_src = left_chan.reshape(halves, -1, columns)
    right_src = right_chan.reshape(halves, halves, -1, columns)
    product = jnp.einsum(
        "bik,bhjk->hij", left_src, right_src, preferred_element_type=jnp.float32
    ).astype(jnp.bfloat16)
    return product.reshape(-1, tile_rows, columns)


def pair_back(
    pair_float,
    gate_vals,
    product_tile,
    triangle_output_weight,
    pairwise_up_weight,
    pairwise_down_weight,
):
    tile_rows, columns, chans = pair_float.shape
    prod_norm = (
        standardize_features(product_tile.astype(jnp.float32), 0)
        .astype(jnp.bfloat16)
        .reshape(chans, tile_rows * columns)
    )
    tri_update = lax.dot_general(
        triangle_output_weight,
        prod_norm,
        (((0,), (0,)), ((), ())),
        preferred_element_type=jnp.float32,
    )
    gated_update = jnp.transpose(gate_vals * tri_update).reshape(tile_rows, columns, chans)
    pair_mid = pair_float + gated_update
    mid_norm = standardize_features(pair_mid, -1).astype(jnp.bfloat16)
    pair_hidden = jax.nn.relu(
        jnp.einsum("ijd,dh->ijh", mid_norm, pairwise_up_weight, preferred_element_type=jnp.float32)
    ).astype(jnp.bfloat16)
    return pair_mid + jnp.einsum(
        "ijh,hd->ijd", pair_hidden, pairwise_down_weight, preferred_element_type=jnp.float32
    )


def outer_kernel(lt_ref, r_ref, wt_ref, out_ref, x_ref):
    n_factor = r_ref.shape[0]
    tile_rows = out_ref.shape[0]
    scale = 1.0 / r_ref.shape[1]

    def fill(d, carry):
        vals = jnp.dot(lt_ref[...], r_ref[d], preferred_element_type=jnp.float32)
        vals = (vals * scale).astype(jnp.bfloat16)
        start = pl.multiple_of(d * n_factor, n_factor)
        for i in range(tile_rows):
            x_ref[i, pl.ds(start, n_factor), :] = vals[i * n_factor : (i + 1) * n_factor, :]
        return carry

    lax.fori_loop(0, n_factor, fill, 0)

    def emit(i, carry):
        upd = jnp.dot(wt_ref[...], x_ref[i], preferred_element_type=jnp.float32)
        out_ref[i] = upd.T
        return carry

    lax.fori_loop(0, tile_rows, emit, 0)


def outer_product(left_gathered, right_gathered, outer_output_weight):
    total_rows, tile_rows, channels = left_gathered.shape
    columns = right_gathered.shape[2]
    pair = outer_output_weight.shape[1]
    left_t = jnp.transpose(left_gathered, (1, 2, 0)).reshape(tile_rows * channels, total_rows)
    weight_t = jnp.transpose(
        outer_output_weight.reshape(channels, channels, pair), (1, 0, 2)
    ).reshape(channels * channels, pair).T
    flops = 4 * tile_rows * channels * channels * columns * (total_rows + pair) // 2
    return pl.pallas_call(
        outer_kernel,
        out_shape=jax.ShapeDtypeStruct((tile_rows, columns, pair), jnp.float32),
        in_specs=[pl.BlockSpec(memory_space=pltpu.VMEM)] * 3,
        out_specs=pl.BlockSpec(memory_space=pltpu.VMEM),
        scratch_shapes=[pltpu.VMEM((tile_rows, channels * channels, columns), jnp.bfloat16)],
        compiler_params=pltpu.CompilerParams(vmem_limit_bytes=56 * 1024 * 1024),
        cost_estimate=pl.CostEstimate(
            flops=flops, transcendentals=0, bytes_accessed=right_gathered.size * 2 + tile_rows * columns * pair * 4
        ),
    )(left_t, right_gathered, weight_t)


def on_device(
    homolog_features,
    pairwise_input,
    transition_expand_matrix,
    transition_contract_matrix,
    factor_pair_matrices,
    outer_output_weight,
    triangle_projection_weight,
    triangle_output_weight,
    pairwise_up_weight,
    pairwise_down_weight,
):
    refreshed_homolog_features, left_side, right_side = alignment_branch(
        homolog_features, transition_expand_matrix, transition_contract_matrix, factor_pair_matrices
    )
    left_gathered, right_gathered = gather_sides(left_side, right_side)
    pairwise_input, right_side = lax.optimization_barrier((pairwise_input, right_side))
    pair_float, gate_vals, tri_left, tri_right = pair_front(
        pairwise_input, triangle_projection_weight
    )
    left_chan, right_chan = send_whole(tri_left, tri_right)
    left_gathered, right_gathered, tri_right = lax.optimization_barrier(
        (left_gathered, right_gathered, tri_right)
    )
    outer_update = outer_product(left_gathered, right_gathered, outer_output_weight)
    left_chan, right_chan, outer_update = lax.optimization_barrier(
        (left_chan, right_chan, outer_update)
    )
    product_tile = send_back(triangle_product(left_chan, right_chan))
    pair_mid = pair_back(
        pair_float,
        gate_vals,
        product_tile,
        triangle_output_weight,
        pairwise_up_weight,
        pairwise_down_weight,
    )
    pairwise_output = (pair_mid + outer_update).astype(jnp.bfloat16)
    return (refreshed_homolog_features, pairwise_output)


def solution(mesh):
    return jax.shard_map(
        on_device,
        mesh=mesh,
        in_specs=(
            P(("branch", "rows"), None, None),
            P("rows", "branch", None),
            P(),
            P(),
            P(),
            P(),
            P(),
            P(),
            P(),
            P(),
        ),
        out_specs=(P(("branch", "rows"), None, None), P("rows", "branch", None)),
        check_vma=False,
    )
```

```python
import jax
import jax.numpy as jnp
from jax import lax
from jax.experimental import pallas as pl
from jax.experimental.pallas import tpu as pltpu
from jax.sharding import PartitionSpec as P


def standardize_features(values, dimension):
    average = jnp.mean(values, axis=dimension, keepdims=True)
    centered = values - average
    variance = jnp.mean(centered * centered, axis=dimension, keepdims=True)
    return centered * lax.rsqrt(variance + 1e-05)


def alignment_branch(
    homolog_features, transition_expand_matrix, transition_contract_matrix, factor_pair_matrices
):
    local_rows, sequence_length, channel_width = homolog_features.shape
    homolog_real_matrix = homolog_features.astype(jnp.float32)
    standardized_homologs = (
        standardize_features(homolog_real_matrix, -1)
        .astype(jnp.bfloat16)
        .reshape(local_rows * sequence_length, channel_width)
    )
    expanded_activations = jax.nn.relu(
        jnp.dot(standardized_homologs, transition_expand_matrix, preferred_element_type=jnp.float32)
    ).astype(jnp.bfloat16)
    refreshed_homolog_features = (
        homolog_real_matrix
        + jnp.dot(
            expanded_activations, transition_contract_matrix, preferred_element_type=jnp.float32
        ).reshape(homolog_features.shape)
    ).astype(jnp.bfloat16)
    standardized_for_factors = (
        standardize_features(refreshed_homolog_features.astype(jnp.float32), -1)
        .astype(jnp.bfloat16)
        .reshape(local_rows * sequence_length, channel_width)
    )
    projected = jnp.dot(
        standardized_for_factors, factor_pair_matrices, preferred_element_type=jnp.float32
    ).reshape(local_rows, sequence_length, -1)
    channels = projected.shape[-1] // 2
    left_side = projected[..., :channels].astype(jnp.bfloat16)
    right_side = jnp.swapaxes(projected[..., channels:].astype(jnp.bfloat16), 1, 2)
    return (refreshed_homolog_features, left_side, right_side)


def branch_pair(mine, theirs):
    first = lax.axis_index("branch") == 0
    return jnp.where(first, jnp.concatenate([mine, theirs]), jnp.concatenate([theirs, mine]))


def gather_sides(left_side, right_side):
    swap = [(0, 1), (1, 0)]
    left_pair = branch_pair(left_side, lax.ppermute(left_side, "branch", swap))
    left_gathered = lax.all_to_all(left_pair, "rows", split_axis=1, concat_axis=0, tiled=True)
    half = right_side.shape[2] // 2
    me = lax.axis_index("branch")
    keep = lax.dynamic_slice_in_dim(right_side, me * half, half, axis=2)
    send = lax.dynamic_slice_in_dim(right_side, (1 - me) * half, half, axis=2)
    right_pair = branch_pair(keep, lax.ppermute(send, "branch", swap))
    right_gathered = lax.all_gather(jnp.swapaxes(right_pair, 0, 1), "rows", axis=1, tiled=True)
    return left_gathered, right_gathered


def send_whole(tri_left, tri_right):
    both = ("branch", "rows")
    moved = lax.all_to_all(
        jnp.stack([tri_left, tri_right], axis=1), both, split_axis=0, concat_axis=0, tiled=True
    )
    return moved[:, 0], moved[:, 1]


def send_back(product):
    return lax.all_to_all(product, ("branch", "rows"), split_axis=0, concat_axis=0, tiled=True)


def pair_front(pairwise_input, triangle_projection_weight):
    tile_rows, columns, chans = pairwise_input.shape
    pair_float = pairwise_input.astype(jnp.float32)
    pair_norm = standardize_features(pair_float, -1).astype(jnp.bfloat16)
    norm_flat = pair_norm.reshape(tile_rows * columns, chans)
    proj_flat = lax.dot_general(
        triangle_projection_weight,
        norm_flat,
        (((0,), (1,)), ((), ())),
        preferred_element_type=jnp.float32,
    )
    proj_tile = proj_flat[: 4 * chans].reshape(4 * chans, tile_rows, columns)
    gate_vals = jax.nn.sigmoid(proj_flat[4 * chans :])
    tri_left = (jax.nn.sigmoid(proj_tile[chans : 2 * chans]) * proj_tile[:chans]).astype(
        jnp.bfloat16
    )
    tri_right = (jax.nn.sigmoid(proj_tile[3 * chans :]) * proj_tile[2 * chans : 3 * chans]).astype(
        jnp.bfloat16
    )
    return pair_float, gate_vals, tri_left, tri_right


def triangle_product(left_chan, right_chan):
    halves = lax.axis_size("branch")
    columns = left_chan.shape[-1]
    tile_rows = left_chan.shape[1]
    left_src = left_chan.reshape(halves, -1, columns)
    right_src = right_chan.reshape(halves, halves, -1, columns)
    product = jnp.einsum(
        "bik,bhjk->hij", left_src, right_src, preferred_element_type=jnp.float32
    ).astype(jnp.bfloat16)
    return product.reshape(-1, tile_rows, columns)


def pair_back(
    pair_float,
    gate_vals,
    product_tile,
    triangle_output_weight,
    pairwise_up_weight,
    pairwise_down_weight,
):
    tile_rows, columns, chans = pair_float.shape
    prod_norm = (
        standardize_features(product_tile.astype(jnp.float32), 0)
        .astype(jnp.bfloat16)
        .reshape(chans, tile_rows * columns)
    )
    tri_update = lax.dot_general(
        triangle_output_weight,
        prod_norm,
        (((0,), (0,)), ((), ())),
        preferred_element_type=jnp.float32,
    )
    gated_update = jnp.transpose(gate_vals * tri_update).reshape(tile_rows, columns, chans)
    pair_mid = pair_float + gated_update
    mid_norm = standardize_features(pair_mid, -1).astype(jnp.bfloat16)
    pair_hidden = jax.nn.relu(
        jnp.einsum("ijd,dh->ijh", mid_norm, pairwise_up_weight, preferred_element_type=jnp.float32)
    ).astype(jnp.bfloat16)
    return pair_mid + jnp.einsum(
        "ijh,hd->ijd", pair_hidden, pairwise_down_weight, preferred_element_type=jnp.float32
    )


def outer_kernel(lt_ref, r_ref, wt_ref, out_ref, x_ref):
    n_factor = r_ref.shape[0]
    tile_rows = out_ref.shape[0]
    scale = 1.0 / r_ref.shape[1]

    def fill(d, carry):
        vals = jnp.dot(lt_ref[...], r_ref[d], preferred_element_type=jnp.float32)
        vals = (vals * scale).astype(jnp.bfloat16)
        start = pl.multiple_of(d * n_factor, n_factor)
        for i in range(tile_rows):
            x_ref[i, pl.ds(start, n_factor), :] = vals[i * n_factor : (i + 1) * n_factor, :]
        return carry

    lax.fori_loop(0, n_factor, fill, 0)

    def emit(i, carry):
        upd = jnp.dot(wt_ref[...], x_ref[i], preferred_element_type=jnp.float32)
        out_ref[i] = upd.T
        return carry

    lax.fori_loop(0, tile_rows, emit, 0)


def outer_product(left_gathered, right_gathered, outer_output_weight):
    total_rows, tile_rows, channels = left_gathered.shape
    columns = right_gathered.shape[2]
    pair = outer_output_weight.shape[1]
    left_t = jnp.transpose(left_gathered, (1, 2, 0)).reshape(tile_rows * channels, total_rows)
    weight_t = jnp.transpose(
        outer_output_weight.reshape(channels, channels, pair), (1, 0, 2)
    ).reshape(channels * channels, pair).T
    flops = 4 * tile_rows * channels * channels * columns * (total_rows + pair) // 2
    return pl.pallas_call(
        outer_kernel,
        out_shape=jax.ShapeDtypeStruct((tile_rows, columns, pair), jnp.float32),
        in_specs=[pl.BlockSpec(memory_space=pltpu.VMEM)] * 3,
        out_specs=pl.BlockSpec(memory_space=pltpu.VMEM),
        scratch_shapes=[pltpu.VMEM((tile_rows, channels * channels, columns), jnp.bfloat16)],
        compiler_params=pltpu.CompilerParams(vmem_limit_bytes=56 * 1024 * 1024),
        cost_estimate=pl.CostEstimate(
            flops=flops, transcendentals=0, bytes_accessed=right_gathered.size * 2 + tile_rows * columns * pair * 4
        ),
    )(left_t, right_gathered, weight_t)


def on_device(
    homolog_features,
    pairwise_input,
    transition_expand_matrix,
    transition_contract_matrix,
    factor_pair_matrices,
    outer_output_weight,
    triangle_projection_weight,
    triangle_output_weight,
    pairwise_up_weight,
    pairwise_down_weight,
):
    refreshed_homolog_features, left_side, right_side = alignment_branch(
        homolog_features, transition_expand_matrix, transition_contract_matrix, factor_pair_matrices
    )
    left_gathered, right_gathered = gather_sides(left_side, right_side)
    pairwise_input, right_side = lax.optimization_barrier((pairwise_input, right_side))
    pair_float, gate_vals, tri_left, tri_right = pair_front(
        pairwise_input, triangle_projection_weight
    )
    left_chan, right_chan = send_whole(tri_left, tri_right)
    product = triangle_product(left_chan, right_chan)
    product, left_gathered, right_gathered = lax.optimization_barrier(
        (product, left_gathered, right_gathered)
    )
    product_tile = send_back(product)
    outer_update = outer_product(left_gathered, right_gathered, outer_output_weight)
    product_tile, outer_update = lax.optimization_barrier((product_tile, outer_update))
    pair_mid = pair_back(
        pair_float,
        gate_vals,
        product_tile,
        triangle_output_weight,
        pairwise_up_weight,
        pairwise_down_weight,
    )
    pairwise_output = (pair_mid + outer_update).astype(jnp.bfloat16)
    return (refreshed_homolog_features, pairwise_output)


def solution(mesh):
    return jax.shard_map(
        on_device,
        mesh=mesh,
        in_specs=(
            P(("branch", "rows"), None, None),
            P("rows", "branch", None),
            P(),
            P(),
            P(),
            P(),
            P(),
            P(),
            P(),
            P(),
        ),
        out_specs=(P(("branch", "rows"), None, None), P("rows", "branch", None)),
        check_vma=False,
    )
```

```python
import jax
import jax.numpy as jnp
from jax import lax
from jax.experimental import pallas as pl
from jax.experimental.pallas import tpu as pltpu
from jax.sharding import PartitionSpec as P


def standardize_features(values, dimension):
    average = jnp.mean(values, axis=dimension, keepdims=True)
    centered = values - average
    variance = jnp.mean(centered * centered, axis=dimension, keepdims=True)
    return centered * lax.rsqrt(variance + 1e-05)


def alignment_branch(
    homolog_features, transition_expand_matrix, transition_contract_matrix, factor_pair_matrices
):
    local_rows, sequence_length, channel_width = homolog_features.shape
    homolog_real_matrix = homolog_features.astype(jnp.float32)
    standardized_homologs = (
        standardize_features(homolog_real_matrix, -1)
        .astype(jnp.bfloat16)
        .reshape(local_rows * sequence_length, channel_width)
    )
    expanded_activations = jax.nn.relu(
        jnp.dot(standardized_homologs, transition_expand_matrix, preferred_element_type=jnp.float32)
    ).astype(jnp.bfloat16)
    refreshed_homolog_features = (
        homolog_real_matrix
        + jnp.dot(
            expanded_activations, transition_contract_matrix, preferred_element_type=jnp.float32
        ).reshape(homolog_features.shape)
    ).astype(jnp.bfloat16)
    standardized_for_factors = (
        standardize_features(refreshed_homolog_features.astype(jnp.float32), -1)
        .astype(jnp.bfloat16)
        .reshape(local_rows * sequence_length, channel_width)
    )
    projected = jnp.dot(
        standardized_for_factors, factor_pair_matrices, preferred_element_type=jnp.float32
    ).reshape(local_rows, sequence_length, -1)
    channels = projected.shape[-1] // 2
    left_side = projected[..., :channels].astype(jnp.bfloat16)
    right_side = jnp.swapaxes(projected[..., channels:].astype(jnp.bfloat16), 1, 2)
    return (refreshed_homolog_features, left_side, right_side)


def branch_pair(mine, theirs):
    first = lax.axis_index("branch") == 0
    return jnp.where(first, jnp.concatenate([mine, theirs]), jnp.concatenate([theirs, mine]))


def gather_sides(left_side, right_side):
    swap = [(0, 1), (1, 0)]
    half = right_side.shape[2] // 2
    me = lax.axis_index("branch")
    keep = lax.dynamic_slice_in_dim(right_side, me * half, half, axis=2)
    send = lax.dynamic_slice_in_dim(right_side, (1 - me) * half, half, axis=2)
    right_pair = branch_pair(keep, lax.ppermute(send, "branch", swap))
    right_gathered = lax.all_gather(jnp.swapaxes(right_pair, 0, 1), "rows", axis=1, tiled=True)
    return right_gathered


def send_whole(tri_left, tri_right, left_side):
    both = ("branch", "rows")
    chans, tile_rows, columns = tri_left.shape
    halves = lax.axis_size("branch")
    tri_flat = jnp.stack([tri_left, tri_right], axis=1).reshape(chans, -1)
    left_dest = left_side.reshape(lax.axis_size("rows"), -1)
    payload = jnp.concatenate([tri_flat, jnp.tile(left_dest, (halves, 1))], axis=1)
    moved = lax.all_to_all(payload, both, split_axis=0, concat_axis=0, tiled=True)
    tri_moved = moved[:, : tri_flat.shape[1]].reshape(chans, 2, tile_rows, columns)
    left_gathered = moved[:, tri_flat.shape[1] :].reshape(halves, chans // halves, -1)
    left_gathered = jnp.swapaxes(left_gathered, 0, 1).reshape(chans, -1, left_side.shape[-1])
    return tri_moved[:, 0], tri_moved[:, 1], left_gathered


def send_back(product):
    return lax.all_to_all(product, ("branch", "rows"), split_axis=0, concat_axis=0, tiled=True)


def pair_front(pairwise_input, triangle_projection_weight):
    tile_rows, columns, chans = pairwise_input.shape
    pair_float = pairwise_input.astype(jnp.float32)
    pair_norm = standardize_features(pair_float, -1).astype(jnp.bfloat16)
    norm_flat = pair_norm.reshape(tile_rows * columns, chans)
    proj_flat = lax.dot_general(
        triangle_projection_weight,
        norm_flat,
        (((0,), (1,)), ((), ())),
        preferred_element_type=jnp.float32,
    )
    proj_tile = proj_flat[: 4 * chans].reshape(4 * chans, tile_rows, columns)
    gate_vals = jax.nn.sigmoid(proj_flat[4 * chans :])
    tri_left = (jax.nn.sigmoid(proj_tile[chans : 2 * chans]) * proj_tile[:chans]).astype(
        jnp.bfloat16
    )
    tri_right = (jax.nn.sigmoid(proj_tile[3 * chans :]) * proj_tile[2 * chans : 3 * chans]).astype(
        jnp.bfloat16
    )
    return pair_float, gate_vals, tri_left, tri_right


def triangle_product(left_chan, right_chan):
    halves = lax.axis_size("branch")
    columns = left_chan.shape[-1]
    tile_rows = left_chan.shape[1]
    left_src = left_chan.reshape(halves, -1, columns)
    right_src = right_chan.reshape(halves, halves, -1, columns)
    product = jnp.einsum(
        "bik,bhjk->hij", left_src, right_src, preferred_element_type=jnp.float32
    ).astype(jnp.bfloat16)
    return product.reshape(-1, tile_rows, columns)


def pair_back(
    pair_float,
    gate_vals,
    product_tile,
    triangle_output_weight,
    pairwise_up_weight,
    pairwise_down_weight,
):
    tile_rows, columns, chans = pair_float.shape
    prod_norm = (
        standardize_features(product_tile.astype(jnp.float32), 0)
        .astype(jnp.bfloat16)
        .reshape(chans, tile_rows * columns)
    )
    tri_update = lax.dot_general(
        triangle_output_weight,
        prod_norm,
        (((0,), (0,)), ((), ())),
        preferred_element_type=jnp.float32,
    )
    gated_update = jnp.transpose(gate_vals * tri_update).reshape(tile_rows, columns, chans)
    pair_mid = pair_float + gated_update
    mid_norm = standardize_features(pair_mid, -1).astype(jnp.bfloat16)
    pair_hidden = jax.nn.relu(
        jnp.einsum("ijd,dh->ijh", mid_norm, pairwise_up_weight, preferred_element_type=jnp.float32)
    ).astype(jnp.bfloat16)
    return pair_mid + jnp.einsum(
        "ijh,hd->ijd", pair_hidden, pairwise_down_weight, preferred_element_type=jnp.float32
    )


def outer_kernel(lt_ref, r_ref, wt_ref, out_ref, x_ref):
    n_factor = r_ref.shape[0]
    tile_rows = out_ref.shape[0]
    scale = 1.0 / r_ref.shape[1]

    def fill(d, carry):
        vals = jnp.dot(lt_ref[...], r_ref[d], preferred_element_type=jnp.float32)
        vals = (vals * scale).astype(jnp.bfloat16)
        start = pl.multiple_of(d * n_factor, n_factor)
        for i in range(tile_rows):
            x_ref[i, pl.ds(start, n_factor), :] = vals[i * n_factor : (i + 1) * n_factor, :]
        return carry

    lax.fori_loop(0, n_factor, fill, 0)

    def emit(i, carry):
        upd = jnp.dot(wt_ref[...], x_ref[i], preferred_element_type=jnp.float32)
        out_ref[i] = upd.T
        return carry

    lax.fori_loop(0, tile_rows, emit, 0)


def outer_product(left_gathered, right_gathered, outer_output_weight):
    total_rows, tile_rows, channels = left_gathered.shape
    columns = right_gathered.shape[2]
    pair = outer_output_weight.shape[1]
    left_t = jnp.transpose(left_gathered, (1, 2, 0)).reshape(tile_rows * channels, total_rows)
    weight_t = jnp.transpose(
        outer_output_weight.reshape(channels, channels, pair), (1, 0, 2)
    ).reshape(channels * channels, pair).T
    flops = 4 * tile_rows * channels * channels * columns * (total_rows + pair) // 2
    return pl.pallas_call(
        outer_kernel,
        out_shape=jax.ShapeDtypeStruct((tile_rows, columns, pair), jnp.float32),
        in_specs=[pl.BlockSpec(memory_space=pltpu.VMEM)] * 3,
        out_specs=pl.BlockSpec(memory_space=pltpu.VMEM),
        scratch_shapes=[pltpu.VMEM((tile_rows, channels * channels, columns), jnp.bfloat16)],
        compiler_params=pltpu.CompilerParams(vmem_limit_bytes=56 * 1024 * 1024),
        cost_estimate=pl.CostEstimate(
            flops=flops, transcendentals=0, bytes_accessed=right_gathered.size * 2 + tile_rows * columns * pair * 4
        ),
    )(left_t, right_gathered, weight_t)


def on_device(
    homolog_features,
    pairwise_input,
    transition_expand_matrix,
    transition_contract_matrix,
    factor_pair_matrices,
    outer_output_weight,
    triangle_projection_weight,
    triangle_output_weight,
    pairwise_up_weight,
    pairwise_down_weight,
):
    refreshed_homolog_features, left_side, right_side = alignment_branch(
        homolog_features, transition_expand_matrix, transition_contract_matrix, factor_pair_matrices
    )
    right_gathered = gather_sides(left_side, right_side)
    pairwise_input, right_side = lax.optimization_barrier((pairwise_input, right_side))
    pair_float, gate_vals, tri_left, tri_right = pair_front(
        pairwise_input, triangle_projection_weight
    )
    left_chan, right_chan, left_gathered = send_whole(tri_left, tri_right, left_side)
    product = triangle_product(left_chan, right_chan)
    product, left_gathered, right_gathered = lax.optimization_barrier(
        (product, left_gathered, right_gathered)
    )
    product_tile = send_back(product)
    outer_update = outer_product(left_gathered, right_gathered, outer_output_weight)
    product_tile, outer_update = lax.optimization_barrier((product_tile, outer_update))
    pair_mid = pair_back(
        pair_float,
        gate_vals,
        product_tile,
        triangle_output_weight,
        pairwise_up_weight,
        pairwise_down_weight,
    )
    pairwise_output = (pair_mid + outer_update).astype(jnp.bfloat16)
    return (refreshed_homolog_features, pairwise_output)


def solution(mesh):
    return jax.shard_map(
        on_device,
        mesh=mesh,
        in_specs=(
            P(("branch", "rows"), None, None),
            P("rows", "branch", None),
            P(),
            P(),
            P(),
            P(),
            P(),
            P(),
            P(),
            P(),
        ),
        out_specs=(P(("branch", "rows"), None, None), P("rows", "branch", None)),
        check_vma=False,
    )
```

```python
import jax
import jax.numpy as jnp
from jax import lax
from jax.experimental import pallas as pl
from jax.experimental.pallas import tpu as pltpu
from jax.sharding import PartitionSpec as P


def standardize_features(values, dimension):
    average = jnp.mean(values, axis=dimension, keepdims=True)
    centered = values - average
    variance = jnp.mean(centered * centered, axis=dimension, keepdims=True)
    return centered * lax.rsqrt(variance + 1e-05)


def alignment_branch(
    homolog_features, transition_expand_matrix, transition_contract_matrix, factor_pair_matrices
):
    local_rows, sequence_length, channel_width = homolog_features.shape
    homolog_real_matrix = homolog_features.astype(jnp.float32)
    standardized_homologs = (
        standardize_features(homolog_real_matrix, -1)
        .astype(jnp.bfloat16)
        .reshape(local_rows * sequence_length, channel_width)
    )
    expanded_activations = jax.nn.relu(
        jnp.dot(standardized_homologs, transition_expand_matrix, preferred_element_type=jnp.float32)
    ).astype(jnp.bfloat16)
    refreshed_homolog_features = (
        homolog_real_matrix
        + jnp.dot(
            expanded_activations, transition_contract_matrix, preferred_element_type=jnp.float32
        ).reshape(homolog_features.shape)
    ).astype(jnp.bfloat16)
    standardized_for_factors = (
        standardize_features(refreshed_homolog_features.astype(jnp.float32), -1)
        .astype(jnp.bfloat16)
        .reshape(local_rows * sequence_length, channel_width)
    )
    projected = jnp.dot(
        standardized_for_factors, factor_pair_matrices, preferred_element_type=jnp.float32
    ).reshape(local_rows, sequence_length, -1)
    channels = projected.shape[-1] // 2
    left_side = projected[..., :channels].astype(jnp.bfloat16)
    right_side = jnp.swapaxes(projected[..., channels:].astype(jnp.bfloat16), 1, 2)
    return (refreshed_homolog_features, left_side, right_side)


def branch_pair(mine, theirs):
    first = lax.axis_index("branch") == 0
    return jnp.where(first, jnp.concatenate([mine, theirs]), jnp.concatenate([theirs, mine]))


def gather_sides(left_side, right_side):
    swap = [(0, 1), (1, 0)]
    left_pair = branch_pair(left_side, lax.ppermute(left_side, "branch", swap))
    left_gathered = lax.all_to_all(left_pair, "rows", split_axis=1, concat_axis=0, tiled=True)
    half = right_side.shape[2] // 2
    me = lax.axis_index("branch")
    keep = lax.dynamic_slice_in_dim(right_side, me * half, half, axis=2)
    send = lax.dynamic_slice_in_dim(right_side, (1 - me) * half, half, axis=2)
    right_pair = branch_pair(keep, lax.ppermute(send, "branch", swap))
    right_gathered = lax.all_gather(jnp.swapaxes(right_pair, 0, 1), "rows", axis=1, tiled=True)
    return left_gathered, right_gathered


def send_whole(tri_left, tri_right):
    both = ("branch", "rows")
    moved = lax.all_to_all(
        jnp.stack([tri_left, tri_right], axis=1), both, split_axis=0, concat_axis=0, tiled=True
    )
    return moved[:, 0], moved[:, 1]


def send_back(product):
    return lax.all_to_all(product, ("branch", "rows"), split_axis=0, concat_axis=0, tiled=True)


def pair_front(pairwise_input, triangle_projection_weight):
    tile_rows, columns, chans = pairwise_input.shape
    pair_float = pairwise_input.astype(jnp.float32)
    pair_norm = standardize_features(pair_float, -1).astype(jnp.bfloat16)
    norm_flat = pair_norm.reshape(tile_rows * columns, chans)
    proj_flat = lax.dot_general(
        triangle_projection_weight[:, : 4 * chans],
        norm_flat,
        (((0,), (1,)), ((), ())),
        preferred_element_type=jnp.float32,
    )
    proj_tile = proj_flat.reshape(4 * chans, tile_rows, columns)
    tri_left = (jax.nn.sigmoid(proj_tile[chans : 2 * chans]) * proj_tile[:chans]).astype(
        jnp.bfloat16
    )
    tri_right = (jax.nn.sigmoid(proj_tile[3 * chans :]) * proj_tile[2 * chans : 3 * chans]).astype(
        jnp.bfloat16
    )
    return tri_left, tri_right


def triangle_product(left_chan, right_chan):
    halves = lax.axis_size("branch")
    columns = left_chan.shape[-1]
    tile_rows = left_chan.shape[1]
    left_src = left_chan.reshape(halves, -1, columns)
    right_src = right_chan.reshape(halves, halves, -1, columns)
    product = jnp.einsum(
        "bik,bhjk->hij", left_src, right_src, preferred_element_type=jnp.float32
    ).astype(jnp.bfloat16)
    return product.reshape(-1, tile_rows, columns)


def back_kernel(prod_ref, pair_ref, outer_ref, wo_ref, wg_ref, wu_ref, wd_ref, out_ref):
    rows, columns, chans = pair_ref.shape
    for r in range(rows):
        prod = prod_ref[:, r * columns : (r + 1) * columns].astype(jnp.float32)
        prod_norm = standardize_features(prod, 0).T.astype(jnp.bfloat16)
        tri_update = jnp.dot(prod_norm, wo_ref[...], preferred_element_type=jnp.float32)
        pair_float = pair_ref[r].astype(jnp.float32)
        pair_norm = standardize_features(pair_float, -1).astype(jnp.bfloat16)
        gate = jax.nn.sigmoid(
            jnp.dot(pair_norm, wg_ref[...], preferred_element_type=jnp.float32)
        )
        pair_mid = pair_float + gate * tri_update
        mid_norm = standardize_features(pair_mid, -1).astype(jnp.bfloat16)
        hidden = jnp.maximum(
            jnp.dot(mid_norm, wu_ref[...], preferred_element_type=jnp.float32), 0.0
        ).astype(jnp.bfloat16)
        down = jnp.dot(hidden, wd_ref[...], preferred_element_type=jnp.float32)
        out_ref[r] = (pair_mid + down + outer_ref[r]).astype(out_ref.dtype)


def pair_back(
    pairwise_input,
    product_tile,
    outer_update,
    triangle_projection_weight,
    triangle_output_weight,
    pairwise_up_weight,
    pairwise_down_weight,
):
    tile_rows, columns, chans = pairwise_input.shape
    step_rows = 4
    prod_flat = product_tile.reshape(chans, tile_rows * columns)
    gate_weight = triangle_projection_weight[:, 4 * chans :]
    hidden = pairwise_up_weight.shape[1]
    row_block = lambda g: (g, 0, 0)
    fixed = lambda g: (0, 0)
    return pl.pallas_call(
        back_kernel,
        out_shape=jax.ShapeDtypeStruct((tile_rows, columns, chans), jnp.bfloat16),
        grid=(tile_rows // step_rows,),
        in_specs=[
            pl.BlockSpec((chans, step_rows * columns), lambda g: (0, g)),
            pl.BlockSpec((step_rows, columns, chans), row_block),
            pl.BlockSpec((step_rows, columns, chans), row_block),
            pl.BlockSpec((chans, chans), fixed),
            pl.BlockSpec((chans, chans), fixed),
            pl.BlockSpec((chans, hidden), fixed),
            pl.BlockSpec((hidden, chans), fixed),
        ],
        out_specs=pl.BlockSpec((step_rows, columns, chans), row_block),
        cost_estimate=pl.CostEstimate(
            flops=2 * tile_rows * columns * chans * (3 * chans + 2 * hidden) // 1,
            transcendentals=tile_rows * columns * chans,
            bytes_accessed=tile_rows * columns * chans * 10,
        ),
    )(
        prod_flat,
        pairwise_input,
        outer_update,
        triangle_output_weight,
        gate_weight,
        pairwise_up_weight,
        pairwise_down_weight,
    )


def outer_kernel(lt_ref, r_ref, wt_ref, out_ref, x_ref):
    n_factor = r_ref.shape[0]
    tile_rows = out_ref.shape[0]
    scale = 1.0 / r_ref.shape[1]

    def fill(d, carry):
        vals = jnp.dot(lt_ref[...], r_ref[d], preferred_element_type=jnp.float32)
        vals = (vals * scale).astype(jnp.bfloat16)
        start = pl.multiple_of(d * n_factor, n_factor)
        for i in range(tile_rows):
            x_ref[i, pl.ds(start, n_factor), :] = vals[i * n_factor : (i + 1) * n_factor, :]
        return carry

    lax.fori_loop(0, n_factor, fill, 0)

    def emit(i, carry):
        upd = jnp.dot(wt_ref[...], x_ref[i], preferred_element_type=jnp.float32)
        out_ref[i] = upd.T
        return carry

    lax.fori_loop(0, tile_rows, emit, 0)


def outer_product(left_gathered, right_gathered, outer_output_weight):
    total_rows, tile_rows, channels = left_gathered.shape
    columns = right_gathered.shape[2]
    pair = outer_output_weight.shape[1]
    left_t = jnp.transpose(left_gathered, (1, 2, 0)).reshape(tile_rows * channels, total_rows)
    weight_t = jnp.transpose(
        outer_output_weight.reshape(channels, channels, pair), (1, 0, 2)
    ).reshape(channels * channels, pair).T
    flops = 4 * tile_rows * channels * channels * columns * (total_rows + pair) // 2
    return pl.pallas_call(
        outer_kernel,
        out_shape=jax.ShapeDtypeStruct((tile_rows, columns, pair), jnp.float32),
        in_specs=[pl.BlockSpec(memory_space=pltpu.VMEM)] * 3,
        out_specs=pl.BlockSpec(memory_space=pltpu.VMEM),
        scratch_shapes=[pltpu.VMEM((tile_rows, channels * channels, columns), jnp.bfloat16)],
        compiler_params=pltpu.CompilerParams(vmem_limit_bytes=56 * 1024 * 1024),
        cost_estimate=pl.CostEstimate(
            flops=flops, transcendentals=0, bytes_accessed=right_gathered.size * 2 + tile_rows * columns * pair * 4
        ),
    )(left_t, right_gathered, weight_t)


def on_device(
    homolog_features,
    pairwise_input,
    transition_expand_matrix,
    transition_contract_matrix,
    factor_pair_matrices,
    outer_output_weight,
    triangle_projection_weight,
    triangle_output_weight,
    pairwise_up_weight,
    pairwise_down_weight,
):
    refreshed_homolog_features, left_side, right_side = alignment_branch(
        homolog_features, transition_expand_matrix, transition_contract_matrix, factor_pair_matrices
    )
    left_gathered, right_gathered = gather_sides(left_side, right_side)
    pairwise_input, right_side = lax.optimization_barrier((pairwise_input, right_side))
    tri_left, tri_right = pair_front(
        pairwise_input, triangle_projection_weight
    )
    left_chan, right_chan = send_whole(tri_left, tri_right)
    product = triangle_product(left_chan, right_chan)
    product, left_gathered, right_gathered = lax.optimization_barrier(
        (product, left_gathered, right_gathered)
    )
    product_tile = send_back(product)
    outer_update = outer_product(left_gathered, right_gathered, outer_output_weight)
    product_tile, outer_update = lax.optimization_barrier((product_tile, outer_update))
    pairwise_output = pair_back(
        pairwise_input,
        product_tile,
        outer_update,
        triangle_projection_weight,
        triangle_output_weight,
        pairwise_up_weight,
        pairwise_down_weight,
    )
    return (refreshed_homolog_features, pairwise_output)


def solution(mesh):
    return jax.shard_map(
        on_device,
        mesh=mesh,
        in_specs=(
            P(("branch", "rows"), None, None),
            P("rows", "branch", None),
            P(),
            P(),
            P(),
            P(),
            P(),
            P(),
            P(),
            P(),
        ),
        out_specs=(P(("branch", "rows"), None, None), P("rows", "branch", None)),
        check_vma=False,
    )
```

```python
import jax
import jax.numpy as jnp
from jax import lax
from jax.experimental import pallas as pl
from jax.experimental.pallas import tpu as pltpu
from jax.sharding import PartitionSpec as P


def standardize_features(values, dimension):
    average = jnp.mean(values, axis=dimension, keepdims=True)
    centered = values - average
    variance = jnp.mean(centered * centered, axis=dimension, keepdims=True)
    return centered * lax.rsqrt(variance + 1e-05)


def alignment_branch(
    homolog_features, transition_expand_matrix, transition_contract_matrix, factor_pair_matrices
):
    local_rows, sequence_length, channel_width = homolog_features.shape
    homolog_real_matrix = homolog_features.astype(jnp.float32)
    standardized_homologs = (
        standardize_features(homolog_real_matrix, -1)
        .astype(jnp.bfloat16)
        .reshape(local_rows * sequence_length, channel_width)
    )
    expanded_activations = jax.nn.relu(
        jnp.dot(standardized_homologs, transition_expand_matrix, preferred_element_type=jnp.float32)
    ).astype(jnp.bfloat16)
    refreshed_homolog_features = (
        homolog_real_matrix
        + jnp.dot(
            expanded_activations, transition_contract_matrix, preferred_element_type=jnp.float32
        ).reshape(homolog_features.shape)
    ).astype(jnp.bfloat16)
    standardized_for_factors = (
        standardize_features(refreshed_homolog_features.astype(jnp.float32), -1)
        .astype(jnp.bfloat16)
        .reshape(local_rows * sequence_length, channel_width)
    )
    projected = jnp.dot(
        standardized_for_factors, factor_pair_matrices, preferred_element_type=jnp.float32
    ).reshape(local_rows, sequence_length, -1)
    channels = projected.shape[-1] // 2
    left_side = projected[..., :channels].astype(jnp.bfloat16)
    right_side = jnp.swapaxes(projected[..., channels:].astype(jnp.bfloat16), 1, 2)
    return (refreshed_homolog_features, left_side, right_side)


def branch_pair(mine, theirs):
    first = lax.axis_index("branch") == 0
    return jnp.where(first, jnp.concatenate([mine, theirs]), jnp.concatenate([theirs, mine]))


def gather_sides(left_side, right_side):
    swap = [(0, 1), (1, 0)]
    left_pair = branch_pair(left_side, lax.ppermute(left_side, "branch", swap))
    left_gathered = lax.all_to_all(left_pair, "rows", split_axis=1, concat_axis=0, tiled=True)
    half = right_side.shape[2] // 2
    me = lax.axis_index("branch")
    keep = lax.dynamic_slice_in_dim(right_side, me * half, half, axis=2)
    send = lax.dynamic_slice_in_dim(right_side, (1 - me) * half, half, axis=2)
    right_pair = branch_pair(keep, lax.ppermute(send, "branch", swap))
    right_gathered = lax.all_gather(jnp.swapaxes(right_pair, 0, 1), "rows", axis=1, tiled=True)
    return left_gathered, right_gathered


def send_whole(tri_left, tri_right):
    both = ("branch", "rows")
    moved = lax.all_to_all(
        jnp.stack([tri_left, tri_right], axis=1), both, split_axis=0, concat_axis=0, tiled=True
    )
    return moved[:, 0], moved[:, 1]


def send_back(product):
    return lax.all_to_all(product, ("branch", "rows"), split_axis=0, concat_axis=0, tiled=True)


def front_kernel(pair_ref, wt_ref, left_ref, right_ref):
    rows, columns, chans = pair_ref.shape
    for r in range(rows):
        pair_norm = standardize_features(pair_ref[r].astype(jnp.float32), -1).astype(jnp.bfloat16)
        proj = lax.dot_general(
            wt_ref[...], pair_norm, (((1,), (1,)), ((), ())), preferred_element_type=jnp.float32
        )
        cols = slice(r * columns, (r + 1) * columns)
        left_ref[:, cols] = (
            jax.nn.sigmoid(proj[chans : 2 * chans]) * proj[:chans]
        ).astype(left_ref.dtype)
        right_ref[:, cols] = (
            jax.nn.sigmoid(proj[3 * chans :]) * proj[2 * chans : 3 * chans]
        ).astype(right_ref.dtype)


def pair_front(pairwise_input, triangle_projection_weight):
    tile_rows, columns, chans = pairwise_input.shape
    step_rows = 4
    weight_t = triangle_projection_weight[:, : 4 * chans].T
    side = jax.ShapeDtypeStruct((chans, tile_rows * columns), jnp.bfloat16)
    out_block = pl.BlockSpec((chans, step_rows * columns), lambda g: (0, g))
    tri_left, tri_right = pl.pallas_call(
        front_kernel,
        out_shape=(side, side),
        grid=(tile_rows // step_rows,),
        in_specs=[
            pl.BlockSpec((step_rows, columns, chans), lambda g: (g, 0, 0)),
            pl.BlockSpec((4 * chans, chans), lambda g: (0, 0)),
        ],
        out_specs=(out_block, out_block),
        cost_estimate=pl.CostEstimate(
            flops=2 * tile_rows * columns * chans * 4 * chans,
            transcendentals=2 * tile_rows * columns * chans,
            bytes_accessed=tile_rows * columns * chans * 6,
        ),
    )(pairwise_input, weight_t)
    return (
        tri_left.reshape(chans, tile_rows, columns),
        tri_right.reshape(chans, tile_rows, columns),
    )


def triangle_product(left_chan, right_chan):
    halves = lax.axis_size("branch")
    columns = left_chan.shape[-1]
    tile_rows = left_chan.shape[1]
    left_src = left_chan.reshape(halves, -1, columns)
    right_src = right_chan.reshape(halves, halves, -1, columns)
    product = jnp.einsum(
        "bik,bhjk->hij", left_src, right_src, preferred_element_type=jnp.float32
    ).astype(jnp.bfloat16)
    return product.reshape(-1, tile_rows, columns)


def back_kernel(prod_ref, pair_ref, outer_ref, wo_ref, wg_ref, wu_ref, wd_ref, out_ref):
    rows, columns, chans = pair_ref.shape
    for r in range(rows):
        prod = prod_ref[:, r * columns : (r + 1) * columns].astype(jnp.float32)
        prod_norm = standardize_features(prod, 0).T.astype(jnp.bfloat16)
        tri_update = jnp.dot(prod_norm, wo_ref[...], preferred_element_type=jnp.float32)
        pair_float = pair_ref[r].astype(jnp.float32)
        pair_norm = standardize_features(pair_float, -1).astype(jnp.bfloat16)
        gate = jax.nn.sigmoid(
            jnp.dot(pair_norm, wg_ref[...], preferred_element_type=jnp.float32)
        )
        pair_mid = pair_float + gate * tri_update
        mid_norm = standardize_features(pair_mid, -1).astype(jnp.bfloat16)
        hidden = jnp.maximum(
            jnp.dot(mid_norm, wu_ref[...], preferred_element_type=jnp.float32), 0.0
        ).astype(jnp.bfloat16)
        down = jnp.dot(hidden, wd_ref[...], preferred_element_type=jnp.float32)
        out_ref[r] = (pair_mid + down + outer_ref[r]).astype(out_ref.dtype)


def pair_back(
    pairwise_input,
    product_tile,
    outer_update,
    triangle_projection_weight,
    triangle_output_weight,
    pairwise_up_weight,
    pairwise_down_weight,
):
    tile_rows, columns, chans = pairwise_input.shape
    step_rows = 4
    prod_flat = product_tile.reshape(chans, tile_rows * columns)
    gate_weight = triangle_projection_weight[:, 4 * chans :]
    hidden = pairwise_up_weight.shape[1]
    row_block = lambda g: (g, 0, 0)
    fixed = lambda g: (0, 0)
    return pl.pallas_call(
        back_kernel,
        out_shape=jax.ShapeDtypeStruct((tile_rows, columns, chans), jnp.bfloat16),
        grid=(tile_rows // step_rows,),
        in_specs=[
            pl.BlockSpec((chans, step_rows * columns), lambda g: (0, g)),
            pl.BlockSpec((step_rows, columns, chans), row_block),
            pl.BlockSpec((step_rows, columns, chans), row_block),
            pl.BlockSpec((chans, chans), fixed),
            pl.BlockSpec((chans, chans), fixed),
            pl.BlockSpec((chans, hidden), fixed),
            pl.BlockSpec((hidden, chans), fixed),
        ],
        out_specs=pl.BlockSpec((step_rows, columns, chans), row_block),
        cost_estimate=pl.CostEstimate(
            flops=2 * tile_rows * columns * chans * (3 * chans + 2 * hidden) // 1,
            transcendentals=tile_rows * columns * chans,
            bytes_accessed=tile_rows * columns * chans * 10,
        ),
    )(
        prod_flat,
        pairwise_input,
        outer_update,
        triangle_output_weight,
        gate_weight,
        pairwise_up_weight,
        pairwise_down_weight,
    )


def outer_kernel(lt_ref, r_ref, wt_ref, out_ref, x_ref):
    n_factor = r_ref.shape[0]
    tile_rows = out_ref.shape[0]
    scale = 1.0 / r_ref.shape[1]

    def fill(d, carry):
        vals = jnp.dot(lt_ref[...], r_ref[d], preferred_element_type=jnp.float32)
        vals = (vals * scale).astype(jnp.bfloat16)
        start = pl.multiple_of(d * n_factor, n_factor)
        for i in range(tile_rows):
            x_ref[i, pl.ds(start, n_factor), :] = vals[i * n_factor : (i + 1) * n_factor, :]
        return carry

    lax.fori_loop(0, n_factor, fill, 0)

    def emit(i, carry):
        upd = jnp.dot(wt_ref[...], x_ref[i], preferred_element_type=jnp.float32)
        out_ref[i] = upd.T
        return carry

    lax.fori_loop(0, tile_rows, emit, 0)


def outer_product(left_gathered, right_gathered, outer_output_weight):
    total_rows, tile_rows, channels = left_gathered.shape
    columns = right_gathered.shape[2]
    pair = outer_output_weight.shape[1]
    left_t = jnp.transpose(left_gathered, (1, 2, 0)).reshape(tile_rows * channels, total_rows)
    weight_t = jnp.transpose(
        outer_output_weight.reshape(channels, channels, pair), (1, 0, 2)
    ).reshape(channels * channels, pair).T
    flops = 4 * tile_rows * channels * channels * columns * (total_rows + pair) // 2
    return pl.pallas_call(
        outer_kernel,
        out_shape=jax.ShapeDtypeStruct((tile_rows, columns, pair), jnp.float32),
        in_specs=[pl.BlockSpec(memory_space=pltpu.VMEM)] * 3,
        out_specs=pl.BlockSpec(memory_space=pltpu.VMEM),
        scratch_shapes=[pltpu.VMEM((tile_rows, channels * channels, columns), jnp.bfloat16)],
        compiler_params=pltpu.CompilerParams(vmem_limit_bytes=56 * 1024 * 1024),
        cost_estimate=pl.CostEstimate(
            flops=flops, transcendentals=0, bytes_accessed=right_gathered.size * 2 + tile_rows * columns * pair * 4
        ),
    )(left_t, right_gathered, weight_t)


def on_device(
    homolog_features,
    pairwise_input,
    transition_expand_matrix,
    transition_contract_matrix,
    factor_pair_matrices,
    outer_output_weight,
    triangle_projection_weight,
    triangle_output_weight,
    pairwise_up_weight,
    pairwise_down_weight,
):
    refreshed_homolog_features, left_side, right_side = alignment_branch(
        homolog_features, transition_expand_matrix, transition_contract_matrix, factor_pair_matrices
    )
    left_gathered, right_gathered = gather_sides(left_side, right_side)
    pairwise_input, right_side = lax.optimization_barrier((pairwise_input, right_side))
    tri_left, tri_right = pair_front(
        pairwise_input, triangle_projection_weight
    )
    left_chan, right_chan = send_whole(tri_left, tri_right)
    product = triangle_product(left_chan, right_chan)
    product, left_gathered, right_gathered = lax.optimization_barrier(
        (product, left_gathered, right_gathered)
    )
    product_tile = send_back(product)
    outer_update = outer_product(left_gathered, right_gathered, outer_output_weight)
    product_tile, outer_update = lax.optimization_barrier((product_tile, outer_update))
    pairwise_output = pair_back(
        pairwise_input,
        product_tile,
        outer_update,
        triangle_projection_weight,
        triangle_output_weight,
        pairwise_up_weight,
        pairwise_down_weight,
    )
    return (refreshed_homolog_features, pairwise_output)


def solution(mesh):
    return jax.shard_map(
        on_device,
        mesh=mesh,
        in_specs=(
            P(("branch", "rows"), None, None),
            P("rows", "branch", None),
            P(),
            P(),
            P(),
            P(),
            P(),
            P(),
            P(),
            P(),
        ),
        out_specs=(P(("branch", "rows"), None, None), P("rows", "branch", None)),
        check_vma=False,
    )
```

```python
import jax
import jax.numpy as jnp
from jax import lax
from jax.experimental import pallas as pl
from jax.experimental.pallas import tpu as pltpu
from jax.sharding import PartitionSpec as P


def standardize_features(values, dimension):
    average = jnp.mean(values, axis=dimension, keepdims=True)
    centered = values - average
    variance = jnp.mean(centered * centered, axis=dimension, keepdims=True)
    return centered * lax.rsqrt(variance + 1e-05)


def alignment_branch(
    homolog_features, transition_expand_matrix, transition_contract_matrix, factor_pair_matrices
):
    local_rows, sequence_length, channel_width = homolog_features.shape
    homolog_real_matrix = homolog_features.astype(jnp.float32)
    standardized_homologs = (
        standardize_features(homolog_real_matrix, -1)
        .astype(jnp.bfloat16)
        .reshape(local_rows * sequence_length, channel_width)
    )
    expanded_activations = jax.nn.relu(
        jnp.dot(standardized_homologs, transition_expand_matrix, preferred_element_type=jnp.float32)
    ).astype(jnp.bfloat16)
    refreshed_homolog_features = (
        homolog_real_matrix
        + jnp.dot(
            expanded_activations, transition_contract_matrix, preferred_element_type=jnp.float32
        ).reshape(homolog_features.shape)
    ).astype(jnp.bfloat16)
    standardized_for_factors = (
        standardize_features(refreshed_homolog_features.astype(jnp.float32), -1)
        .astype(jnp.bfloat16)
        .reshape(local_rows * sequence_length, channel_width)
    )
    projected = jnp.dot(
        standardized_for_factors, factor_pair_matrices, preferred_element_type=jnp.float32
    ).reshape(local_rows, sequence_length, -1)
    channels = projected.shape[-1] // 2
    left_side = projected[..., :channels].astype(jnp.bfloat16)
    right_side = jnp.swapaxes(projected[..., channels:].astype(jnp.bfloat16), 1, 2)
    return (refreshed_homolog_features, left_side, right_side)


def branch_pair(mine, theirs):
    first = lax.axis_index("branch") == 0
    return jnp.where(first, jnp.concatenate([mine, theirs]), jnp.concatenate([theirs, mine]))


def gather_sides(left_side, right_side):
    swap = [(0, 1), (1, 0)]
    left_pair = branch_pair(left_side, lax.ppermute(left_side, "branch", swap))
    left_gathered = lax.all_to_all(left_pair, "rows", split_axis=1, concat_axis=0, tiled=True)
    half = right_side.shape[2] // 2
    me = lax.axis_index("branch")
    keep = lax.dynamic_slice_in_dim(right_side, me * half, half, axis=2)
    send = lax.dynamic_slice_in_dim(right_side, (1 - me) * half, half, axis=2)
    right_pair = branch_pair(keep, lax.ppermute(send, "branch", swap))
    right_gathered = lax.all_gather(jnp.swapaxes(right_pair, 0, 1), "rows", axis=1, tiled=True)
    return left_gathered, right_gathered


def send_whole(tri_left, tri_right):
    both = ("branch", "rows")
    moved = lax.all_to_all(
        jnp.stack([tri_left, tri_right], axis=1), both, split_axis=0, concat_axis=0, tiled=True
    )
    return moved


def send_back(product):
    return lax.all_to_all(product, ("branch", "rows"), split_axis=0, concat_axis=0, tiled=True)


def front_kernel(pair_ref, wt_ref, left_ref, right_ref):
    rows, columns, chans = pair_ref.shape
    for r in range(rows):
        pair_norm = standardize_features(pair_ref[r].astype(jnp.float32), -1).astype(jnp.bfloat16)
        proj = lax.dot_general(
            wt_ref[...], pair_norm, (((1,), (1,)), ((), ())), preferred_element_type=jnp.float32
        )
        cols = slice(r * columns, (r + 1) * columns)
        left_ref[:, cols] = (
            jax.nn.sigmoid(proj[chans : 2 * chans]) * proj[:chans]
        ).astype(left_ref.dtype)
        right_ref[:, cols] = (
            jax.nn.sigmoid(proj[3 * chans :]) * proj[2 * chans : 3 * chans]
        ).astype(right_ref.dtype)


def pair_front(pairwise_input, triangle_projection_weight):
    tile_rows, columns, chans = pairwise_input.shape
    step_rows = 4
    weight_t = triangle_projection_weight[:, : 4 * chans].T
    side = jax.ShapeDtypeStruct((chans, tile_rows * columns), jnp.bfloat16)
    out_block = pl.BlockSpec((chans, step_rows * columns), lambda g: (0, g))
    tri_left, tri_right = pl.pallas_call(
        front_kernel,
        out_shape=(side, side),
        grid=(tile_rows // step_rows,),
        in_specs=[
            pl.BlockSpec((step_rows, columns, chans), lambda g: (g, 0, 0)),
            pl.BlockSpec((4 * chans, chans), lambda g: (0, 0)),
        ],
        out_specs=(out_block, out_block),
        cost_estimate=pl.CostEstimate(
            flops=2 * tile_rows * columns * chans * 4 * chans,
            transcendentals=2 * tile_rows * columns * chans,
            bytes_accessed=tile_rows * columns * chans * 6,
        ),
    )(pairwise_input, weight_t)
    return (
        tri_left.reshape(chans, tile_rows, columns),
        tri_right.reshape(chans, tile_rows, columns),
    )


def product_kernel(moved_ref, out_ref):
    halves, span, columns = out_ref.shape
    n_src, _, tile_rows, _ = moved_ref.shape
    per_half = n_src // halves
    per_out = per_half // halves
    for h in range(halves):
        total = None
        for b in range(halves):
            left = moved_ref[b * per_half : (b + 1) * per_half, 0]
            first = b * per_half + h * per_out
            right = moved_ref[first : first + per_out, 1]
            part = lax.dot_general(
                left.reshape(per_half * tile_rows, columns),
                right.reshape(per_out * tile_rows, columns),
                (((1,), (1,)), ((), ())),
                preferred_element_type=jnp.float32,
            )
            total = part if total is None else total + part
        out_ref[h] = total.astype(out_ref.dtype)


def triangle_product(moved):
    n_src, _, tile_rows, columns = moved.shape
    halves = lax.axis_size("branch")
    product = pl.pallas_call(
        product_kernel,
        out_shape=jax.ShapeDtypeStruct((halves, n_src * tile_rows // halves, columns), jnp.bfloat16),
        in_specs=[pl.BlockSpec(memory_space=pltpu.VMEM)],
        out_specs=pl.BlockSpec(memory_space=pltpu.VMEM),
        cost_estimate=pl.CostEstimate(
            flops=2 * (n_src * tile_rows) ** 2 * columns // halves,
            transcendentals=0,
            bytes_accessed=moved.size * 2 + n_src * tile_rows * columns * 2,
        ),
    )(moved)
    return product.reshape(-1, tile_rows, columns)


def back_kernel(prod_ref, pair_ref, outer_ref, wo_ref, wg_ref, wu_ref, wd_ref, out_ref):
    rows, columns, chans = pair_ref.shape
    for r in range(rows):
        prod = prod_ref[:, r * columns : (r + 1) * columns].astype(jnp.float32)
        prod_norm = standardize_features(prod, 0).T.astype(jnp.bfloat16)
        tri_update = jnp.dot(prod_norm, wo_ref[...], preferred_element_type=jnp.float32)
        pair_float = pair_ref[r].astype(jnp.float32)
        pair_norm = standardize_features(pair_float, -1).astype(jnp.bfloat16)
        gate = jax.nn.sigmoid(
            jnp.dot(pair_norm, wg_ref[...], preferred_element_type=jnp.float32)
        )
        pair_mid = pair_float + gate * tri_update
        mid_norm = standardize_features(pair_mid, -1).astype(jnp.bfloat16)
        hidden = jnp.maximum(
            jnp.dot(mid_norm, wu_ref[...], preferred_element_type=jnp.float32), 0.0
        ).astype(jnp.bfloat16)
        down = jnp.dot(hidden, wd_ref[...], preferred_element_type=jnp.float32)
        out_ref[r] = (pair_mid + down + outer_ref[r]).astype(out_ref.dtype)


def pair_back(
    pairwise_input,
    product_tile,
    outer_update,
    triangle_projection_weight,
    triangle_output_weight,
    pairwise_up_weight,
    pairwise_down_weight,
):
    tile_rows, columns, chans = pairwise_input.shape
    step_rows = 4
    prod_flat = product_tile.reshape(chans, tile_rows * columns)
    gate_weight = triangle_projection_weight[:, 4 * chans :]
    hidden = pairwise_up_weight.shape[1]
    row_block = lambda g: (g, 0, 0)
    fixed = lambda g: (0, 0)
    return pl.pallas_call(
        back_kernel,
        out_shape=jax.ShapeDtypeStruct((tile_rows, columns, chans), jnp.bfloat16),
        grid=(tile_rows // step_rows,),
        in_specs=[
            pl.BlockSpec((chans, step_rows * columns), lambda g: (0, g)),
            pl.BlockSpec((step_rows, columns, chans), row_block),
            pl.BlockSpec((step_rows, columns, chans), row_block),
            pl.BlockSpec((chans, chans), fixed),
            pl.BlockSpec((chans, chans), fixed),
            pl.BlockSpec((chans, hidden), fixed),
            pl.BlockSpec((hidden, chans), fixed),
        ],
        out_specs=pl.BlockSpec((step_rows, columns, chans), row_block),
        cost_estimate=pl.CostEstimate(
            flops=2 * tile_rows * columns * chans * (3 * chans + 2 * hidden) // 1,
            transcendentals=tile_rows * columns * chans,
            bytes_accessed=tile_rows * columns * chans * 10,
        ),
    )(
        prod_flat,
        pairwise_input,
        outer_update,
        triangle_output_weight,
        gate_weight,
        pairwise_up_weight,
        pairwise_down_weight,
    )


def outer_kernel(lt_ref, r_ref, wt_ref, out_ref, x_ref):
    n_factor = r_ref.shape[0]
    tile_rows = out_ref.shape[0]
    scale = 1.0 / r_ref.shape[1]

    def fill(d, carry):
        vals = jnp.dot(lt_ref[...], r_ref[d], preferred_element_type=jnp.float32)
        vals = (vals * scale).astype(jnp.bfloat16)
        start = pl.multiple_of(d * n_factor, n_factor)
        for i in range(tile_rows):
            x_ref[i, pl.ds(start, n_factor), :] = vals[i * n_factor : (i + 1) * n_factor, :]
        return carry

    lax.fori_loop(0, n_factor, fill, 0)

    def emit(i, carry):
        upd = jnp.dot(wt_ref[...], x_ref[i], preferred_element_type=jnp.float32)
        out_ref[i] = upd.T
        return carry

    lax.fori_loop(0, tile_rows, emit, 0)


def outer_product(left_gathered, right_gathered, outer_output_weight):
    total_rows, tile_rows, channels = left_gathered.shape
    columns = right_gathered.shape[2]
    pair = outer_output_weight.shape[1]
    left_t = jnp.transpose(left_gathered, (1, 2, 0)).reshape(tile_rows * channels, total_rows)
    weight_t = jnp.transpose(
        outer_output_weight.reshape(channels, channels, pair), (1, 0, 2)
    ).reshape(channels * channels, pair).T
    flops = 4 * tile_rows * channels * channels * columns * (total_rows + pair) // 2
    return pl.pallas_call(
        outer_kernel,
        out_shape=jax.ShapeDtypeStruct((tile_rows, columns, pair), jnp.float32),
        in_specs=[pl.BlockSpec(memory_space=pltpu.VMEM)] * 3,
        out_specs=pl.BlockSpec(memory_space=pltpu.VMEM),
        scratch_shapes=[pltpu.VMEM((tile_rows, channels * channels, columns), jnp.bfloat16)],
        compiler_params=pltpu.CompilerParams(vmem_limit_bytes=56 * 1024 * 1024),
        cost_estimate=pl.CostEstimate(
            flops=flops, transcendentals=0, bytes_accessed=right_gathered.size * 2 + tile_rows * columns * pair * 4
        ),
    )(left_t, right_gathered, weight_t)


def on_device(
    homolog_features,
    pairwise_input,
    transition_expand_matrix,
    transition_contract_matrix,
    factor_pair_matrices,
    outer_output_weight,
    triangle_projection_weight,
    triangle_output_weight,
    pairwise_up_weight,
    pairwise_down_weight,
):
    refreshed_homolog_features, left_side, right_side = alignment_branch(
        homolog_features, transition_expand_matrix, transition_contract_matrix, factor_pair_matrices
    )
    left_gathered, right_gathered = gather_sides(left_side, right_side)
    pairwise_input, right_side = lax.optimization_barrier((pairwise_input, right_side))
    tri_left, tri_right = pair_front(
        pairwise_input, triangle_projection_weight
    )
    moved = send_whole(tri_left, tri_right)
    product = triangle_product(moved)
    product, left_gathered, right_gathered = lax.optimization_barrier(
        (product, left_gathered, right_gathered)
    )
    product_tile = send_back(product)
    outer_update = outer_product(left_gathered, right_gathered, outer_output_weight)
    product_tile, outer_update = lax.optimization_barrier((product_tile, outer_update))
    pairwise_output = pair_back(
        pairwise_input,
        product_tile,
        outer_update,
        triangle_projection_weight,
        triangle_output_weight,
        pairwise_up_weight,
        pairwise_down_weight,
    )
    return (refreshed_homolog_features, pairwise_output)


def solution(mesh):
    return jax.shard_map(
        on_device,
        mesh=mesh,
        in_specs=(
            P(("branch", "rows"), None, None),
            P("rows", "branch", None),
            P(),
            P(),
            P(),
            P(),
            P(),
            P(),
            P(),
            P(),
        ),
        out_specs=(P(("branch", "rows"), None, None), P("rows", "branch", None)),
        check_vma=False,
    )
```

```python
import jax
import jax.numpy as jnp
from jax import lax
from jax.experimental import pallas as pl
from jax.experimental.pallas import tpu as pltpu
from jax.sharding import PartitionSpec as P


def standardize_features(values, dimension):
    average = jnp.mean(values, axis=dimension, keepdims=True)
    centered = values - average
    variance = jnp.mean(centered * centered, axis=dimension, keepdims=True)
    return centered * lax.rsqrt(variance + 1e-05)


def alignment_branch(
    homolog_features, transition_expand_matrix, transition_contract_matrix, factor_pair_matrices
):
    local_rows, sequence_length, channel_width = homolog_features.shape
    homolog_real_matrix = homolog_features.astype(jnp.float32)
    standardized_homologs = (
        standardize_features(homolog_real_matrix, -1)
        .astype(jnp.bfloat16)
        .reshape(local_rows * sequence_length, channel_width)
    )
    expanded_activations = jax.nn.relu(
        jnp.dot(standardized_homologs, transition_expand_matrix, preferred_element_type=jnp.float32)
    ).astype(jnp.bfloat16)
    refreshed_homolog_features = (
        homolog_real_matrix
        + jnp.dot(
            expanded_activations, transition_contract_matrix, preferred_element_type=jnp.float32
        ).reshape(homolog_features.shape)
    ).astype(jnp.bfloat16)
    standardized_for_factors = (
        standardize_features(refreshed_homolog_features.astype(jnp.float32), -1)
        .astype(jnp.bfloat16)
        .reshape(local_rows * sequence_length, channel_width)
    )
    projected = jnp.dot(
        standardized_for_factors, factor_pair_matrices, preferred_element_type=jnp.float32
    ).reshape(local_rows, sequence_length, -1)
    channels = projected.shape[-1] // 2
    left_side = projected[..., :channels].astype(jnp.bfloat16)
    right_side = jnp.swapaxes(projected[..., channels:].astype(jnp.bfloat16), 1, 2)
    return (refreshed_homolog_features, left_side, right_side)


def branch_pair(mine, theirs):
    first = lax.axis_index("branch") == 0
    return jnp.where(first, jnp.concatenate([mine, theirs]), jnp.concatenate([theirs, mine]))


def gather_sides(left_side, right_side):
    swap = [(0, 1), (1, 0)]
    left_pair = branch_pair(left_side, lax.ppermute(left_side, "branch", swap))
    left_gathered = lax.all_to_all(left_pair, "rows", split_axis=1, concat_axis=0, tiled=True)
    half = right_side.shape[2] // 2
    me = lax.axis_index("branch")
    keep = lax.dynamic_slice_in_dim(right_side, me * half, half, axis=2)
    send = lax.dynamic_slice_in_dim(right_side, (1 - me) * half, half, axis=2)
    right_pair = branch_pair(keep, lax.ppermute(send, "branch", swap))
    right_gathered = lax.all_gather(jnp.swapaxes(right_pair, 0, 1), "rows", axis=1, tiled=True)
    return left_gathered, right_gathered


def send_whole(tri_left, tri_right):
    both = ("branch", "rows")
    moved = lax.all_to_all(
        jnp.stack([tri_left, tri_right], axis=1), both, split_axis=0, concat_axis=0, tiled=True
    )
    return moved


def send_back(product):
    return lax.all_to_all(product, ("branch", "rows"), split_axis=0, concat_axis=0, tiled=True)


def front_kernel(pair_ref, wt_ref, left_ref, right_ref):
    rows, columns, chans = pair_ref.shape
    for r in range(rows):
        pair_norm = standardize_features(pair_ref[r].astype(jnp.float32), -1).astype(jnp.bfloat16)
        proj = lax.dot_general(
            wt_ref[...], pair_norm, (((1,), (1,)), ((), ())), preferred_element_type=jnp.float32
        )
        cols = slice(r * columns, (r + 1) * columns)
        left_ref[:, cols] = (
            jax.nn.sigmoid(proj[chans : 2 * chans]) * proj[:chans]
        ).astype(left_ref.dtype)
        right_ref[:, cols] = (
            jax.nn.sigmoid(proj[3 * chans :]) * proj[2 * chans : 3 * chans]
        ).astype(right_ref.dtype)


def pair_front(pairwise_input, triangle_projection_weight):
    tile_rows, columns, chans = pairwise_input.shape
    step_rows = 4
    weight_t = triangle_projection_weight[:, : 4 * chans].T
    side = jax.ShapeDtypeStruct((chans, tile_rows * columns), jnp.bfloat16)
    out_block = pl.BlockSpec((chans, step_rows * columns), lambda g: (0, g))
    tri_left, tri_right = pl.pallas_call(
        front_kernel,
        out_shape=(side, side),
        grid=(tile_rows // step_rows,),
        in_specs=[
            pl.BlockSpec((step_rows, columns, chans), lambda g: (g, 0, 0)),
            pl.BlockSpec((4 * chans, chans), lambda g: (0, 0)),
        ],
        out_specs=(out_block, out_block),
        cost_estimate=pl.CostEstimate(
            flops=2 * tile_rows * columns * chans * 4 * chans,
            transcendentals=2 * tile_rows * columns * chans,
            bytes_accessed=tile_rows * columns * chans * 6,
        ),
    )(pairwise_input, weight_t)
    return (
        tri_left.reshape(chans, tile_rows, columns),
        tri_right.reshape(chans, tile_rows, columns),
    )


def product_kernel(moved_ref, out_ref):
    halves, span, columns = out_ref.shape
    n_src, _, tile_rows, _ = moved_ref.shape
    per_half = n_src // halves
    per_out = per_half // halves
    for h in range(halves):
        total = None
        for b in range(halves):
            left = moved_ref[b * per_half : (b + 1) * per_half, 0]
            first = b * per_half + h * per_out
            right = moved_ref[first : first + per_out, 1]
            part = lax.dot_general(
                left.reshape(per_half * tile_rows, columns),
                right.reshape(per_out * tile_rows, columns),
                (((1,), (1,)), ((), ())),
                preferred_element_type=jnp.float32,
            )
            total = part if total is None else total + part
        out_ref[h] = total.astype(out_ref.dtype)


def triangle_product(moved):
    n_src, _, tile_rows, columns = moved.shape
    halves = lax.axis_size("branch")
    product = pl.pallas_call(
        product_kernel,
        out_shape=jax.ShapeDtypeStruct((halves, n_src * tile_rows // halves, columns), jnp.bfloat16),
        in_specs=[pl.BlockSpec(memory_space=pltpu.VMEM)],
        out_specs=pl.BlockSpec(memory_space=pltpu.VMEM),
        cost_estimate=pl.CostEstimate(
            flops=2 * (n_src * tile_rows) ** 2 * columns // halves,
            transcendentals=0,
            bytes_accessed=moved.size * 2 + n_src * tile_rows * columns * 2,
        ),
    )(moved)
    return product.reshape(-1, tile_rows, columns)


def back_kernel(prod_ref, pair_ref, outer_ref, wo_ref, wg_ref, wu_ref, wd_ref, out_ref):
    rows, columns, chans = pair_ref.shape
    for r in range(rows):
        prod = prod_ref[:, r * columns : (r + 1) * columns].astype(jnp.float32)
        prod_norm = standardize_features(prod, 0).T.astype(jnp.bfloat16)
        tri_update = jnp.dot(prod_norm, wo_ref[...], preferred_element_type=jnp.float32)
        pair_float = pair_ref[r].astype(jnp.float32)
        pair_norm = standardize_features(pair_float, -1).astype(jnp.bfloat16)
        gate = jax.nn.sigmoid(
            jnp.dot(pair_norm, wg_ref[...], preferred_element_type=jnp.float32)
        )
        pair_mid = pair_float + gate * tri_update
        mid_norm = standardize_features(pair_mid, -1).astype(jnp.bfloat16)
        hidden = jnp.maximum(
            jnp.dot(mid_norm, wu_ref[...], preferred_element_type=jnp.float32), 0.0
        ).astype(jnp.bfloat16)
        down = jnp.dot(hidden, wd_ref[...], preferred_element_type=jnp.float32)
        out_ref[r] = (pair_mid + down + outer_ref[r]).astype(out_ref.dtype)


def pair_back(
    pairwise_input,
    product_tile,
    outer_update,
    triangle_projection_weight,
    triangle_output_weight,
    pairwise_up_weight,
    pairwise_down_weight,
):
    tile_rows, columns, chans = pairwise_input.shape
    step_rows = 4
    prod_flat = product_tile.reshape(chans, tile_rows * columns)
    gate_weight = triangle_projection_weight[:, 4 * chans :]
    hidden = pairwise_up_weight.shape[1]
    row_block = lambda g: (g, 0, 0)
    fixed = lambda g: (0, 0)
    return pl.pallas_call(
        back_kernel,
        out_shape=jax.ShapeDtypeStruct((tile_rows, columns, chans), jnp.bfloat16),
        grid=(tile_rows // step_rows,),
        in_specs=[
            pl.BlockSpec((chans, step_rows * columns), lambda g: (0, g)),
            pl.BlockSpec((step_rows, columns, chans), row_block),
            pl.BlockSpec((step_rows, columns, chans), row_block),
            pl.BlockSpec((chans, chans), fixed),
            pl.BlockSpec((chans, chans), fixed),
            pl.BlockSpec((chans, hidden), fixed),
            pl.BlockSpec((hidden, chans), fixed),
        ],
        out_specs=pl.BlockSpec((step_rows, columns, chans), row_block),
        cost_estimate=pl.CostEstimate(
            flops=2 * tile_rows * columns * chans * (3 * chans + 2 * hidden) // 1,
            transcendentals=tile_rows * columns * chans,
            bytes_accessed=tile_rows * columns * chans * 10,
        ),
    )(
        prod_flat,
        pairwise_input,
        outer_update,
        triangle_output_weight,
        gate_weight,
        pairwise_up_weight,
        pairwise_down_weight,
    )


def outer_kernel(lt_ref, r_ref, wt_ref, out_ref, x_ref):
    n_factor = r_ref.shape[0]
    tile_rows = out_ref.shape[0]
    scale = 1.0 / r_ref.shape[1]

    def fill(d, carry):
        vals = jnp.dot(lt_ref[...], r_ref[d], preferred_element_type=jnp.float32)
        vals = (vals * scale).astype(jnp.bfloat16)
        start = pl.multiple_of(d * n_factor, n_factor)
        for i in range(tile_rows):
            x_ref[i, pl.ds(start, n_factor), :] = vals[i * n_factor : (i + 1) * n_factor, :]
        return carry

    lax.fori_loop(0, n_factor, fill, 0)

    def emit(i, carry):
        upd = jnp.dot(wt_ref[...], x_ref[i], preferred_element_type=jnp.float32)
        out_ref[i] = upd.T
        return carry

    lax.fori_loop(0, tile_rows, emit, 0)


def outer_product(left_gathered, right_gathered, outer_output_weight):
    total_rows, tile_rows, channels = left_gathered.shape
    columns = right_gathered.shape[2]
    pair = outer_output_weight.shape[1]
    left_t = jnp.transpose(left_gathered, (1, 2, 0)).reshape(tile_rows * channels, total_rows)
    weight_t = jnp.transpose(
        outer_output_weight.reshape(channels, channels, pair), (1, 0, 2)
    ).reshape(channels * channels, pair).T
    flops = 4 * tile_rows * channels * channels * columns * (total_rows + pair) // 2
    return pl.pallas_call(
        outer_kernel,
        out_shape=jax.ShapeDtypeStruct((tile_rows, columns, pair), jnp.float32),
        in_specs=[pl.BlockSpec(memory_space=pltpu.VMEM)] * 3,
        out_specs=pl.BlockSpec(memory_space=pltpu.VMEM),
        scratch_shapes=[pltpu.VMEM((tile_rows, channels * channels, columns), jnp.bfloat16)],
        compiler_params=pltpu.CompilerParams(vmem_limit_bytes=56 * 1024 * 1024),
        cost_estimate=pl.CostEstimate(
            flops=flops, transcendentals=0, bytes_accessed=right_gathered.size * 2 + tile_rows * columns * pair * 4
        ),
    )(left_t, right_gathered, weight_t)


def on_device(
    homolog_features,
    pairwise_input,
    transition_expand_matrix,
    transition_contract_matrix,
    factor_pair_matrices,
    outer_output_weight,
    triangle_projection_weight,
    triangle_output_weight,
    pairwise_up_weight,
    pairwise_down_weight,
):
    refreshed_homolog_features, left_side, right_side = alignment_branch(
        homolog_features, transition_expand_matrix, transition_contract_matrix, factor_pair_matrices
    )
    left_gathered, right_gathered = gather_sides(left_side, right_side)
    pairwise_input, right_side = lax.optimization_barrier((pairwise_input, right_side))
    tri_left, tri_right = pair_front(
        pairwise_input, triangle_projection_weight
    )
    moved = send_whole(tri_left, tri_right)
    product = triangle_product(moved)
    product, left_gathered = lax.optimization_barrier((product, left_gathered))
    product_tile = send_back(product)
    outer_update = outer_product(left_gathered, right_gathered, outer_output_weight)
    product_tile, outer_update = lax.optimization_barrier((product_tile, outer_update))
    pairwise_output = pair_back(
        pairwise_input,
        product_tile,
        outer_update,
        triangle_projection_weight,
        triangle_output_weight,
        pairwise_up_weight,
        pairwise_down_weight,
    )
    return (refreshed_homolog_features, pairwise_output)


def solution(mesh):
    return jax.shard_map(
        on_device,
        mesh=mesh,
        in_specs=(
            P(("branch", "rows"), None, None),
            P("rows", "branch", None),
            P(),
            P(),
            P(),
            P(),
            P(),
            P(),
            P(),
            P(),
        ),
        out_specs=(P(("branch", "rows"), None, None), P("rows", "branch", None)),
        check_vma=False,
    )
```

```python
import jax
import jax.numpy as jnp
from jax import lax
from jax.experimental import pallas as pl
from jax.experimental.pallas import tpu as pltpu
from jax.sharding import PartitionSpec as P


def standardize_features(values, dimension):
    average = jnp.mean(values, axis=dimension, keepdims=True)
    centered = values - average
    variance = jnp.mean(centered * centered, axis=dimension, keepdims=True)
    return centered * lax.rsqrt(variance + 1e-05)


def alignment_branch(
    homolog_features, transition_expand_matrix, transition_contract_matrix, factor_pair_matrices
):
    local_rows, sequence_length, channel_width = homolog_features.shape
    homolog_real_matrix = homolog_features.astype(jnp.float32)
    standardized_homologs = (
        standardize_features(homolog_real_matrix, -1)
        .astype(jnp.bfloat16)
        .reshape(local_rows * sequence_length, channel_width)
    )
    expanded_activations = jax.nn.relu(
        jnp.dot(standardized_homologs, transition_expand_matrix, preferred_element_type=jnp.float32)
    ).astype(jnp.bfloat16)
    refreshed_homolog_features = (
        homolog_real_matrix
        + jnp.dot(
            expanded_activations, transition_contract_matrix, preferred_element_type=jnp.float32
        ).reshape(homolog_features.shape)
    ).astype(jnp.bfloat16)
    standardized_for_factors = (
        standardize_features(refreshed_homolog_features.astype(jnp.float32), -1)
        .astype(jnp.bfloat16)
        .reshape(local_rows * sequence_length, channel_width)
    )
    projected = jnp.dot(
        standardized_for_factors, factor_pair_matrices, preferred_element_type=jnp.float32
    ).reshape(local_rows, sequence_length, -1)
    channels = projected.shape[-1] // 2
    left_side = projected[..., :channels].astype(jnp.bfloat16)
    right_side = jnp.swapaxes(projected[..., channels:].astype(jnp.bfloat16), 1, 2)
    return (refreshed_homolog_features, left_side, right_side)


def branch_pair(mine, theirs):
    first = lax.axis_index("branch") == 0
    return jnp.where(first, jnp.concatenate([mine, theirs]), jnp.concatenate([theirs, mine]))


def gather_sides(left_side, right_side):
    swap = [(0, 1), (1, 0)]
    left_pair = branch_pair(left_side, lax.ppermute(left_side, "branch", swap))
    left_gathered = lax.all_to_all(left_pair, "rows", split_axis=1, concat_axis=0, tiled=True)
    half = right_side.shape[2] // 2
    me = lax.axis_index("branch")
    keep = lax.dynamic_slice_in_dim(right_side, me * half, half, axis=2)
    send = lax.dynamic_slice_in_dim(right_side, (1 - me) * half, half, axis=2)
    right_pair = branch_pair(keep, lax.ppermute(send, "branch", swap))
    right_flat = right_pair.reshape(right_pair.shape[0], -1)
    right_gathered = lax.all_gather(right_flat, "rows", axis=0, tiled=True)
    return left_gathered, right_gathered


def send_whole(tri_left, tri_right):
    both = ("branch", "rows")
    moved = lax.all_to_all(
        jnp.stack([tri_left, tri_right], axis=1), both, split_axis=0, concat_axis=0, tiled=True
    )
    return moved


def send_back(product):
    return lax.all_to_all(product, ("branch", "rows"), split_axis=0, concat_axis=0, tiled=True)


def front_kernel(pair_ref, wt_ref, left_ref, right_ref):
    rows, columns, chans = pair_ref.shape
    for r in range(rows):
        pair_norm = standardize_features(pair_ref[r].astype(jnp.float32), -1).astype(jnp.bfloat16)
        proj = lax.dot_general(
            wt_ref[...], pair_norm, (((1,), (1,)), ((), ())), preferred_element_type=jnp.float32
        )
        cols = slice(r * columns, (r + 1) * columns)
        left_ref[:, cols] = (
            jax.nn.sigmoid(proj[chans : 2 * chans]) * proj[:chans]
        ).astype(left_ref.dtype)
        right_ref[:, cols] = (
            jax.nn.sigmoid(proj[3 * chans :]) * proj[2 * chans : 3 * chans]
        ).astype(right_ref.dtype)


def pair_front(pairwise_input, triangle_projection_weight):
    tile_rows, columns, chans = pairwise_input.shape
    step_rows = 4
    weight_t = triangle_projection_weight[:, : 4 * chans].T
    side = jax.ShapeDtypeStruct((chans, tile_rows * columns), jnp.bfloat16)
    out_block = pl.BlockSpec((chans, step_rows * columns), lambda g: (0, g))
    tri_left, tri_right = pl.pallas_call(
        front_kernel,
        out_shape=(side, side),
        grid=(tile_rows // step_rows,),
        in_specs=[
            pl.BlockSpec((step_rows, columns, chans), lambda g: (g, 0, 0)),
            pl.BlockSpec((4 * chans, chans), lambda g: (0, 0)),
        ],
        out_specs=(out_block, out_block),
        cost_estimate=pl.CostEstimate(
            flops=2 * tile_rows * columns * chans * 4 * chans,
            transcendentals=2 * tile_rows * columns * chans,
            bytes_accessed=tile_rows * columns * chans * 6,
        ),
    )(pairwise_input, weight_t)
    return (
        tri_left.reshape(chans, tile_rows, columns),
        tri_right.reshape(chans, tile_rows, columns),
    )


def product_kernel(moved_ref, out_ref):
    halves, span, columns = out_ref.shape
    n_src, _, tile_rows, _ = moved_ref.shape
    per_half = n_src // halves
    per_out = per_half // halves
    for h in range(halves):
        total = None
        for b in range(halves):
            left = moved_ref[b * per_half : (b + 1) * per_half, 0]
            first = b * per_half + h * per_out
            right = moved_ref[first : first + per_out, 1]
            part = lax.dot_general(
                left.reshape(per_half * tile_rows, columns),
                right.reshape(per_out * tile_rows, columns),
                (((1,), (1,)), ((), ())),
                preferred_element_type=jnp.float32,
            )
            total = part if total is None else total + part
        out_ref[h] = total.astype(out_ref.dtype)


def triangle_product(moved):
    n_src, _, tile_rows, columns = moved.shape
    halves = lax.axis_size("branch")
    product = pl.pallas_call(
        product_kernel,
        out_shape=jax.ShapeDtypeStruct((halves, n_src * tile_rows // halves, columns), jnp.bfloat16),
        in_specs=[pl.BlockSpec(memory_space=pltpu.VMEM)],
        out_specs=pl.BlockSpec(memory_space=pltpu.VMEM),
        cost_estimate=pl.CostEstimate(
            flops=2 * (n_src * tile_rows) ** 2 * columns // halves,
            transcendentals=0,
            bytes_accessed=moved.size * 2 + n_src * tile_rows * columns * 2,
        ),
    )(moved)
    return product.reshape(-1, tile_rows, columns)


def back_kernel(prod_ref, pair_ref, outer_ref, wo_ref, wg_ref, wu_ref, wd_ref, out_ref):
    rows, columns, chans = pair_ref.shape
    for r in range(rows):
        prod = prod_ref[:, r * columns : (r + 1) * columns].astype(jnp.float32)
        prod_norm = standardize_features(prod, 0).T.astype(jnp.bfloat16)
        tri_update = jnp.dot(prod_norm, wo_ref[...], preferred_element_type=jnp.float32)
        pair_float = pair_ref[r].astype(jnp.float32)
        pair_norm = standardize_features(pair_float, -1).astype(jnp.bfloat16)
        gate = jax.nn.sigmoid(
            jnp.dot(pair_norm, wg_ref[...], preferred_element_type=jnp.float32)
        )
        pair_mid = pair_float + gate * tri_update
        mid_norm = standardize_features(pair_mid, -1).astype(jnp.bfloat16)
        hidden = jnp.maximum(
            jnp.dot(mid_norm, wu_ref[...], preferred_element_type=jnp.float32), 0.0
        ).astype(jnp.bfloat16)
        down = jnp.dot(hidden, wd_ref[...], preferred_element_type=jnp.float32)
        out_ref[r] = (pair_mid + down + outer_ref[r]).astype(out_ref.dtype)


def pair_back(
    pairwise_input,
    product_tile,
    outer_update,
    triangle_projection_weight,
    triangle_output_weight,
    pairwise_up_weight,
    pairwise_down_weight,
):
    tile_rows, columns, chans = pairwise_input.shape
    step_rows = 4
    prod_flat = product_tile.reshape(chans, tile_rows * columns)
    gate_weight = triangle_projection_weight[:, 4 * chans :]
    hidden = pairwise_up_weight.shape[1]
    row_block = lambda g: (g, 0, 0)
    fixed = lambda g: (0, 0)
    return pl.pallas_call(
        back_kernel,
        out_shape=jax.ShapeDtypeStruct((tile_rows, columns, chans), jnp.bfloat16),
        grid=(tile_rows // step_rows,),
        in_specs=[
            pl.BlockSpec((chans, step_rows * columns), lambda g: (0, g)),
            pl.BlockSpec((step_rows, columns, chans), row_block),
            pl.BlockSpec((step_rows, columns, chans), row_block),
            pl.BlockSpec((chans, chans), fixed),
            pl.BlockSpec((chans, chans), fixed),
            pl.BlockSpec((chans, hidden), fixed),
            pl.BlockSpec((hidden, chans), fixed),
        ],
        out_specs=pl.BlockSpec((step_rows, columns, chans), row_block),
        cost_estimate=pl.CostEstimate(
            flops=2 * tile_rows * columns * chans * (3 * chans + 2 * hidden) // 1,
            transcendentals=tile_rows * columns * chans,
            bytes_accessed=tile_rows * columns * chans * 10,
        ),
    )(
        prod_flat,
        pairwise_input,
        outer_update,
        triangle_output_weight,
        gate_weight,
        pairwise_up_weight,
        pairwise_down_weight,
    )


def outer_kernel(lt_ref, r_ref, wt_ref, out_ref, x_ref):
    tile_rows, columns, _ = out_ref.shape
    n_factor = r_ref.shape[1] // columns
    scale = 1.0 / r_ref.shape[0]

    def fill(d, carry):
        lanes = pl.ds(pl.multiple_of(d * columns, columns), columns)
        vals = jnp.dot(lt_ref[...], r_ref[:, lanes], preferred_element_type=jnp.float32)
        vals = (vals * scale).astype(jnp.bfloat16)
        start = pl.multiple_of(d * n_factor, n_factor)
        for i in range(tile_rows):
            x_ref[i, pl.ds(start, n_factor), :] = vals[i * n_factor : (i + 1) * n_factor, :]
        return carry

    lax.fori_loop(0, n_factor, fill, 0)

    def emit(i, carry):
        upd = jnp.dot(wt_ref[...], x_ref[i], preferred_element_type=jnp.float32)
        out_ref[i] = upd.T
        return carry

    lax.fori_loop(0, tile_rows, emit, 0)


def outer_product(left_gathered, right_gathered, outer_output_weight):
    total_rows, tile_rows, channels = left_gathered.shape
    columns = right_gathered.shape[1] // channels
    pair = outer_output_weight.shape[1]
    left_t = jnp.transpose(left_gathered, (1, 2, 0)).reshape(tile_rows * channels, total_rows)
    weight_t = jnp.transpose(
        outer_output_weight.reshape(channels, channels, pair), (1, 0, 2)
    ).reshape(channels * channels, pair).T
    flops = 4 * tile_rows * channels * channels * columns * (total_rows + pair) // 2
    return pl.pallas_call(
        outer_kernel,
        out_shape=jax.ShapeDtypeStruct((tile_rows, columns, pair), jnp.float32),
        in_specs=[pl.BlockSpec(memory_space=pltpu.VMEM)] * 3,
        out_specs=pl.BlockSpec(memory_space=pltpu.VMEM),
        scratch_shapes=[pltpu.VMEM((tile_rows, channels * channels, columns), jnp.bfloat16)],
        compiler_params=pltpu.CompilerParams(vmem_limit_bytes=56 * 1024 * 1024),
        cost_estimate=pl.CostEstimate(
            flops=flops, transcendentals=0, bytes_accessed=right_gathered.size * 2 + tile_rows * columns * pair * 4
        ),
    )(left_t, right_gathered, weight_t)


def on_device(
    homolog_features,
    pairwise_input,
    transition_expand_matrix,
    transition_contract_matrix,
    factor_pair_matrices,
    outer_output_weight,
    triangle_projection_weight,
    triangle_output_weight,
    pairwise_up_weight,
    pairwise_down_weight,
):
    refreshed_homolog_features, left_side, right_side = alignment_branch(
        homolog_features, transition_expand_matrix, transition_contract_matrix, factor_pair_matrices
    )
    left_gathered, right_gathered = gather_sides(left_side, right_side)
    pairwise_input, right_side = lax.optimization_barrier((pairwise_input, right_side))
    tri_left, tri_right = pair_front(
        pairwise_input, triangle_projection_weight
    )
    moved = send_whole(tri_left, tri_right)
    product = triangle_product(moved)
    product, left_gathered = lax.optimization_barrier((product, left_gathered))
    product_tile = send_back(product)
    outer_update = outer_product(left_gathered, right_gathered, outer_output_weight)
    product_tile, outer_update = lax.optimization_barrier((product_tile, outer_update))
    pairwise_output = pair_back(
        pairwise_input,
        product_tile,
        outer_update,
        triangle_projection_weight,
        triangle_output_weight,
        pairwise_up_weight,
        pairwise_down_weight,
    )
    return (refreshed_homolog_features, pairwise_output)


def solution(mesh):
    return jax.shard_map(
        on_device,
        mesh=mesh,
        in_specs=(
            P(("branch", "rows"), None, None),
            P("rows", "branch", None),
            P(),
            P(),
            P(),
            P(),
            P(),
            P(),
            P(),
            P(),
        ),
        out_specs=(P(("branch", "rows"), None, None), P("rows", "branch", None)),
        check_vma=False,
    )
```

```python
import jax
import jax.numpy as jnp
from jax import lax
from jax.experimental import pallas as pl
from jax.experimental.pallas import tpu as pltpu
from jax.sharding import PartitionSpec as P


def standardize_features(values, dimension):
    average = jnp.mean(values, axis=dimension, keepdims=True)
    centered = values - average
    variance = jnp.mean(centered * centered, axis=dimension, keepdims=True)
    return centered * lax.rsqrt(variance + 1e-05)


def alignment_branch(
    homolog_features, transition_expand_matrix, transition_contract_matrix, factor_pair_matrices
):
    local_rows, sequence_length, channel_width = homolog_features.shape
    homolog_real_matrix = homolog_features.astype(jnp.float32)
    standardized_homologs = (
        standardize_features(homolog_real_matrix, -1)
        .astype(jnp.bfloat16)
        .reshape(local_rows * sequence_length, channel_width)
    )
    expanded_activations = jax.nn.relu(
        jnp.dot(standardized_homologs, transition_expand_matrix, preferred_element_type=jnp.float32)
    ).astype(jnp.bfloat16)
    refreshed_homolog_features = (
        homolog_real_matrix
        + jnp.dot(
            expanded_activations, transition_contract_matrix, preferred_element_type=jnp.float32
        ).reshape(homolog_features.shape)
    ).astype(jnp.bfloat16)
    standardized_for_factors = (
        standardize_features(refreshed_homolog_features.astype(jnp.float32), -1)
        .astype(jnp.bfloat16)
        .reshape(local_rows * sequence_length, channel_width)
    )
    projected = jnp.dot(
        standardized_for_factors, factor_pair_matrices, preferred_element_type=jnp.float32
    ).reshape(local_rows, sequence_length, -1)
    channels = projected.shape[-1] // 2
    left_side = projected[..., :channels].astype(jnp.bfloat16)
    right_side = jnp.swapaxes(projected[..., channels:].astype(jnp.bfloat16), 1, 2)
    return (refreshed_homolog_features, left_side, right_side)


def branch_pair(mine, theirs):
    first = lax.axis_index("branch") == 0
    return jnp.where(first, jnp.concatenate([mine, theirs]), jnp.concatenate([theirs, mine]))


def gather_sides(left_side, right_side):
    swap = [(0, 1), (1, 0)]
    left_pair = branch_pair(left_side, lax.ppermute(left_side, "branch", swap))
    left_gathered = lax.all_to_all(left_pair, "rows", split_axis=1, concat_axis=0, tiled=True)
    half = right_side.shape[2] // 2
    me = lax.axis_index("branch")
    keep = lax.dynamic_slice_in_dim(right_side, me * half, half, axis=2)
    send = lax.dynamic_slice_in_dim(right_side, (1 - me) * half, half, axis=2)
    right_pair = branch_pair(keep, lax.ppermute(send, "branch", swap))
    right_gathered = lax.all_gather(jnp.swapaxes(right_pair, 0, 1), "rows", axis=1, tiled=True)
    return left_gathered, right_gathered


def send_whole(tri_stack):
    both = ("branch", "rows")
    moved = lax.all_to_all(tri_stack, both, split_axis=0, concat_axis=0, tiled=True)
    return moved


def send_back(product):
    return lax.all_to_all(product, ("branch", "rows"), split_axis=0, concat_axis=0, tiled=True)


def front_kernel(pair_ref, w_ref, out_ref, norm_ref):
    tile_rows, columns, chans = pair_ref.shape
    block = out_ref.shape[0]

    @pl.when(pl.program_id(0) == 0)
    def _():
        for r in range(tile_rows):
            norm_ref[r] = standardize_features(pair_ref[r].astype(jnp.float32), -1).astype(
                norm_ref.dtype
            )

    weight = w_ref[...].reshape(4 * block, chans)
    for r in range(tile_rows):
        proj = lax.dot_general(
            weight, norm_ref[r], (((1,), (1,)), ((), ())), preferred_element_type=jnp.float32
        )
        out_ref[:, 0, r, :] = (
            jax.nn.sigmoid(proj[block : 2 * block]) * proj[:block]
        ).astype(out_ref.dtype)
        out_ref[:, 1, r, :] = (
            jax.nn.sigmoid(proj[3 * block :]) * proj[2 * block : 3 * block]
        ).astype(out_ref.dtype)


def pair_front(pairwise_input, triangle_projection_weight):
    tile_rows, columns, chans = pairwise_input.shape
    block = 32
    weight = triangle_projection_weight[:, : 4 * chans].T.reshape(4, chans, chans)
    return pl.pallas_call(
        front_kernel,
        out_shape=jax.ShapeDtypeStruct((chans, 2, tile_rows, columns), jnp.bfloat16),
        grid=(chans // block,),
        in_specs=[
            pl.BlockSpec((tile_rows, columns, chans), lambda g: (0, 0, 0)),
            pl.BlockSpec((4, block, chans), lambda g: (0, g, 0)),
        ],
        out_specs=pl.BlockSpec((block, 2, tile_rows, columns), lambda g: (g, 0, 0, 0)),
        scratch_shapes=[pltpu.VMEM((tile_rows, columns, chans), jnp.bfloat16)],
        cost_estimate=pl.CostEstimate(
            flops=2 * tile_rows * columns * chans * 4 * chans,
            transcendentals=2 * tile_rows * columns * chans,
            bytes_accessed=tile_rows * columns * chans * 6,
        ),
    )(pairwise_input, weight)


def product_kernel(moved_ref, out_ref):
    halves, span, columns = out_ref.shape
    n_src, _, tile_rows, _ = moved_ref.shape
    per_half = n_src // halves
    per_out = per_half // halves
    for h in range(halves):
        total = None
        for b in range(halves):
            left = moved_ref[b * per_half : (b + 1) * per_half, 0]
            first = b * per_half + h * per_out
            right = moved_ref[first : first + per_out, 1]
            part = lax.dot_general(
                left.reshape(per_half * tile_rows, columns),
                right.reshape(per_out * tile_rows, columns),
                (((1,), (1,)), ((), ())),
                preferred_element_type=jnp.float32,
            )
            total = part if total is None else total + part
        out_ref[h] = total.astype(out_ref.dtype)


def triangle_product(moved):
    n_src, _, tile_rows, columns = moved.shape
    halves = lax.axis_size("branch")
    product = pl.pallas_call(
        product_kernel,
        out_shape=jax.ShapeDtypeStruct((halves, n_src * tile_rows // halves, columns), jnp.bfloat16),
        in_specs=[pl.BlockSpec(memory_space=pltpu.VMEM)],
        out_specs=pl.BlockSpec(memory_space=pltpu.VMEM),
        cost_estimate=pl.CostEstimate(
            flops=2 * (n_src * tile_rows) ** 2 * columns // halves,
            transcendentals=0,
            bytes_accessed=moved.size * 2 + n_src * tile_rows * columns * 2,
        ),
    )(moved)
    return product.reshape(-1, tile_rows, columns)


def back_kernel(prod_ref, pair_ref, outer_ref, wo_ref, wg_ref, wu_ref, wd_ref, out_ref):
    rows, columns, chans = pair_ref.shape
    for r in range(rows):
        prod = prod_ref[:, r * columns : (r + 1) * columns].astype(jnp.float32)
        prod_norm = standardize_features(prod, 0).T.astype(jnp.bfloat16)
        tri_update = jnp.dot(prod_norm, wo_ref[...], preferred_element_type=jnp.float32)
        pair_float = pair_ref[r].astype(jnp.float32)
        pair_norm = standardize_features(pair_float, -1).astype(jnp.bfloat16)
        gate = jax.nn.sigmoid(
            jnp.dot(pair_norm, wg_ref[...], preferred_element_type=jnp.float32)
        )
        pair_mid = pair_float + gate * tri_update
        mid_norm = standardize_features(pair_mid, -1).astype(jnp.bfloat16)
        hidden = jnp.maximum(
            jnp.dot(mid_norm, wu_ref[...], preferred_element_type=jnp.float32), 0.0
        ).astype(jnp.bfloat16)
        down = jnp.dot(hidden, wd_ref[...], preferred_element_type=jnp.float32)
        out_ref[r] = (pair_mid + down + outer_ref[r]).astype(out_ref.dtype)


def pair_back(
    pairwise_input,
    product_tile,
    outer_update,
    triangle_projection_weight,
    triangle_output_weight,
    pairwise_up_weight,
    pairwise_down_weight,
):
    tile_rows, columns, chans = pairwise_input.shape
    step_rows = 4
    prod_flat = product_tile.reshape(chans, tile_rows * columns)
    gate_weight = triangle_projection_weight[:, 4 * chans :]
    hidden = pairwise_up_weight.shape[1]
    row_block = lambda g: (g, 0, 0)
    fixed = lambda g: (0, 0)
    return pl.pallas_call(
        back_kernel,
        out_shape=jax.ShapeDtypeStruct((tile_rows, columns, chans), jnp.bfloat16),
        grid=(tile_rows // step_rows,),
        in_specs=[
            pl.BlockSpec((chans, step_rows * columns), lambda g: (0, g)),
            pl.BlockSpec((step_rows, columns, chans), row_block),
            pl.BlockSpec((step_rows, columns, chans), row_block),
            pl.BlockSpec((chans, chans), fixed),
            pl.BlockSpec((chans, chans), fixed),
            pl.BlockSpec((chans, hidden), fixed),
            pl.BlockSpec((hidden, chans), fixed),
        ],
        out_specs=pl.BlockSpec((step_rows, columns, chans), row_block),
        cost_estimate=pl.CostEstimate(
            flops=2 * tile_rows * columns * chans * (3 * chans + 2 * hidden) // 1,
            transcendentals=tile_rows * columns * chans,
            bytes_accessed=tile_rows * columns * chans * 10,
        ),
    )(
        prod_flat,
        pairwise_input,
        outer_update,
        triangle_output_weight,
        gate_weight,
        pairwise_up_weight,
        pairwise_down_weight,
    )


def outer_kernel(lt_ref, r_ref, wt_ref, out_ref, x_ref):
    n_factor = r_ref.shape[0]
    tile_rows = out_ref.shape[0]
    scale = 1.0 / r_ref.shape[1]

    def fill(d, carry):
        vals = jnp.dot(lt_ref[...], r_ref[d], preferred_element_type=jnp.float32)
        vals = (vals * scale).astype(jnp.bfloat16)
        start = pl.multiple_of(d * n_factor, n_factor)
        for i in range(tile_rows):
            x_ref[i, pl.ds(start, n_factor), :] = vals[i * n_factor : (i + 1) * n_factor, :]
        return carry

    lax.fori_loop(0, n_factor, fill, 0)

    def emit(i, carry):
        upd = jnp.dot(wt_ref[...], x_ref[i], preferred_element_type=jnp.float32)
        out_ref[i] = upd.T
        return carry

    lax.fori_loop(0, tile_rows, emit, 0)


def outer_product(left_gathered, right_gathered, outer_output_weight):
    total_rows, tile_rows, channels = left_gathered.shape
    columns = right_gathered.shape[2]
    pair = outer_output_weight.shape[1]
    left_t = jnp.transpose(left_gathered, (1, 2, 0)).reshape(tile_rows * channels, total_rows)
    weight_t = jnp.transpose(
        outer_output_weight.reshape(channels, channels, pair), (1, 0, 2)
    ).reshape(channels * channels, pair).T
    flops = 4 * tile_rows * channels * channels * columns * (total_rows + pair) // 2
    return pl.pallas_call(
        outer_kernel,
        out_shape=jax.ShapeDtypeStruct((tile_rows, columns, pair), jnp.float32),
        in_specs=[pl.BlockSpec(memory_space=pltpu.VMEM)] * 3,
        out_specs=pl.BlockSpec(memory_space=pltpu.VMEM),
        scratch_shapes=[pltpu.VMEM((tile_rows, channels * channels, columns), jnp.bfloat16)],
        compiler_params=pltpu.CompilerParams(vmem_limit_bytes=56 * 1024 * 1024),
        cost_estimate=pl.CostEstimate(
            flops=flops, transcendentals=0, bytes_accessed=right_gathered.size * 2 + tile_rows * columns * pair * 4
        ),
    )(left_t, right_gathered, weight_t)


def on_device(
    homolog_features,
    pairwise_input,
    transition_expand_matrix,
    transition_contract_matrix,
    factor_pair_matrices,
    outer_output_weight,
    triangle_projection_weight,
    triangle_output_weight,
    pairwise_up_weight,
    pairwise_down_weight,
):
    refreshed_homolog_features, left_side, right_side = alignment_branch(
        homolog_features, transition_expand_matrix, transition_contract_matrix, factor_pair_matrices
    )
    left_gathered, right_gathered = gather_sides(left_side, right_side)
    pairwise_input, right_side = lax.optimization_barrier((pairwise_input, right_side))
    tri_stack = pair_front(pairwise_input, triangle_projection_weight)
    moved = send_whole(tri_stack)
    product = triangle_product(moved)
    product, left_gathered = lax.optimization_barrier((product, left_gathered))
    product_tile = send_back(product)
    outer_update = outer_product(left_gathered, right_gathered, outer_output_weight)
    product_tile, outer_update = lax.optimization_barrier((product_tile, outer_update))
    pairwise_output = pair_back(
        pairwise_input,
        product_tile,
        outer_update,
        triangle_projection_weight,
        triangle_output_weight,
        pairwise_up_weight,
        pairwise_down_weight,
    )
    return (refreshed_homolog_features, pairwise_output)


def solution(mesh):
    return jax.shard_map(
        on_device,
        mesh=mesh,
        in_specs=(
            P(("branch", "rows"), None, None),
            P("rows", "branch", None),
            P(),
            P(),
            P(),
            P(),
            P(),
            P(),
            P(),
            P(),
        ),
        out_specs=(P(("branch", "rows"), None, None), P("rows", "branch", None)),
        check_vma=False,
    )
```

```python
import jax
import jax.numpy as jnp
from jax import lax
from jax.experimental import pallas as pl
from jax.experimental.pallas import tpu as pltpu
from jax.sharding import PartitionSpec as P


def standardize_features(values, dimension):
    average = jnp.mean(values, axis=dimension, keepdims=True)
    centered = values - average
    variance = jnp.mean(centered * centered, axis=dimension, keepdims=True)
    return centered * lax.rsqrt(variance + 1e-05)


def alignment_branch(
    homolog_features, transition_expand_matrix, transition_contract_matrix, factor_pair_matrices
):
    local_rows, sequence_length, channel_width = homolog_features.shape
    homolog_real_matrix = homolog_features.astype(jnp.float32)
    standardized_homologs = (
        standardize_features(homolog_real_matrix, -1)
        .astype(jnp.bfloat16)
        .reshape(local_rows * sequence_length, channel_width)
    )
    expanded_activations = jax.nn.relu(
        jnp.dot(standardized_homologs, transition_expand_matrix, preferred_element_type=jnp.float32)
    ).astype(jnp.bfloat16)
    refreshed_homolog_features = (
        homolog_real_matrix
        + jnp.dot(
            expanded_activations, transition_contract_matrix, preferred_element_type=jnp.float32
        ).reshape(homolog_features.shape)
    ).astype(jnp.bfloat16)
    standardized_for_factors = (
        standardize_features(refreshed_homolog_features.astype(jnp.float32), -1)
        .astype(jnp.bfloat16)
        .reshape(local_rows * sequence_length, channel_width)
    )
    projected = jnp.dot(
        standardized_for_factors, factor_pair_matrices, preferred_element_type=jnp.float32
    ).reshape(local_rows, sequence_length, -1)
    channels = projected.shape[-1] // 2
    left_side = projected[..., :channels].astype(jnp.bfloat16)
    right_side = jnp.swapaxes(projected[..., channels:].astype(jnp.bfloat16), 1, 2)
    return (refreshed_homolog_features, left_side, right_side)


def branch_pair(mine, theirs):
    first = lax.axis_index("branch") == 0
    return jnp.where(first, jnp.concatenate([mine, theirs]), jnp.concatenate([theirs, mine]))


def gather_sides(left_side, right_side):
    swap = [(0, 1), (1, 0)]
    left_pair = branch_pair(left_side, lax.ppermute(left_side, "branch", swap))
    left_gathered = lax.all_to_all(left_pair, "rows", split_axis=1, concat_axis=0, tiled=True)
    half = right_side.shape[2] // 2
    me = lax.axis_index("branch")
    keep = lax.dynamic_slice_in_dim(right_side, me * half, half, axis=2)
    send = lax.dynamic_slice_in_dim(right_side, (1 - me) * half, half, axis=2)
    right_pair = branch_pair(keep, lax.ppermute(send, "branch", swap))
    right_gathered = lax.all_gather(jnp.swapaxes(right_pair, 0, 1), "rows", axis=1, tiled=True)
    return left_gathered, right_gathered


def send_whole(tri_stack):
    both = ("branch", "rows")
    moved = lax.all_to_all(tri_stack, both, split_axis=0, concat_axis=0, tiled=True)
    return moved


def send_back(product):
    return lax.all_to_all(product, ("branch", "rows"), split_axis=0, concat_axis=0, tiled=True)


def logistic(values):
    return 0.5 * jnp.tanh(0.5 * values) + 0.5


def front_kernel(pair_ref, w_ref, out_ref, norm_ref):
    tile_rows, columns, chans = pair_ref.shape
    block = out_ref.shape[0]

    @pl.when(pl.program_id(0) == 0)
    def _():
        for r in range(tile_rows):
            norm_ref[r] = standardize_features(pair_ref[r].astype(jnp.float32), -1).astype(
                norm_ref.dtype
            )

    weight = w_ref[...].reshape(4 * block, chans)
    for r in range(tile_rows):
        proj = lax.dot_general(
            weight, norm_ref[r], (((1,), (1,)), ((), ())), preferred_element_type=jnp.float32
        )
        out_ref[:, 0, r, :] = (
            logistic(proj[block : 2 * block]) * proj[:block]
        ).astype(out_ref.dtype)
        out_ref[:, 1, r, :] = (
            logistic(proj[3 * block :]) * proj[2 * block : 3 * block]
        ).astype(out_ref.dtype)


def pair_front(pairwise_input, triangle_projection_weight):
    tile_rows, columns, chans = pairwise_input.shape
    block = 32
    weight = triangle_projection_weight[:, : 4 * chans].T.reshape(4, chans, chans)
    return pl.pallas_call(
        front_kernel,
        out_shape=jax.ShapeDtypeStruct((chans, 2, tile_rows, columns), jnp.bfloat16),
        grid=(chans // block,),
        in_specs=[
            pl.BlockSpec((tile_rows, columns, chans), lambda g: (0, 0, 0)),
            pl.BlockSpec((4, block, chans), lambda g: (0, g, 0)),
        ],
        out_specs=pl.BlockSpec((block, 2, tile_rows, columns), lambda g: (g, 0, 0, 0)),
        scratch_shapes=[pltpu.VMEM((tile_rows, columns, chans), jnp.bfloat16)],
        cost_estimate=pl.CostEstimate(
            flops=2 * tile_rows * columns * chans * 4 * chans,
            transcendentals=2 * tile_rows * columns * chans,
            bytes_accessed=tile_rows * columns * chans * 6,
        ),
    )(pairwise_input, weight)


def product_kernel(moved_ref, out_ref):
    halves, span, columns = out_ref.shape
    n_src, _, tile_rows, _ = moved_ref.shape
    per_half = n_src // halves
    per_out = per_half // halves
    for h in range(halves):
        total = None
        for b in range(halves):
            left = moved_ref[b * per_half : (b + 1) * per_half, 0]
            first = b * per_half + h * per_out
            right = moved_ref[first : first + per_out, 1]
            part = lax.dot_general(
                left.reshape(per_half * tile_rows, columns),
                right.reshape(per_out * tile_rows, columns),
                (((1,), (1,)), ((), ())),
                preferred_element_type=jnp.float32,
            )
            total = part if total is None else total + part
        out_ref[h] = total.astype(out_ref.dtype)


def triangle_product(moved):
    n_src, _, tile_rows, columns = moved.shape
    halves = lax.axis_size("branch")
    product = pl.pallas_call(
        product_kernel,
        out_shape=jax.ShapeDtypeStruct((halves, n_src * tile_rows // halves, columns), jnp.bfloat16),
        in_specs=[pl.BlockSpec(memory_space=pltpu.VMEM)],
        out_specs=pl.BlockSpec(memory_space=pltpu.VMEM),
        cost_estimate=pl.CostEstimate(
            flops=2 * (n_src * tile_rows) ** 2 * columns // halves,
            transcendentals=0,
            bytes_accessed=moved.size * 2 + n_src * tile_rows * columns * 2,
        ),
    )(moved)
    return product.reshape(-1, tile_rows, columns)


def back_kernel(prod_ref, pair_ref, outer_ref, wo_ref, wg_ref, wu_ref, wd_ref, out_ref):
    rows, columns, chans = pair_ref.shape
    for r in range(rows):
        prod = prod_ref[:, r * columns : (r + 1) * columns].astype(jnp.float32)
        prod_norm = standardize_features(prod, 0).T.astype(jnp.bfloat16)
        tri_update = jnp.dot(prod_norm, wo_ref[...], preferred_element_type=jnp.float32)
        pair_float = pair_ref[r].astype(jnp.float32)
        pair_norm = standardize_features(pair_float, -1).astype(jnp.bfloat16)
        gate = logistic(
            jnp.dot(pair_norm, wg_ref[...], preferred_element_type=jnp.float32)
        )
        pair_mid = pair_float + gate * tri_update
        mid_norm = standardize_features(pair_mid, -1).astype(jnp.bfloat16)
        hidden = jnp.maximum(
            jnp.dot(mid_norm, wu_ref[...], preferred_element_type=jnp.float32), 0.0
        ).astype(jnp.bfloat16)
        down = jnp.dot(hidden, wd_ref[...], preferred_element_type=jnp.float32)
        out_ref[r] = (pair_mid + down + outer_ref[r]).astype(out_ref.dtype)


def pair_back(
    pairwise_input,
    product_tile,
    outer_update,
    triangle_projection_weight,
    triangle_output_weight,
    pairwise_up_weight,
    pairwise_down_weight,
):
    tile_rows, columns, chans = pairwise_input.shape
    step_rows = 4
    prod_flat = product_tile.reshape(chans, tile_rows * columns)
    gate_weight = triangle_projection_weight[:, 4 * chans :]
    hidden = pairwise_up_weight.shape[1]
    row_block = lambda g: (g, 0, 0)
    fixed = lambda g: (0, 0)
    return pl.pallas_call(
        back_kernel,
        out_shape=jax.ShapeDtypeStruct((tile_rows, columns, chans), jnp.bfloat16),
        grid=(tile_rows // step_rows,),
        in_specs=[
            pl.BlockSpec((chans, step_rows * columns), lambda g: (0, g)),
            pl.BlockSpec((step_rows, columns, chans), row_block),
            pl.BlockSpec((step_rows, columns, chans), row_block),
            pl.BlockSpec((chans, chans), fixed),
            pl.BlockSpec((chans, chans), fixed),
            pl.BlockSpec((chans, hidden), fixed),
            pl.BlockSpec((hidden, chans), fixed),
        ],
        out_specs=pl.BlockSpec((step_rows, columns, chans), row_block),
        cost_estimate=pl.CostEstimate(
            flops=2 * tile_rows * columns * chans * (3 * chans + 2 * hidden) // 1,
            transcendentals=tile_rows * columns * chans,
            bytes_accessed=tile_rows * columns * chans * 10,
        ),
    )(
        prod_flat,
        pairwise_input,
        outer_update,
        triangle_output_weight,
        gate_weight,
        pairwise_up_weight,
        pairwise_down_weight,
    )


def outer_kernel(lt_ref, r_ref, wt_ref, out_ref, x_ref):
    n_factor = r_ref.shape[0]
    tile_rows = out_ref.shape[0]
    scale = 1.0 / r_ref.shape[1]

    def fill(d, carry):
        vals = jnp.dot(lt_ref[...], r_ref[d], preferred_element_type=jnp.float32)
        vals = (vals * scale).astype(jnp.bfloat16)
        start = pl.multiple_of(d * n_factor, n_factor)
        for i in range(tile_rows):
            x_ref[i, pl.ds(start, n_factor), :] = vals[i * n_factor : (i + 1) * n_factor, :]
        return carry

    lax.fori_loop(0, n_factor, fill, 0)

    def emit(i, carry):
        upd = jnp.dot(wt_ref[...], x_ref[i], preferred_element_type=jnp.float32)
        out_ref[i] = upd.T
        return carry

    lax.fori_loop(0, tile_rows, emit, 0)


def outer_product(left_gathered, right_gathered, outer_output_weight):
    total_rows, tile_rows, channels = left_gathered.shape
    columns = right_gathered.shape[2]
    pair = outer_output_weight.shape[1]
    left_t = jnp.transpose(left_gathered, (1, 2, 0)).reshape(tile_rows * channels, total_rows)
    weight_t = jnp.transpose(
        outer_output_weight.reshape(channels, channels, pair), (1, 0, 2)
    ).reshape(channels * channels, pair).T
    flops = 4 * tile_rows * channels * channels * columns * (total_rows + pair) // 2
    return pl.pallas_call(
        outer_kernel,
        out_shape=jax.ShapeDtypeStruct((tile_rows, columns, pair), jnp.float32),
        in_specs=[pl.BlockSpec(memory_space=pltpu.VMEM)] * 3,
        out_specs=pl.BlockSpec(memory_space=pltpu.VMEM),
        scratch_shapes=[pltpu.VMEM((tile_rows, channels * channels, columns), jnp.bfloat16)],
        compiler_params=pltpu.CompilerParams(vmem_limit_bytes=56 * 1024 * 1024),
        cost_estimate=pl.CostEstimate(
            flops=flops, transcendentals=0, bytes_accessed=right_gathered.size * 2 + tile_rows * columns * pair * 4
        ),
    )(left_t, right_gathered, weight_t)


def on_device(
    homolog_features,
    pairwise_input,
    transition_expand_matrix,
    transition_contract_matrix,
    factor_pair_matrices,
    outer_output_weight,
    triangle_projection_weight,
    triangle_output_weight,
    pairwise_up_weight,
    pairwise_down_weight,
):
    refreshed_homolog_features, left_side, right_side = alignment_branch(
        homolog_features, transition_expand_matrix, transition_contract_matrix, factor_pair_matrices
    )
    left_gathered, right_gathered = gather_sides(left_side, right_side)
    pairwise_input, right_side = lax.optimization_barrier((pairwise_input, right_side))
    tri_stack = pair_front(pairwise_input, triangle_projection_weight)
    moved = send_whole(tri_stack)
    product = triangle_product(moved)
    product, left_gathered = lax.optimization_barrier((product, left_gathered))
    product_tile = send_back(product)
    outer_update = outer_product(left_gathered, right_gathered, outer_output_weight)
    product_tile, outer_update = lax.optimization_barrier((product_tile, outer_update))
    pairwise_output = pair_back(
        pairwise_input,
        product_tile,
        outer_update,
        triangle_projection_weight,
        triangle_output_weight,
        pairwise_up_weight,
        pairwise_down_weight,
    )
    return (refreshed_homolog_features, pairwise_output)


def solution(mesh):
    return jax.shard_map(
        on_device,
        mesh=mesh,
        in_specs=(
            P(("branch", "rows"), None, None),
            P("rows", "branch", None),
            P(),
            P(),
            P(),
            P(),
            P(),
            P(),
            P(),
            P(),
        ),
        out_specs=(P(("branch", "rows"), None, None), P("rows", "branch", None)),
        check_vma=False,
    )
```

```python
import jax
import jax.numpy as jnp
from jax import lax
from jax.experimental import pallas as pl
from jax.experimental.pallas import tpu as pltpu
from jax.sharding import PartitionSpec as P


def standardize_features(values, dimension):
    average = jnp.mean(values, axis=dimension, keepdims=True)
    centered = values - average
    variance = jnp.mean(centered * centered, axis=dimension, keepdims=True)
    return centered * lax.rsqrt(variance + 1e-05)


def alignment_branch(
    homolog_features, transition_expand_matrix, transition_contract_matrix, factor_pair_matrices
):
    local_rows, sequence_length, channel_width = homolog_features.shape
    homolog_real_matrix = homolog_features.astype(jnp.float32)
    standardized_homologs = (
        standardize_features(homolog_real_matrix, -1)
        .astype(jnp.bfloat16)
        .reshape(local_rows * sequence_length, channel_width)
    )
    expanded_activations = jax.nn.relu(
        jnp.dot(standardized_homologs, transition_expand_matrix, preferred_element_type=jnp.float32)
    ).astype(jnp.bfloat16)
    refreshed_homolog_features = (
        homolog_real_matrix
        + jnp.dot(
            expanded_activations, transition_contract_matrix, preferred_element_type=jnp.float32
        ).reshape(homolog_features.shape)
    ).astype(jnp.bfloat16)
    standardized_for_factors = (
        standardize_features(refreshed_homolog_features.astype(jnp.float32), -1)
        .astype(jnp.bfloat16)
        .reshape(local_rows * sequence_length, channel_width)
    )
    projected = jnp.dot(
        standardized_for_factors, factor_pair_matrices, preferred_element_type=jnp.float32
    ).reshape(local_rows, sequence_length, -1)
    channels = projected.shape[-1] // 2
    left_side = projected[..., :channels].astype(jnp.bfloat16)
    right_side = jnp.swapaxes(projected[..., channels:].astype(jnp.bfloat16), 1, 2)
    return (refreshed_homolog_features, left_side, right_side)


def branch_pair(mine, theirs):
    first = lax.axis_index("branch") == 0
    return jnp.where(first, jnp.concatenate([mine, theirs]), jnp.concatenate([theirs, mine]))


def gather_sides(left_side, right_side):
    swap = [(0, 1), (1, 0)]
    left_pair = branch_pair(left_side, lax.ppermute(left_side, "branch", swap))
    left_gathered = lax.all_to_all(left_pair, "rows", split_axis=1, concat_axis=0, tiled=True)
    half = right_side.shape[2] // 2
    me = lax.axis_index("branch")
    keep = lax.dynamic_slice_in_dim(right_side, me * half, half, axis=2)
    send = lax.dynamic_slice_in_dim(right_side, (1 - me) * half, half, axis=2)
    right_pair = branch_pair(keep, lax.ppermute(send, "branch", swap))
    right_gathered = lax.all_gather(jnp.swapaxes(right_pair, 0, 1), "rows", axis=1, tiled=True)
    return left_gathered, right_gathered


def send_whole(tri_stack):
    both = ("branch", "rows")
    moved = lax.all_to_all(tri_stack, both, split_axis=0, concat_axis=0, tiled=True)
    return moved


def send_back(product):
    return lax.all_to_all(product, ("branch", "rows"), split_axis=0, concat_axis=0, tiled=True)


def logistic(values):
    return 0.5 * jnp.tanh(0.5 * values) + 0.5


def front_kernel(pair_ref, w_ref, out_ref, norm_ref, left_ref, right_ref):
    tile_rows, columns, chans = pair_ref.shape
    block = out_ref.shape[0]

    @pl.when(pl.program_id(0) == 0)
    def _():
        for r in range(tile_rows):
            norm_ref[r] = standardize_features(pair_ref[r].astype(jnp.float32), -1).astype(
                norm_ref.dtype
            )

    weight = w_ref[...].reshape(4 * block, chans)
    for r in range(tile_rows):
        proj = lax.dot_general(
            weight, norm_ref[r], (((1,), (1,)), ((), ())), preferred_element_type=jnp.float32
        )
        left_ref[:, r, :] = logistic(proj[block : 2 * block]) * proj[:block]
        right_ref[:, r, :] = logistic(proj[3 * block :]) * proj[2 * block : 3 * block]
    out_ref[:, 0] = left_ref[...].astype(out_ref.dtype)
    out_ref[:, 1] = right_ref[...].astype(out_ref.dtype)


def pair_front(pairwise_input, triangle_projection_weight):
    tile_rows, columns, chans = pairwise_input.shape
    block = 32
    weight = triangle_projection_weight[:, : 4 * chans].T.reshape(4, chans, chans)
    return pl.pallas_call(
        front_kernel,
        out_shape=jax.ShapeDtypeStruct((chans, 2, tile_rows, columns), jnp.bfloat16),
        grid=(chans // block,),
        in_specs=[
            pl.BlockSpec((tile_rows, columns, chans), lambda g: (0, 0, 0)),
            pl.BlockSpec((4, block, chans), lambda g: (0, g, 0)),
        ],
        out_specs=pl.BlockSpec((block, 2, tile_rows, columns), lambda g: (g, 0, 0, 0)),
        scratch_shapes=[
            pltpu.VMEM((tile_rows, columns, chans), jnp.bfloat16),
            pltpu.VMEM((block, tile_rows, columns), jnp.float32),
            pltpu.VMEM((block, tile_rows, columns), jnp.float32),
        ],
        cost_estimate=pl.CostEstimate(
            flops=2 * tile_rows * columns * chans * 4 * chans,
            transcendentals=2 * tile_rows * columns * chans,
            bytes_accessed=tile_rows * columns * chans * 6,
        ),
    )(pairwise_input, weight)


def product_kernel(moved_ref, out_ref):
    halves, span, columns = out_ref.shape
    n_src, _, tile_rows, _ = moved_ref.shape
    per_half = n_src // halves
    per_out = per_half // halves
    for h in range(halves):
        total = None
        for b in range(halves):
            left = moved_ref[b * per_half : (b + 1) * per_half, 0]
            first = b * per_half + h * per_out
            right = moved_ref[first : first + per_out, 1]
            part = lax.dot_general(
                left.reshape(per_half * tile_rows, columns),
                right.reshape(per_out * tile_rows, columns),
                (((1,), (1,)), ((), ())),
                preferred_element_type=jnp.float32,
            )
            total = part if total is None else total + part
        out_ref[h] = total.astype(out_ref.dtype)


def triangle_product(moved):
    n_src, _, tile_rows, columns = moved.shape
    halves = lax.axis_size("branch")
    product = pl.pallas_call(
        product_kernel,
        out_shape=jax.ShapeDtypeStruct((halves, n_src * tile_rows // halves, columns), jnp.bfloat16),
        in_specs=[pl.BlockSpec(memory_space=pltpu.VMEM)],
        out_specs=pl.BlockSpec(memory_space=pltpu.VMEM),
        cost_estimate=pl.CostEstimate(
            flops=2 * (n_src * tile_rows) ** 2 * columns // halves,
            transcendentals=0,
            bytes_accessed=moved.size * 2 + n_src * tile_rows * columns * 2,
        ),
    )(moved)
    return product.reshape(-1, tile_rows, columns)


def back_kernel(prod_ref, pair_ref, outer_ref, wo_ref, wg_ref, wu_ref, wd_ref, out_ref):
    rows, columns, chans = pair_ref.shape
    for r in range(rows):
        prod = prod_ref[:, r * columns : (r + 1) * columns].astype(jnp.float32)
        prod_norm = standardize_features(prod, 0).T.astype(jnp.bfloat16)
        tri_update = jnp.dot(prod_norm, wo_ref[...], preferred_element_type=jnp.float32)
        pair_float = pair_ref[r].astype(jnp.float32)
        pair_norm = standardize_features(pair_float, -1).astype(jnp.bfloat16)
        gate = logistic(
            jnp.dot(pair_norm, wg_ref[...], preferred_element_type=jnp.float32)
        )
        pair_mid = pair_float + gate * tri_update
        mid_norm = standardize_features(pair_mid, -1).astype(jnp.bfloat16)
        hidden = jnp.maximum(
            jnp.dot(mid_norm, wu_ref[...], preferred_element_type=jnp.float32), 0.0
        ).astype(jnp.bfloat16)
        down = jnp.dot(hidden, wd_ref[...], preferred_element_type=jnp.float32)
        out_ref[r] = (pair_mid + down + outer_ref[r]).astype(out_ref.dtype)


def pair_back(
    pairwise_input,
    product_tile,
    outer_update,
    triangle_projection_weight,
    triangle_output_weight,
    pairwise_up_weight,
    pairwise_down_weight,
):
    tile_rows, columns, chans = pairwise_input.shape
    step_rows = 4
    prod_flat = product_tile.reshape(chans, tile_rows * columns)
    gate_weight = triangle_projection_weight[:, 4 * chans :]
    hidden = pairwise_up_weight.shape[1]
    row_block = lambda g: (g, 0, 0)
    fixed = lambda g: (0, 0)
    return pl.pallas_call(
        back_kernel,
        out_shape=jax.ShapeDtypeStruct((tile_rows, columns, chans), jnp.bfloat16),
        grid=(tile_rows // step_rows,),
        in_specs=[
            pl.BlockSpec((chans, step_rows * columns), lambda g: (0, g)),
            pl.BlockSpec((step_rows, columns, chans), row_block),
            pl.BlockSpec((step_rows, columns, chans), row_block),
            pl.BlockSpec((chans, chans), fixed),
            pl.BlockSpec((chans, chans), fixed),
            pl.BlockSpec((chans, hidden), fixed),
            pl.BlockSpec((hidden, chans), fixed),
        ],
        out_specs=pl.BlockSpec((step_rows, columns, chans), row_block),
        cost_estimate=pl.CostEstimate(
            flops=2 * tile_rows * columns * chans * (3 * chans + 2 * hidden) // 1,
            transcendentals=tile_rows * columns * chans,
            bytes_accessed=tile_rows * columns * chans * 10,
        ),
    )(
        prod_flat,
        pairwise_input,
        outer_update,
        triangle_output_weight,
        gate_weight,
        pairwise_up_weight,
        pairwise_down_weight,
    )


def outer_kernel(lt_ref, r_ref, wt_ref, out_ref, x_ref):
    n_factor = r_ref.shape[0]
    tile_rows = out_ref.shape[0]
    scale = 1.0 / r_ref.shape[1]

    def fill(d, carry):
        vals = jnp.dot(lt_ref[...], r_ref[d], preferred_element_type=jnp.float32)
        vals = (vals * scale).astype(jnp.bfloat16)
        start = pl.multiple_of(d * n_factor, n_factor)
        for i in range(tile_rows):
            x_ref[i, pl.ds(start, n_factor), :] = vals[i * n_factor : (i + 1) * n_factor, :]
        return carry

    lax.fori_loop(0, n_factor, fill, 0)

    def emit(i, carry):
        upd = jnp.dot(wt_ref[...], x_ref[i], preferred_element_type=jnp.float32)
        out_ref[i] = upd.T
        return carry

    lax.fori_loop(0, tile_rows, emit, 0)


def outer_product(left_gathered, right_gathered, outer_output_weight):
    total_rows, tile_rows, channels = left_gathered.shape
    columns = right_gathered.shape[2]
    pair = outer_output_weight.shape[1]
    left_t = jnp.transpose(left_gathered, (1, 2, 0)).reshape(tile_rows * channels, total_rows)
    weight_t = jnp.transpose(
        outer_output_weight.reshape(channels, channels, pair), (1, 0, 2)
    ).reshape(channels * channels, pair).T
    flops = 4 * tile_rows * channels * channels * columns * (total_rows + pair) // 2
    return pl.pallas_call(
        outer_kernel,
        out_shape=jax.ShapeDtypeStruct((tile_rows, columns, pair), jnp.float32),
        in_specs=[pl.BlockSpec(memory_space=pltpu.VMEM)] * 3,
        out_specs=pl.BlockSpec(memory_space=pltpu.VMEM),
        scratch_shapes=[pltpu.VMEM((tile_rows, channels * channels, columns), jnp.bfloat16)],
        compiler_params=pltpu.CompilerParams(vmem_limit_bytes=56 * 1024 * 1024),
        cost_estimate=pl.CostEstimate(
            flops=flops, transcendentals=0, bytes_accessed=right_gathered.size * 2 + tile_rows * columns * pair * 4
        ),
    )(left_t, right_gathered, weight_t)


def on_device(
    homolog_features,
    pairwise_input,
    transition_expand_matrix,
    transition_contract_matrix,
    factor_pair_matrices,
    outer_output_weight,
    triangle_projection_weight,
    triangle_output_weight,
    pairwise_up_weight,
    pairwise_down_weight,
):
    refreshed_homolog_features, left_side, right_side = alignment_branch(
        homolog_features, transition_expand_matrix, transition_contract_matrix, factor_pair_matrices
    )
    left_gathered, right_gathered = gather_sides(left_side, right_side)
    pairwise_input, right_side = lax.optimization_barrier((pairwise_input, right_side))
    tri_stack = pair_front(pairwise_input, triangle_projection_weight)
    moved = send_whole(tri_stack)
    product = triangle_product(moved)
    product, left_gathered = lax.optimization_barrier((product, left_gathered))
    product_tile = send_back(product)
    outer_update = outer_product(left_gathered, right_gathered, outer_output_weight)
    product_tile, outer_update = lax.optimization_barrier((product_tile, outer_update))
    pairwise_output = pair_back(
        pairwise_input,
        product_tile,
        outer_update,
        triangle_projection_weight,
        triangle_output_weight,
        pairwise_up_weight,
        pairwise_down_weight,
    )
    return (refreshed_homolog_features, pairwise_output)


def solution(mesh):
    return jax.shard_map(
        on_device,
        mesh=mesh,
        in_specs=(
            P(("branch", "rows"), None, None),
            P("rows", "branch", None),
            P(),
            P(),
            P(),
            P(),
            P(),
            P(),
            P(),
            P(),
        ),
        out_specs=(P(("branch", "rows"), None, None), P("rows", "branch", None)),
        check_vma=False,
    )
```

```python
import jax
import jax.numpy as jnp
from jax import lax
from jax.experimental import pallas as pl
from jax.experimental.pallas import tpu as pltpu
from jax.sharding import PartitionSpec as P


def standardize_features(values, dimension):
    average = jnp.mean(values, axis=dimension, keepdims=True)
    centered = values - average
    variance = jnp.mean(centered * centered, axis=dimension, keepdims=True)
    return centered * lax.rsqrt(variance + 1e-05)


def alignment_branch(
    homolog_features, transition_expand_matrix, transition_contract_matrix, factor_pair_matrices
):
    local_rows, sequence_length, channel_width = homolog_features.shape
    homolog_real_matrix = homolog_features.astype(jnp.float32)
    standardized_homologs = (
        standardize_features(homolog_real_matrix, -1)
        .astype(jnp.bfloat16)
        .reshape(local_rows * sequence_length, channel_width)
    )
    expanded_activations = jax.nn.relu(
        jnp.dot(standardized_homologs, transition_expand_matrix, preferred_element_type=jnp.float32)
    ).astype(jnp.bfloat16)
    refreshed_homolog_features = (
        homolog_real_matrix
        + jnp.dot(
            expanded_activations, transition_contract_matrix, preferred_element_type=jnp.float32
        ).reshape(homolog_features.shape)
    ).astype(jnp.bfloat16)
    standardized_for_factors = (
        standardize_features(refreshed_homolog_features.astype(jnp.float32), -1)
        .astype(jnp.bfloat16)
        .reshape(local_rows * sequence_length, channel_width)
    )
    projected = jnp.dot(
        standardized_for_factors, factor_pair_matrices, preferred_element_type=jnp.float32
    ).reshape(local_rows, sequence_length, -1)
    channels = projected.shape[-1] // 2
    left_side = projected[..., :channels].astype(jnp.bfloat16)
    right_side = jnp.swapaxes(projected[..., channels:].astype(jnp.bfloat16), 1, 2)
    return (refreshed_homolog_features, left_side, right_side)


def branch_pair(mine, theirs):
    first = lax.axis_index("branch") == 0
    return jnp.where(first, jnp.concatenate([mine, theirs]), jnp.concatenate([theirs, mine]))


def gather_sides(left_side, right_side):
    swap = [(0, 1), (1, 0)]
    left_pair = branch_pair(left_side, lax.ppermute(left_side, "branch", swap))
    left_gathered = lax.all_to_all(left_pair, "rows", split_axis=1, concat_axis=0, tiled=True)
    half = right_side.shape[2] // 2
    me = lax.axis_index("branch")
    keep = lax.dynamic_slice_in_dim(right_side, me * half, half, axis=2)
    send = lax.dynamic_slice_in_dim(right_side, (1 - me) * half, half, axis=2)
    right_pair = branch_pair(keep, lax.ppermute(send, "branch", swap))
    right_gathered = lax.all_gather(jnp.swapaxes(right_pair, 0, 1), "rows", axis=1, tiled=True)
    return left_gathered, right_gathered


def send_whole(tri_stack):
    both = ("branch", "rows")
    moved = lax.all_to_all(tri_stack, both, split_axis=0, concat_axis=0, tiled=True)
    return moved


def send_back(product):
    return lax.all_to_all(product, ("branch", "rows"), split_axis=0, concat_axis=0, tiled=True)


def logistic(values):
    return 0.5 * jnp.tanh(0.5 * values) + 0.5


def front_kernel(pair_ref, w_ref, out_ref, norm_ref):
    tile_rows, columns, chans = pair_ref.shape
    block = out_ref.shape[0]

    @pl.when(pl.program_id(0) == 0)
    def _():
        for r in range(tile_rows):
            norm_ref[r] = standardize_features(pair_ref[r].astype(jnp.float32), -1).astype(
                norm_ref.dtype
            )

    weight = w_ref[...].reshape(4 * block, chans)
    for r in range(tile_rows):
        proj = lax.dot_general(
            weight, norm_ref[r], (((1,), (1,)), ((), ())), preferred_element_type=jnp.float32
        )
        out_ref[:, 0, r, :] = (
            logistic(proj[block : 2 * block]) * proj[:block]
        ).astype(out_ref.dtype)
        out_ref[:, 1, r, :] = (
            logistic(proj[3 * block :]) * proj[2 * block : 3 * block]
        ).astype(out_ref.dtype)


def pair_front(pairwise_input, triangle_projection_weight):
    tile_rows, columns, chans = pairwise_input.shape
    block = 32
    weight = triangle_projection_weight[:, : 4 * chans].T.reshape(4, chans, chans)
    return pl.pallas_call(
        front_kernel,
        out_shape=jax.ShapeDtypeStruct((chans, 2, tile_rows, columns), jnp.bfloat16),
        grid=(chans // block,),
        in_specs=[
            pl.BlockSpec((tile_rows, columns, chans), lambda g: (0, 0, 0)),
            pl.BlockSpec((4, block, chans), lambda g: (0, g, 0)),
        ],
        out_specs=pl.BlockSpec((block, 2, tile_rows, columns), lambda g: (g, 0, 0, 0)),
        scratch_shapes=[pltpu.VMEM((tile_rows, columns, chans), jnp.bfloat16)],
        cost_estimate=pl.CostEstimate(
            flops=2 * tile_rows * columns * chans * 4 * chans,
            transcendentals=2 * tile_rows * columns * chans,
            bytes_accessed=tile_rows * columns * chans * 6,
        ),
    )(pairwise_input, weight)


def product_kernel(moved_ref, out_ref):
    halves, span, columns = out_ref.shape
    n_src, _, tile_rows, _ = moved_ref.shape
    per_half = n_src // halves
    per_out = per_half // halves
    for h in range(halves):
        total = None
        for b in range(halves):
            left = moved_ref[b * per_half : (b + 1) * per_half, 0]
            first = b * per_half + h * per_out
            right = moved_ref[first : first + per_out, 1]
            part = lax.dot_general(
                left.reshape(per_half * tile_rows, columns),
                right.reshape(per_out * tile_rows, columns),
                (((1,), (1,)), ((), ())),
                preferred_element_type=jnp.float32,
            )
            total = part if total is None else total + part
        out_ref[h] = total.astype(out_ref.dtype)


def triangle_product(moved):
    n_src, _, tile_rows, columns = moved.shape
    halves = lax.axis_size("branch")
    product = pl.pallas_call(
        product_kernel,
        out_shape=jax.ShapeDtypeStruct((halves, n_src * tile_rows // halves, columns), jnp.bfloat16),
        in_specs=[pl.BlockSpec(memory_space=pltpu.VMEM)],
        out_specs=pl.BlockSpec(memory_space=pltpu.VMEM),
        cost_estimate=pl.CostEstimate(
            flops=2 * (n_src * tile_rows) ** 2 * columns // halves,
            transcendentals=0,
            bytes_accessed=moved.size * 2 + n_src * tile_rows * columns * 2,
        ),
    )(moved)
    return product.reshape(-1, tile_rows, columns)


def back_kernel(prod_ref, pair_ref, outer_ref, wo_ref, wg_ref, wu_ref, wd_ref, out_ref):
    rows, columns, chans = pair_ref.shape
    for r in range(rows):
        prod = prod_ref[:, r, :].astype(jnp.float32)
        prod_norm = standardize_features(prod, 0).T.astype(jnp.bfloat16)
        tri_update = jnp.dot(prod_norm, wo_ref[...], preferred_element_type=jnp.float32)
        pair_float = pair_ref[r].astype(jnp.float32)
        pair_norm = standardize_features(pair_float, -1).astype(jnp.bfloat16)
        gate = logistic(
            jnp.dot(pair_norm, wg_ref[...], preferred_element_type=jnp.float32)
        )
        pair_mid = pair_float + gate * tri_update
        mid_norm = standardize_features(pair_mid, -1).astype(jnp.bfloat16)
        hidden = jnp.maximum(
            jnp.dot(mid_norm, wu_ref[...], preferred_element_type=jnp.float32), 0.0
        ).astype(jnp.bfloat16)
        down = jnp.dot(hidden, wd_ref[...], preferred_element_type=jnp.float32)
        out_ref[r] = (pair_mid + down + outer_ref[r]).astype(out_ref.dtype)


def pair_back(
    pairwise_input,
    product_tile,
    outer_update,
    triangle_projection_weight,
    triangle_output_weight,
    pairwise_up_weight,
    pairwise_down_weight,
):
    tile_rows, columns, chans = pairwise_input.shape
    step_rows = 8
    gate_weight = triangle_projection_weight[:, 4 * chans :]
    hidden = pairwise_up_weight.shape[1]
    row_block = lambda g: (g, 0, 0)
    fixed = lambda g: (0, 0)
    return pl.pallas_call(
        back_kernel,
        out_shape=jax.ShapeDtypeStruct((tile_rows, columns, chans), jnp.bfloat16),
        grid=(tile_rows // step_rows,),
        in_specs=[
            pl.BlockSpec((chans, step_rows, columns), lambda g: (0, g, 0)),
            pl.BlockSpec((step_rows, columns, chans), row_block),
            pl.BlockSpec((step_rows, columns, chans), row_block),
            pl.BlockSpec((chans, chans), fixed),
            pl.BlockSpec((chans, chans), fixed),
            pl.BlockSpec((chans, hidden), fixed),
            pl.BlockSpec((hidden, chans), fixed),
        ],
        out_specs=pl.BlockSpec((step_rows, columns, chans), row_block),
        cost_estimate=pl.CostEstimate(
            flops=2 * tile_rows * columns * chans * (3 * chans + 2 * hidden) // 1,
            transcendentals=tile_rows * columns * chans,
            bytes_accessed=tile_rows * columns * chans * 10,
        ),
    )(
        product_tile,
        pairwise_input,
        outer_update,
        triangle_output_weight,
        gate_weight,
        pairwise_up_weight,
        pairwise_down_weight,
    )


def outer_kernel(lt_ref, r_ref, wt_ref, out_ref, x_ref):
    n_factor = r_ref.shape[0]
    tile_rows = out_ref.shape[0]
    scale = 1.0 / r_ref.shape[1]

    def fill(d, carry):
        vals = jnp.dot(lt_ref[...], r_ref[d], preferred_element_type=jnp.float32)
        vals = (vals * scale).astype(jnp.bfloat16)
        start = pl.multiple_of(d * n_factor, n_factor)
        for i in range(tile_rows):
            x_ref[i, pl.ds(start, n_factor), :] = vals[i * n_factor : (i + 1) * n_factor, :]
        return carry

    lax.fori_loop(0, n_factor, fill, 0)

    def emit(i, carry):
        upd = jnp.dot(wt_ref[...], x_ref[i], preferred_element_type=jnp.float32)
        out_ref[i] = upd.T
        return carry

    lax.fori_loop(0, tile_rows, emit, 0)


def outer_product(left_gathered, right_gathered, outer_output_weight):
    total_rows, tile_rows, channels = left_gathered.shape
    columns = right_gathered.shape[2]
    pair = outer_output_weight.shape[1]
    left_t = jnp.transpose(left_gathered, (1, 2, 0)).reshape(tile_rows * channels, total_rows)
    weight_t = jnp.transpose(
        outer_output_weight.reshape(channels, channels, pair), (1, 0, 2)
    ).reshape(channels * channels, pair).T
    flops = 4 * tile_rows * channels * channels * columns * (total_rows + pair) // 2
    return pl.pallas_call(
        outer_kernel,
        out_shape=jax.ShapeDtypeStruct((tile_rows, columns, pair), jnp.float32),
        in_specs=[pl.BlockSpec(memory_space=pltpu.VMEM)] * 3,
        out_specs=pl.BlockSpec(memory_space=pltpu.VMEM),
        scratch_shapes=[pltpu.VMEM((tile_rows, channels * channels, columns), jnp.bfloat16)],
        compiler_params=pltpu.CompilerParams(vmem_limit_bytes=56 * 1024 * 1024),
        cost_estimate=pl.CostEstimate(
            flops=flops, transcendentals=0, bytes_accessed=right_gathered.size * 2 + tile_rows * columns * pair * 4
        ),
    )(left_t, right_gathered, weight_t)


def on_device(
    homolog_features,
    pairwise_input,
    transition_expand_matrix,
    transition_contract_matrix,
    factor_pair_matrices,
    outer_output_weight,
    triangle_projection_weight,
    triangle_output_weight,
    pairwise_up_weight,
    pairwise_down_weight,
):
    refreshed_homolog_features, left_side, right_side = alignment_branch(
        homolog_features, transition_expand_matrix, transition_contract_matrix, factor_pair_matrices
    )
    left_gathered, right_gathered = gather_sides(left_side, right_side)
    pairwise_input, right_side = lax.optimization_barrier((pairwise_input, right_side))
    tri_stack = pair_front(pairwise_input, triangle_projection_weight)
    moved = send_whole(tri_stack)
    product = triangle_product(moved)
    product, left_gathered = lax.optimization_barrier((product, left_gathered))
    product_tile = send_back(product)
    outer_update = outer_product(left_gathered, right_gathered, outer_output_weight)
    product_tile, outer_update = lax.optimization_barrier((product_tile, outer_update))
    pairwise_output = pair_back(
        pairwise_input,
        product_tile,
        outer_update,
        triangle_projection_weight,
        triangle_output_weight,
        pairwise_up_weight,
        pairwise_down_weight,
    )
    return (refreshed_homolog_features, pairwise_output)


def solution(mesh):
    return jax.shard_map(
        on_device,
        mesh=mesh,
        in_specs=(
            P(("branch", "rows"), None, None),
            P("rows", "branch", None),
            P(),
            P(),
            P(),
            P(),
            P(),
            P(),
            P(),
            P(),
        ),
        out_specs=(P(("branch", "rows"), None, None), P("rows", "branch", None)),
        check_vma=False,
    )
```

```python
import jax
import jax.numpy as jnp
from jax import lax
from jax.experimental import pallas as pl
from jax.experimental.pallas import tpu as pltpu
from jax.sharding import PartitionSpec as P


def standardize_features(values, dimension):
    average = jnp.mean(values, axis=dimension, keepdims=True)
    centered = values - average
    variance = jnp.mean(centered * centered, axis=dimension, keepdims=True)
    return centered * lax.rsqrt(variance + 1e-05)


def alignment_branch(
    homolog_features, transition_expand_matrix, transition_contract_matrix, factor_pair_matrices
):
    local_rows, sequence_length, channel_width = homolog_features.shape
    homolog_real_matrix = homolog_features.astype(jnp.float32)
    standardized_homologs = (
        standardize_features(homolog_real_matrix, -1)
        .astype(jnp.bfloat16)
        .reshape(local_rows * sequence_length, channel_width)
    )
    expanded_activations = jax.nn.relu(
        jnp.dot(standardized_homologs, transition_expand_matrix, preferred_element_type=jnp.float32)
    ).astype(jnp.bfloat16)
    refreshed_homolog_features = (
        homolog_real_matrix
        + jnp.dot(
            expanded_activations, transition_contract_matrix, preferred_element_type=jnp.float32
        ).reshape(homolog_features.shape)
    ).astype(jnp.bfloat16)
    standardized_for_factors = (
        standardize_features(refreshed_homolog_features.astype(jnp.float32), -1)
        .astype(jnp.bfloat16)
        .reshape(local_rows * sequence_length, channel_width)
    )
    projected = jnp.dot(
        standardized_for_factors, factor_pair_matrices, preferred_element_type=jnp.float32
    ).reshape(local_rows, sequence_length, -1)
    channels = projected.shape[-1] // 2
    left_side = projected[..., :channels].astype(jnp.bfloat16)
    right_side = jnp.swapaxes(projected[..., channels:].astype(jnp.bfloat16), 1, 2)
    return (refreshed_homolog_features, left_side, right_side)


def branch_pair(mine, theirs):
    first = lax.axis_index("branch") == 0
    return jnp.where(first, jnp.concatenate([mine, theirs]), jnp.concatenate([theirs, mine]))


def gather_sides(left_side, right_side):
    swap = [(0, 1), (1, 0)]
    left_pair = branch_pair(left_side, lax.ppermute(left_side, "branch", swap))
    left_gathered = lax.all_to_all(left_pair, "rows", split_axis=1, concat_axis=0, tiled=True)
    half = right_side.shape[2] // 2
    me = lax.axis_index("branch")
    keep = lax.dynamic_slice_in_dim(right_side, me * half, half, axis=2)
    send = lax.dynamic_slice_in_dim(right_side, (1 - me) * half, half, axis=2)
    right_pair = branch_pair(keep, lax.ppermute(send, "branch", swap))
    right_gathered = lax.all_gather(jnp.swapaxes(right_pair, 0, 1), "rows", axis=1, tiled=True)
    return left_gathered, right_gathered


def send_whole(tri_stack):
    both = ("branch", "rows")
    moved = lax.all_to_all(tri_stack, both, split_axis=0, concat_axis=0, tiled=True)
    return moved


def send_back(product):
    return lax.all_to_all(product, ("branch", "rows"), split_axis=0, concat_axis=0, tiled=True)


def logistic(values):
    return 0.5 * jnp.tanh(0.5 * values) + 0.5


def front_kernel(pair_ref, w_ref, out_ref, norm_ref):
    tile_rows, columns, chans = pair_ref.shape
    block = out_ref.shape[0]

    @pl.when(pl.program_id(0) == 0)
    def _():
        for r in range(tile_rows):
            norm_ref[r] = standardize_features(pair_ref[r].astype(jnp.float32), -1).astype(
                norm_ref.dtype
            )

    weight = w_ref[...].reshape(4 * block, chans)
    for r in range(tile_rows):
        proj = lax.dot_general(
            weight, norm_ref[r], (((1,), (1,)), ((), ())), preferred_element_type=jnp.float32
        )
        out_ref[:, 0, r, :] = (
            logistic(proj[block : 2 * block]) * proj[:block]
        ).astype(out_ref.dtype)
        out_ref[:, 1, r, :] = (
            logistic(proj[3 * block :]) * proj[2 * block : 3 * block]
        ).astype(out_ref.dtype)


def pair_front(pairwise_input, triangle_projection_weight):
    tile_rows, columns, chans = pairwise_input.shape
    block = 32
    weight = triangle_projection_weight[:, : 4 * chans].T.reshape(4, chans, chans)
    return pl.pallas_call(
        front_kernel,
        out_shape=jax.ShapeDtypeStruct((chans, 2, tile_rows, columns), jnp.bfloat16),
        grid=(chans // block,),
        in_specs=[
            pl.BlockSpec((tile_rows, columns, chans), lambda g: (0, 0, 0)),
            pl.BlockSpec((4, block, chans), lambda g: (0, g, 0)),
        ],
        out_specs=pl.BlockSpec((block, 2, tile_rows, columns), lambda g: (g, 0, 0, 0)),
        scratch_shapes=[pltpu.VMEM((tile_rows, columns, chans), jnp.bfloat16)],
        cost_estimate=pl.CostEstimate(
            flops=2 * tile_rows * columns * chans * 4 * chans,
            transcendentals=2 * tile_rows * columns * chans,
            bytes_accessed=tile_rows * columns * chans * 6,
        ),
    )(pairwise_input, weight)


def product_kernel(moved_ref, out_ref):
    halves, span, columns = out_ref.shape
    n_src, _, tile_rows, _ = moved_ref.shape
    per_half = n_src // halves
    per_out = per_half // halves
    for h in range(halves):
        total = None
        for b in range(halves):
            left = moved_ref[b * per_half : (b + 1) * per_half, 0]
            first = b * per_half + h * per_out
            right = moved_ref[first : first + per_out, 1]
            part = lax.dot_general(
                left.reshape(per_half * tile_rows, columns),
                right.reshape(per_out * tile_rows, columns),
                (((1,), (1,)), ((), ())),
                preferred_element_type=jnp.float32,
            )
            total = part if total is None else total + part
        out_ref[h] = total.astype(out_ref.dtype)


def triangle_product(moved):
    n_src, _, tile_rows, columns = moved.shape
    halves = lax.axis_size("branch")
    product = pl.pallas_call(
        product_kernel,
        out_shape=jax.ShapeDtypeStruct((halves, n_src * tile_rows // halves, columns), jnp.bfloat16),
        in_specs=[pl.BlockSpec(memory_space=pltpu.VMEM)],
        out_specs=pl.BlockSpec(memory_space=pltpu.VMEM),
        cost_estimate=pl.CostEstimate(
            flops=2 * (n_src * tile_rows) ** 2 * columns // halves,
            transcendentals=0,
            bytes_accessed=moved.size * 2 + n_src * tile_rows * columns * 2,
        ),
    )(moved)
    return product.reshape(-1, tile_rows, columns)


def back_kernel(prod_ref, pair_ref, outer_ref, wo_ref, wg_ref, wu_ref, wd_ref, out_ref):
    rows, columns, chans = pair_ref.shape
    for r in range(rows):
        prod = prod_ref[:, r * columns : (r + 1) * columns].astype(jnp.float32)
        prod_norm = standardize_features(prod, 0).T.astype(jnp.bfloat16)
        tri_update = jnp.dot(prod_norm, wo_ref[...], preferred_element_type=jnp.float32)
        pair_float = pair_ref[r].astype(jnp.float32)
        pair_norm = standardize_features(pair_float, -1).astype(jnp.bfloat16)
        gate = logistic(
            jnp.dot(pair_norm, wg_ref[...], preferred_element_type=jnp.float32)
        )
        pair_mid = pair_float + gate * tri_update
        mid_norm = standardize_features(pair_mid, -1).astype(jnp.bfloat16)
        hidden = jnp.maximum(
            jnp.dot(mid_norm, wu_ref[...], preferred_element_type=jnp.float32), 0.0
        ).astype(jnp.bfloat16)
        down = jnp.dot(hidden, wd_ref[...], preferred_element_type=jnp.float32)
        out_ref[r] = (pair_mid + down + outer_ref[r]).astype(out_ref.dtype)


def pair_back(
    pairwise_input,
    product_tile,
    outer_update,
    triangle_projection_weight,
    triangle_output_weight,
    pairwise_up_weight,
    pairwise_down_weight,
):
    tile_rows, columns, chans = pairwise_input.shape
    step_rows = 4
    prod_flat = product_tile.reshape(chans, tile_rows * columns)
    gate_weight = triangle_projection_weight[:, 4 * chans :]
    hidden = pairwise_up_weight.shape[1]
    row_block = lambda g: (g, 0, 0)
    fixed = lambda g: (0, 0)
    return pl.pallas_call(
        back_kernel,
        out_shape=jax.ShapeDtypeStruct((tile_rows, columns, chans), jnp.bfloat16),
        grid=(tile_rows // step_rows,),
        in_specs=[
            pl.BlockSpec((chans, step_rows * columns), lambda g: (0, g)),
            pl.BlockSpec((step_rows, columns, chans), row_block),
            pl.BlockSpec((step_rows, columns, chans), row_block),
            pl.BlockSpec((chans, chans), fixed),
            pl.BlockSpec((chans, chans), fixed),
            pl.BlockSpec((chans, hidden), fixed),
            pl.BlockSpec((hidden, chans), fixed),
        ],
        out_specs=pl.BlockSpec((step_rows, columns, chans), row_block),
        cost_estimate=pl.CostEstimate(
            flops=2 * tile_rows * columns * chans * (3 * chans + 2 * hidden) // 1,
            transcendentals=tile_rows * columns * chans,
            bytes_accessed=tile_rows * columns * chans * 10,
        ),
    )(
        prod_flat,
        pairwise_input,
        outer_update,
        triangle_output_weight,
        gate_weight,
        pairwise_up_weight,
        pairwise_down_weight,
    )


def outer_kernel(lt_ref, r_ref, wt_ref, out_ref, x_ref):
    n_factor = r_ref.shape[0]
    tile_rows = out_ref.shape[0]
    scale = 1.0 / r_ref.shape[1]

    def fill(d, carry):
        vals = jnp.dot(lt_ref[...], r_ref[d], preferred_element_type=jnp.float32)
        vals = (vals * scale).astype(jnp.bfloat16)
        start = pl.multiple_of(d * n_factor, n_factor)
        for i in range(tile_rows):
            x_ref[i, pl.ds(start, n_factor), :] = vals[i * n_factor : (i + 1) * n_factor, :]
        return carry

    lax.fori_loop(0, n_factor, fill, 0)

    def emit(i, carry):
        upd = jnp.dot(wt_ref[...], x_ref[i], preferred_element_type=jnp.float32)
        out_ref[i] = upd.T
        return carry

    lax.fori_loop(0, tile_rows, emit, 0)


def outer_product(left_gathered, right_gathered, outer_output_weight):
    total_rows, tile_rows, channels = left_gathered.shape
    columns = right_gathered.shape[2]
    pair = outer_output_weight.shape[1]
    left_t = jnp.transpose(left_gathered, (1, 2, 0)).reshape(tile_rows * channels, total_rows)
    weight_t = jnp.transpose(
        outer_output_weight.reshape(channels, channels, pair), (1, 0, 2)
    ).reshape(channels * channels, pair).T
    flops = 4 * tile_rows * channels * channels * columns * (total_rows + pair) // 2
    return pl.pallas_call(
        outer_kernel,
        out_shape=jax.ShapeDtypeStruct((tile_rows, columns, pair), jnp.float32),
        in_specs=[pl.BlockSpec(memory_space=pltpu.VMEM)] * 3,
        out_specs=pl.BlockSpec(memory_space=pltpu.VMEM),
        scratch_shapes=[pltpu.VMEM((tile_rows, channels * channels, columns), jnp.bfloat16)],
        compiler_params=pltpu.CompilerParams(vmem_limit_bytes=56 * 1024 * 1024),
        cost_estimate=pl.CostEstimate(
            flops=flops, transcendentals=0, bytes_accessed=right_gathered.size * 2 + tile_rows * columns * pair * 4
        ),
    )(left_t, right_gathered, weight_t)


def on_device(
    homolog_features,
    pairwise_input,
    transition_expand_matrix,
    transition_contract_matrix,
    factor_pair_matrices,
    outer_output_weight,
    triangle_projection_weight,
    triangle_output_weight,
    pairwise_up_weight,
    pairwise_down_weight,
):
    tri_stack = pair_front(pairwise_input, triangle_projection_weight)
    moved = send_whole(tri_stack)
    homolog_features, tri_stack = lax.optimization_barrier((homolog_features, tri_stack))
    refreshed_homolog_features, left_side, right_side = alignment_branch(
        homolog_features, transition_expand_matrix, transition_contract_matrix, factor_pair_matrices
    )
    left_gathered, right_gathered = gather_sides(left_side, right_side)
    product = triangle_product(moved)
    product, left_gathered = lax.optimization_barrier((product, left_gathered))
    product_tile = send_back(product)
    outer_update = outer_product(left_gathered, right_gathered, outer_output_weight)
    product_tile, outer_update = lax.optimization_barrier((product_tile, outer_update))
    pairwise_output = pair_back(
        pairwise_input,
        product_tile,
        outer_update,
        triangle_projection_weight,
        triangle_output_weight,
        pairwise_up_weight,
        pairwise_down_weight,
    )
    return (refreshed_homolog_features, pairwise_output)


def solution(mesh):
    return jax.shard_map(
        on_device,
        mesh=mesh,
        in_specs=(
            P(("branch", "rows"), None, None),
            P("rows", "branch", None),
            P(),
            P(),
            P(),
            P(),
            P(),
            P(),
            P(),
            P(),
        ),
        out_specs=(P(("branch", "rows"), None, None), P("rows", "branch", None)),
        check_vma=False,
    )
```

```python
import jax
import jax.numpy as jnp
from jax import lax
from jax.experimental import pallas as pl
from jax.experimental.pallas import tpu as pltpu
from jax.sharding import PartitionSpec as P


def standardize_features(values, dimension):
    average = jnp.mean(values, axis=dimension, keepdims=True)
    centered = values - average
    variance = jnp.mean(centered * centered, axis=dimension, keepdims=True)
    return centered * lax.rsqrt(variance + 1e-05)


def alignment_branch(
    homolog_features, transition_expand_matrix, transition_contract_matrix, factor_pair_matrices
):
    local_rows, sequence_length, channel_width = homolog_features.shape
    homolog_real_matrix = homolog_features.astype(jnp.float32)
    standardized_homologs = (
        standardize_features(homolog_real_matrix, -1)
        .astype(jnp.bfloat16)
        .reshape(local_rows * sequence_length, channel_width)
    )
    expanded_activations = jax.nn.relu(
        jnp.dot(standardized_homologs, transition_expand_matrix, preferred_element_type=jnp.float32)
    ).astype(jnp.bfloat16)
    refreshed_homolog_features = (
        homolog_real_matrix
        + jnp.dot(
            expanded_activations, transition_contract_matrix, preferred_element_type=jnp.float32
        ).reshape(homolog_features.shape)
    ).astype(jnp.bfloat16)
    standardized_for_factors = (
        standardize_features(refreshed_homolog_features.astype(jnp.float32), -1)
        .astype(jnp.bfloat16)
        .reshape(local_rows * sequence_length, channel_width)
    )
    projected = jnp.dot(
        standardized_for_factors, factor_pair_matrices, preferred_element_type=jnp.float32
    ).reshape(local_rows, sequence_length, -1)
    channels = projected.shape[-1] // 2
    left_side = projected[..., :channels].astype(jnp.bfloat16)
    right_side = jnp.swapaxes(projected[..., channels:].astype(jnp.bfloat16), 1, 2)
    return (refreshed_homolog_features, left_side, right_side)


def branch_pair(mine, theirs):
    first = lax.axis_index("branch") == 0
    return jnp.where(first, jnp.concatenate([mine, theirs]), jnp.concatenate([theirs, mine]))


def gather_sides(left_side, right_side):
    swap = [(0, 1), (1, 0)]
    left_pair = branch_pair(left_side, lax.ppermute(left_side, "branch", swap))
    left_gathered = lax.all_to_all(left_pair, "rows", split_axis=1, concat_axis=0, tiled=True)
    half = right_side.shape[2] // 2
    me = lax.axis_index("branch")
    keep = lax.dynamic_slice_in_dim(right_side, me * half, half, axis=2)
    send = lax.dynamic_slice_in_dim(right_side, (1 - me) * half, half, axis=2)
    right_pair = branch_pair(keep, lax.ppermute(send, "branch", swap))
    right_gathered = lax.all_gather(jnp.swapaxes(right_pair, 0, 1), "rows", axis=1, tiled=True)
    return left_gathered, right_gathered


def send_whole(tri_stack):
    both = ("branch", "rows")
    moved = lax.all_to_all(tri_stack, both, split_axis=0, concat_axis=0, tiled=True)
    return moved


def send_back(product):
    return lax.all_to_all(product, ("branch", "rows"), split_axis=0, concat_axis=0, tiled=True)


def logistic(values):
    return 0.5 * jnp.tanh(0.5 * values) + 0.5


def front_kernel(pair_ref, w_ref, out_ref, norm_ref):
    tile_rows, columns, chans = pair_ref.shape
    block = out_ref.shape[0]

    @pl.when(pl.program_id(0) == 0)
    def _():
        for r in range(tile_rows):
            norm_ref[r] = standardize_features(pair_ref[r].astype(jnp.float32), -1).astype(
                norm_ref.dtype
            )

    weight = w_ref[...].reshape(4 * block, chans)
    for r in range(tile_rows):
        proj = lax.dot_general(
            weight, norm_ref[r], (((1,), (1,)), ((), ())), preferred_element_type=jnp.float32
        )
        out_ref[:, 0, r, :] = (
            logistic(proj[block : 2 * block]) * proj[:block]
        ).astype(out_ref.dtype)
        out_ref[:, 1, r, :] = (
            logistic(proj[3 * block :]) * proj[2 * block : 3 * block]
        ).astype(out_ref.dtype)


def pair_front(pairwise_input, triangle_projection_weight):
    tile_rows, columns, chans = pairwise_input.shape
    block = 64
    weight = triangle_projection_weight[:, : 4 * chans].T.reshape(4, chans, chans)
    return pl.pallas_call(
        front_kernel,
        out_shape=jax.ShapeDtypeStruct((chans, 2, tile_rows, columns), jnp.bfloat16),
        grid=(chans // block,),
        in_specs=[
            pl.BlockSpec((tile_rows, columns, chans), lambda g: (0, 0, 0)),
            pl.BlockSpec((4, block, chans), lambda g: (0, g, 0)),
        ],
        out_specs=pl.BlockSpec((block, 2, tile_rows, columns), lambda g: (g, 0, 0, 0)),
        scratch_shapes=[pltpu.VMEM((tile_rows, columns, chans), jnp.bfloat16)],
        cost_estimate=pl.CostEstimate(
            flops=2 * tile_rows * columns * chans * 4 * chans,
            transcendentals=2 * tile_rows * columns * chans,
            bytes_accessed=tile_rows * columns * chans * 6,
        ),
    )(pairwise_input, weight)


def product_kernel(moved_ref, out_ref):
    halves, span, columns = out_ref.shape
    n_src, _, tile_rows, _ = moved_ref.shape
    per_half = n_src // halves
    per_out = per_half // halves
    for h in range(halves):
        total = None
        for b in range(halves):
            left = moved_ref[b * per_half : (b + 1) * per_half, 0]
            first = b * per_half + h * per_out
            right = moved_ref[first : first + per_out, 1]
            part = lax.dot_general(
                left.reshape(per_half * tile_rows, columns),
                right.reshape(per_out * tile_rows, columns),
                (((1,), (1,)), ((), ())),
                preferred_element_type=jnp.float32,
            )
            total = part if total is None else total + part
        out_ref[h] = total.astype(out_ref.dtype)


def triangle_product(moved):
    n_src, _, tile_rows, columns = moved.shape
    halves = lax.axis_size("branch")
    product = pl.pallas_call(
        product_kernel,
        out_shape=jax.ShapeDtypeStruct((halves, n_src * tile_rows // halves, columns), jnp.bfloat16),
        in_specs=[pl.BlockSpec(memory_space=pltpu.VMEM)],
        out_specs=pl.BlockSpec(memory_space=pltpu.VMEM),
        cost_estimate=pl.CostEstimate(
            flops=2 * (n_src * tile_rows) ** 2 * columns // halves,
            transcendentals=0,
            bytes_accessed=moved.size * 2 + n_src * tile_rows * columns * 2,
        ),
    )(moved)
    return product.reshape(-1, tile_rows, columns)


def back_kernel(prod_ref, pair_ref, outer_ref, wo_ref, wg_ref, wu_ref, wd_ref, out_ref):
    rows, columns, chans = pair_ref.shape
    for r in range(rows):
        prod = prod_ref[:, r * columns : (r + 1) * columns].astype(jnp.float32)
        prod_norm = standardize_features(prod, 0).T.astype(jnp.bfloat16)
        tri_update = jnp.dot(prod_norm, wo_ref[...], preferred_element_type=jnp.float32)
        pair_float = pair_ref[r].astype(jnp.float32)
        pair_norm = standardize_features(pair_float, -1).astype(jnp.bfloat16)
        gate = logistic(
            jnp.dot(pair_norm, wg_ref[...], preferred_element_type=jnp.float32)
        )
        pair_mid = pair_float + gate * tri_update
        mid_norm = standardize_features(pair_mid, -1).astype(jnp.bfloat16)
        hidden = jnp.maximum(
            jnp.dot(mid_norm, wu_ref[...], preferred_element_type=jnp.float32), 0.0
        ).astype(jnp.bfloat16)
        down = jnp.dot(hidden, wd_ref[...], preferred_element_type=jnp.float32)
        out_ref[r] = (pair_mid + down + outer_ref[r]).astype(out_ref.dtype)


def pair_back(
    pairwise_input,
    product_tile,
    outer_update,
    triangle_projection_weight,
    triangle_output_weight,
    pairwise_up_weight,
    pairwise_down_weight,
):
    tile_rows, columns, chans = pairwise_input.shape
    step_rows = 4
    prod_flat = product_tile.reshape(chans, tile_rows * columns)
    gate_weight = triangle_projection_weight[:, 4 * chans :]
    hidden = pairwise_up_weight.shape[1]
    row_block = lambda g: (g, 0, 0)
    fixed = lambda g: (0, 0)
    return pl.pallas_call(
        back_kernel,
        out_shape=jax.ShapeDtypeStruct((tile_rows, columns, chans), jnp.bfloat16),
        grid=(tile_rows // step_rows,),
        in_specs=[
            pl.BlockSpec((chans, step_rows * columns), lambda g: (0, g)),
            pl.BlockSpec((step_rows, columns, chans), row_block),
            pl.BlockSpec((step_rows, columns, chans), row_block),
            pl.BlockSpec((chans, chans), fixed),
            pl.BlockSpec((chans, chans), fixed),
            pl.BlockSpec((chans, hidden), fixed),
            pl.BlockSpec((hidden, chans), fixed),
        ],
        out_specs=pl.BlockSpec((step_rows, columns, chans), row_block),
        cost_estimate=pl.CostEstimate(
            flops=2 * tile_rows * columns * chans * (3 * chans + 2 * hidden) // 1,
            transcendentals=tile_rows * columns * chans,
            bytes_accessed=tile_rows * columns * chans * 10,
        ),
    )(
        prod_flat,
        pairwise_input,
        outer_update,
        triangle_output_weight,
        gate_weight,
        pairwise_up_weight,
        pairwise_down_weight,
    )


def outer_kernel(lt_ref, r_ref, wt_ref, out_ref, x_ref):
    n_factor = r_ref.shape[0]
    tile_rows = out_ref.shape[0]
    scale = 1.0 / r_ref.shape[1]

    def fill(d, carry):
        vals = jnp.dot(lt_ref[...], r_ref[d], preferred_element_type=jnp.float32)
        vals = (vals * scale).astype(jnp.bfloat16)
        start = pl.multiple_of(d * n_factor, n_factor)
        for i in range(tile_rows):
            x_ref[i, pl.ds(start, n_factor), :] = vals[i * n_factor : (i + 1) * n_factor, :]
        return carry

    lax.fori_loop(0, n_factor, fill, 0)

    def emit(i, carry):
        upd = jnp.dot(wt_ref[...], x_ref[i], preferred_element_type=jnp.float32)
        out_ref[i] = upd.T
        return carry

    lax.fori_loop(0, tile_rows, emit, 0)


def outer_product(left_gathered, right_gathered, outer_output_weight):
    total_rows, tile_rows, channels = left_gathered.shape
    columns = right_gathered.shape[2]
    pair = outer_output_weight.shape[1]
    left_t = jnp.transpose(left_gathered, (1, 2, 0)).reshape(tile_rows * channels, total_rows)
    weight_t = jnp.transpose(
        outer_output_weight.reshape(channels, channels, pair), (1, 0, 2)
    ).reshape(channels * channels, pair).T
    flops = 4 * tile_rows * channels * channels * columns * (total_rows + pair) // 2
    return pl.pallas_call(
        outer_kernel,
        out_shape=jax.ShapeDtypeStruct((tile_rows, columns, pair), jnp.float32),
        in_specs=[pl.BlockSpec(memory_space=pltpu.VMEM)] * 3,
        out_specs=pl.BlockSpec(memory_space=pltpu.VMEM),
        scratch_shapes=[pltpu.VMEM((tile_rows, channels * channels, columns), jnp.bfloat16)],
        compiler_params=pltpu.CompilerParams(vmem_limit_bytes=56 * 1024 * 1024),
        cost_estimate=pl.CostEstimate(
            flops=flops, transcendentals=0, bytes_accessed=right_gathered.size * 2 + tile_rows * columns * pair * 4
        ),
    )(left_t, right_gathered, weight_t)


def on_device(
    homolog_features,
    pairwise_input,
    transition_expand_matrix,
    transition_contract_matrix,
    factor_pair_matrices,
    outer_output_weight,
    triangle_projection_weight,
    triangle_output_weight,
    pairwise_up_weight,
    pairwise_down_weight,
):
    refreshed_homolog_features, left_side, right_side = alignment_branch(
        homolog_features, transition_expand_matrix, transition_contract_matrix, factor_pair_matrices
    )
    left_gathered, right_gathered = gather_sides(left_side, right_side)
    pairwise_input, right_side = lax.optimization_barrier((pairwise_input, right_side))
    tri_stack = pair_front(pairwise_input, triangle_projection_weight)
    moved = send_whole(tri_stack)
    product = triangle_product(moved)
    product, left_gathered = lax.optimization_barrier((product, left_gathered))
    product_tile = send_back(product)
    outer_update = outer_product(left_gathered, right_gathered, outer_output_weight)
    product_tile, outer_update = lax.optimization_barrier((product_tile, outer_update))
    pairwise_output = pair_back(
        pairwise_input,
        product_tile,
        outer_update,
        triangle_projection_weight,
        triangle_output_weight,
        pairwise_up_weight,
        pairwise_down_weight,
    )
    return (refreshed_homolog_features, pairwise_output)


def solution(mesh):
    return jax.shard_map(
        on_device,
        mesh=mesh,
        in_specs=(
            P(("branch", "rows"), None, None),
            P("rows", "branch", None),
            P(),
            P(),
            P(),
            P(),
            P(),
            P(),
            P(),
            P(),
        ),
        out_specs=(P(("branch", "rows"), None, None), P("rows", "branch", None)),
        check_vma=False,
    )
```

```python
import jax
import jax.numpy as jnp
from jax import lax
from jax.experimental import pallas as pl
from jax.experimental.pallas import tpu as pltpu
from jax.sharding import PartitionSpec as P


def standardize_features(values, dimension):
    average = jnp.mean(values, axis=dimension, keepdims=True)
    centered = values - average
    variance = jnp.mean(centered * centered, axis=dimension, keepdims=True)
    return centered * lax.rsqrt(variance + 1e-05)


def alignment_branch(
    homolog_features, transition_expand_matrix, transition_contract_matrix, factor_pair_matrices
):
    local_rows, sequence_length, channel_width = homolog_features.shape
    homolog_real_matrix = homolog_features.astype(jnp.float32)
    standardized_homologs = (
        standardize_features(homolog_real_matrix, -1)
        .astype(jnp.bfloat16)
        .reshape(local_rows * sequence_length, channel_width)
    )
    expanded_activations = jax.nn.relu(
        jnp.dot(standardized_homologs, transition_expand_matrix, preferred_element_type=jnp.float32)
    ).astype(jnp.bfloat16)
    refreshed_homolog_features = (
        homolog_real_matrix
        + jnp.dot(
            expanded_activations, transition_contract_matrix, preferred_element_type=jnp.float32
        ).reshape(homolog_features.shape)
    ).astype(jnp.bfloat16)
    standardized_for_factors = (
        standardize_features(refreshed_homolog_features.astype(jnp.float32), -1)
        .astype(jnp.bfloat16)
        .reshape(local_rows * sequence_length, channel_width)
    )
    projected = jnp.dot(
        standardized_for_factors, factor_pair_matrices, preferred_element_type=jnp.float32
    ).reshape(local_rows, sequence_length, -1)
    channels = projected.shape[-1] // 2
    left_side = projected[..., :channels].astype(jnp.bfloat16)
    right_side = jnp.swapaxes(projected[..., channels:].astype(jnp.bfloat16), 1, 2)
    return (refreshed_homolog_features, left_side, right_side)


def branch_pair(mine, theirs):
    first = lax.axis_index("branch") == 0
    return jnp.where(first, jnp.concatenate([mine, theirs]), jnp.concatenate([theirs, mine]))


def gather_sides(left_side, right_side):
    swap = [(0, 1), (1, 0)]
    left_pair = branch_pair(left_side, lax.ppermute(left_side, "branch", swap))
    left_gathered = lax.all_to_all(left_pair, "rows", split_axis=1, concat_axis=0, tiled=True)
    half = right_side.shape[2] // 2
    me = lax.axis_index("branch")
    keep = lax.dynamic_slice_in_dim(right_side, me * half, half, axis=2)
    send = lax.dynamic_slice_in_dim(right_side, (1 - me) * half, half, axis=2)
    right_pair = branch_pair(keep, lax.ppermute(send, "branch", swap))
    right_gathered = lax.all_gather(jnp.swapaxes(right_pair, 0, 1), "rows", axis=1, tiled=True)
    return left_gathered, right_gathered


def send_whole(tri_stack):
    both = ("branch", "rows")
    moved = lax.all_to_all(tri_stack, both, split_axis=0, concat_axis=0, tiled=True)
    return moved


def send_back(product):
    return lax.all_to_all(product, ("branch", "rows"), split_axis=0, concat_axis=0, tiled=True)


def logistic(values):
    return 0.5 * jnp.tanh(0.5 * values) + 0.5


def front_kernel(pair_ref, w_ref, out_ref, norm_ref):
    tile_rows, columns, chans = pair_ref.shape
    block = out_ref.shape[0]

    @pl.when(pl.program_id(0) == 0)
    def _():
        for r in range(tile_rows):
            norm_ref[r] = standardize_features(pair_ref[r].astype(jnp.float32), -1).astype(
                norm_ref.dtype
            )

    weight = w_ref[...].reshape(4 * block, chans)
    for r in range(tile_rows):
        proj = lax.dot_general(
            weight, norm_ref[r], (((1,), (1,)), ((), ())), preferred_element_type=jnp.float32
        )
        out_ref[:, 0, r, :] = (
            logistic(proj[block : 2 * block]) * proj[:block]
        ).astype(out_ref.dtype)
        out_ref[:, 1, r, :] = (
            logistic(proj[3 * block :]) * proj[2 * block : 3 * block]
        ).astype(out_ref.dtype)


def pair_front(pairwise_input, triangle_projection_weight):
    tile_rows, columns, chans = pairwise_input.shape
    block = 32
    weight = triangle_projection_weight[:, : 4 * chans].T.reshape(4, chans, chans)
    return pl.pallas_call(
        front_kernel,
        out_shape=jax.ShapeDtypeStruct((chans, 2, tile_rows, columns), jnp.bfloat16),
        grid=(chans // block,),
        in_specs=[
            pl.BlockSpec((tile_rows, columns, chans), lambda g: (0, 0, 0)),
            pl.BlockSpec((4, block, chans), lambda g: (0, g, 0)),
        ],
        out_specs=pl.BlockSpec((block, 2, tile_rows, columns), lambda g: (g, 0, 0, 0)),
        scratch_shapes=[pltpu.VMEM((tile_rows, columns, chans), jnp.bfloat16)],
        cost_estimate=pl.CostEstimate(
            flops=2 * tile_rows * columns * chans * 4 * chans,
            transcendentals=2 * tile_rows * columns * chans,
            bytes_accessed=tile_rows * columns * chans * 6,
        ),
    )(pairwise_input, weight)


def product_kernel(moved_ref, out_ref):
    halves, span, columns = out_ref.shape
    n_src, _, tile_rows, _ = moved_ref.shape
    per_half = n_src // halves
    per_out = per_half // halves
    for h in range(halves):
        total = None
        for b in range(halves):
            left = moved_ref[b * per_half : (b + 1) * per_half, 0]
            first = b * per_half + h * per_out
            right = moved_ref[first : first + per_out, 1]
            part = lax.dot_general(
                left.reshape(per_half * tile_rows, columns),
                right.reshape(per_out * tile_rows, columns),
                (((1,), (1,)), ((), ())),
                preferred_element_type=jnp.float32,
            )
            total = part if total is None else total + part
        out_ref[h] = total.astype(out_ref.dtype)


def triangle_product(moved):
    n_src, _, tile_rows, columns = moved.shape
    halves = lax.axis_size("branch")
    product = pl.pallas_call(
        product_kernel,
        out_shape=jax.ShapeDtypeStruct((halves, n_src * tile_rows // halves, columns), jnp.bfloat16),
        in_specs=[pl.BlockSpec(memory_space=pltpu.VMEM)],
        out_specs=pl.BlockSpec(memory_space=pltpu.VMEM),
        cost_estimate=pl.CostEstimate(
            flops=2 * (n_src * tile_rows) ** 2 * columns // halves,
            transcendentals=0,
            bytes_accessed=moved.size * 2 + n_src * tile_rows * columns * 2,
        ),
    )(moved)
    return product.reshape(-1, tile_rows, columns)


def back_kernel(prod_ref, pair_ref, outer_ref, wo_ref, wg_ref, wu_ref, wd_ref, out_ref):
    rows, columns, chans = pair_ref.shape
    for r in range(rows):
        prod = prod_ref[:, r * columns : (r + 1) * columns].astype(jnp.float32)
        prod_norm = standardize_features(prod, 0).T.astype(jnp.bfloat16)
        tri_update = jnp.dot(prod_norm, wo_ref[...], preferred_element_type=jnp.float32)
        pair_float = pair_ref[r].astype(jnp.float32)
        pair_norm = standardize_features(pair_float, -1).astype(jnp.bfloat16)
        gate = logistic(
            jnp.dot(pair_norm, wg_ref[...], preferred_element_type=jnp.float32)
        )
        pair_mid = pair_float + gate * tri_update
        mid_norm = standardize_features(pair_mid, -1).astype(jnp.bfloat16)
        hidden = jnp.maximum(
            jnp.dot(mid_norm, wu_ref[...], preferred_element_type=jnp.float32), 0.0
        ).astype(jnp.bfloat16)
        down = jnp.dot(hidden, wd_ref[...], preferred_element_type=jnp.float32)
        out_ref[r] = (pair_mid + down + outer_ref[r]).astype(out_ref.dtype)


def pair_back(
    pairwise_input,
    product_tile,
    outer_update,
    triangle_projection_weight,
    triangle_output_weight,
    pairwise_up_weight,
    pairwise_down_weight,
):
    tile_rows, columns, chans = pairwise_input.shape
    step_rows = 4
    prod_flat = product_tile.reshape(chans, tile_rows * columns)
    gate_weight = triangle_projection_weight
    hidden = pairwise_up_weight.shape[1]
    row_block = lambda g: (g, 0, 0)
    fixed = lambda g: (0, 0)
    return pl.pallas_call(
        back_kernel,
        out_shape=jax.ShapeDtypeStruct((tile_rows, columns, chans), jnp.bfloat16),
        grid=(tile_rows // step_rows,),
        in_specs=[
            pl.BlockSpec((chans, step_rows * columns), lambda g: (0, g)),
            pl.BlockSpec((step_rows, columns, chans), row_block),
            pl.BlockSpec((step_rows, columns, chans), row_block),
            pl.BlockSpec((chans, chans), fixed),
            pl.BlockSpec((chans, chans), fixed),
            pl.BlockSpec((chans, hidden), fixed),
            pl.BlockSpec((hidden, chans), fixed),
        ],
        out_specs=pl.BlockSpec((step_rows, columns, chans), row_block),
        cost_estimate=pl.CostEstimate(
            flops=2 * tile_rows * columns * chans * (3 * chans + 2 * hidden) // 1,
            transcendentals=tile_rows * columns * chans,
            bytes_accessed=tile_rows * columns * chans * 10,
        ),
    )(
        prod_flat,
        pairwise_input,
        outer_update,
        triangle_output_weight,
        gate_weight,
        pairwise_up_weight,
        pairwise_down_weight,
    )


def outer_kernel(lt_ref, r_ref, wt_ref, out_ref, x_ref):
    n_factor = r_ref.shape[0]
    tile_rows = out_ref.shape[0]
    scale = 1.0 / r_ref.shape[1]

    def fill(d, carry):
        vals = jnp.dot(lt_ref[...], r_ref[d], preferred_element_type=jnp.float32)
        vals = (vals * scale).astype(jnp.bfloat16)
        start = pl.multiple_of(d * n_factor, n_factor)
        for i in range(tile_rows):
            x_ref[i, pl.ds(start, n_factor), :] = vals[i * n_factor : (i + 1) * n_factor, :]
        return carry

    lax.fori_loop(0, n_factor, fill, 0)

    def emit(i, carry):
        upd = jnp.dot(wt_ref[...], x_ref[i], preferred_element_type=jnp.float32)
        out_ref[i] = upd.T
        return carry

    lax.fori_loop(0, tile_rows, emit, 0)


def outer_operands(left_gathered, outer_output_weight):
    total_rows, tile_rows, channels = left_gathered.shape
    pair = outer_output_weight.shape[1]
    left_t = jnp.transpose(left_gathered, (1, 2, 0)).reshape(tile_rows * channels, total_rows)
    weight_t = jnp.transpose(
        outer_output_weight.reshape(channels, channels, pair), (1, 0, 2)
    ).reshape(channels * channels, pair).T
    return left_t, weight_t


def outer_product(left_t, right_gathered, weight_t, tile_rows):
    channels = left_t.shape[0] // tile_rows
    total_rows = left_t.shape[1]
    columns = right_gathered.shape[2]
    pair = weight_t.shape[0]
    flops = 4 * tile_rows * channels * channels * columns * (total_rows + pair) // 2
    return pl.pallas_call(
        outer_kernel,
        out_shape=jax.ShapeDtypeStruct((tile_rows, columns, pair), jnp.float32),
        in_specs=[pl.BlockSpec(memory_space=pltpu.VMEM)] * 3,
        out_specs=pl.BlockSpec(memory_space=pltpu.VMEM),
        scratch_shapes=[pltpu.VMEM((tile_rows, channels * channels, columns), jnp.bfloat16)],
        compiler_params=pltpu.CompilerParams(vmem_limit_bytes=56 * 1024 * 1024),
        cost_estimate=pl.CostEstimate(
            flops=flops, transcendentals=0, bytes_accessed=right_gathered.size * 2 + tile_rows * columns * pair * 4
        ),
    )(left_t, right_gathered, weight_t)


def on_device(
    homolog_features,
    pairwise_input,
    transition_expand_matrix,
    transition_contract_matrix,
    factor_pair_matrices,
    outer_output_weight,
    triangle_projection_weight,
    triangle_output_weight,
    pairwise_up_weight,
    pairwise_down_weight,
):
    refreshed_homolog_features, left_side, right_side = alignment_branch(
        homolog_features, transition_expand_matrix, transition_contract_matrix, factor_pair_matrices
    )
    left_gathered, right_gathered = gather_sides(left_side, right_side)
    pairwise_input, right_side = lax.optimization_barrier((pairwise_input, right_side))
    tri_stack = pair_front(pairwise_input, triangle_projection_weight)
    moved = send_whole(tri_stack)
    product = triangle_product(moved)
    left_t, weight_t = outer_operands(left_gathered, outer_output_weight)
    gate_weight = triangle_projection_weight[:, 4 * pairwise_input.shape[2] :]
    product, left_t, weight_t, gate_weight = lax.optimization_barrier(
        (product, left_t, weight_t, gate_weight)
    )
    product_tile = send_back(product)
    outer_update = outer_product(left_t, right_gathered, weight_t, pairwise_input.shape[0])
    product_tile, outer_update = lax.optimization_barrier((product_tile, outer_update))
    pairwise_output = pair_back(
        pairwise_input,
        product_tile,
        outer_update,
        gate_weight,
        triangle_output_weight,
        pairwise_up_weight,
        pairwise_down_weight,
    )
    return (refreshed_homolog_features, pairwise_output)


def solution(mesh):
    return jax.shard_map(
        on_device,
        mesh=mesh,
        in_specs=(
            P(("branch", "rows"), None, None),
            P("rows", "branch", None),
            P(),
            P(),
            P(),
            P(),
            P(),
            P(),
            P(),
            P(),
        ),
        out_specs=(P(("branch", "rows"), None, None), P("rows", "branch", None)),
        check_vma=False,
    )
```

```python
import jax
import jax.numpy as jnp
from jax import lax
from jax.experimental import pallas as pl
from jax.experimental.pallas import tpu as pltpu
from jax.sharding import PartitionSpec as P


def standardize_features(values, dimension):
    average = jnp.mean(values, axis=dimension, keepdims=True)
    centered = values - average
    variance = jnp.mean(centered * centered, axis=dimension, keepdims=True)
    return centered * lax.rsqrt(variance + 1e-05)


def alignment_branch(
    homolog_features, transition_expand_matrix, transition_contract_matrix, factor_pair_matrices
):
    local_rows, sequence_length, channel_width = homolog_features.shape
    homolog_real_matrix = homolog_features.astype(jnp.float32)
    standardized_homologs = (
        standardize_features(homolog_real_matrix, -1)
        .astype(jnp.bfloat16)
        .reshape(local_rows * sequence_length, channel_width)
    )
    expanded_activations = jax.nn.relu(
        jnp.dot(standardized_homologs, transition_expand_matrix, preferred_element_type=jnp.float32)
    ).astype(jnp.bfloat16)
    refreshed_homolog_features = (
        homolog_real_matrix
        + jnp.dot(
            expanded_activations, transition_contract_matrix, preferred_element_type=jnp.float32
        ).reshape(homolog_features.shape)
    ).astype(jnp.bfloat16)
    standardized_for_factors = (
        standardize_features(refreshed_homolog_features.astype(jnp.float32), -1)
        .astype(jnp.bfloat16)
        .reshape(local_rows * sequence_length, channel_width)
    )
    projected = jnp.dot(
        standardized_for_factors, factor_pair_matrices, preferred_element_type=jnp.float32
    ).reshape(local_rows, sequence_length, -1)
    channels = projected.shape[-1] // 2
    left_side = projected[..., :channels].astype(jnp.bfloat16)
    right_side = jnp.swapaxes(projected[..., channels:].astype(jnp.bfloat16), 1, 2)
    return (refreshed_homolog_features, left_side, right_side)


def branch_pair(mine, theirs):
    first = lax.axis_index("branch") == 0
    return jnp.where(first, jnp.concatenate([mine, theirs]), jnp.concatenate([theirs, mine]))


def gather_sides(left_side, right_side):
    swap = [(0, 1), (1, 0)]
    halves = lax.axis_size("branch")
    n_rows = lax.axis_size("rows")
    left_dest = jnp.tile(left_side.reshape(n_rows, -1, left_side.shape[-1]), (halves, 1, 1))
    left_src = lax.all_to_all(left_dest, ("branch", "rows"), split_axis=0, concat_axis=0, tiled=True)
    left_gathered = jnp.swapaxes(
        left_src.reshape(halves, n_rows, -1, left_side.shape[-1]), 0, 1
    ).reshape(halves * n_rows, -1, left_side.shape[-1])
    half = right_side.shape[2] // 2
    me = lax.axis_index("branch")
    keep = lax.dynamic_slice_in_dim(right_side, me * half, half, axis=2)
    send = lax.dynamic_slice_in_dim(right_side, (1 - me) * half, half, axis=2)
    right_pair = branch_pair(keep, lax.ppermute(send, "branch", swap))
    right_gathered = lax.all_gather(jnp.swapaxes(right_pair, 0, 1), "rows", axis=1, tiled=True)
    return left_gathered, right_gathered


def send_whole(tri_stack):
    both = ("branch", "rows")
    moved = lax.all_to_all(tri_stack, both, split_axis=0, concat_axis=0, tiled=True)
    return moved


def send_back(product):
    return lax.all_to_all(product, ("branch", "rows"), split_axis=0, concat_axis=0, tiled=True)


def logistic(values):
    return 0.5 * jnp.tanh(0.5 * values) + 0.5


def front_kernel(pair_ref, w_ref, out_ref, norm_ref):
    tile_rows, columns, chans = pair_ref.shape
    block = out_ref.shape[0]

    @pl.when(pl.program_id(0) == 0)
    def _():
        for r in range(tile_rows):
            norm_ref[r] = standardize_features(pair_ref[r].astype(jnp.float32), -1).astype(
                norm_ref.dtype
            )

    weight = w_ref[...].reshape(4 * block, chans)
    for r in range(tile_rows):
        proj = lax.dot_general(
            weight, norm_ref[r], (((1,), (1,)), ((), ())), preferred_element_type=jnp.float32
        )
        out_ref[:, 0, r, :] = (
            logistic(proj[block : 2 * block]) * proj[:block]
        ).astype(out_ref.dtype)
        out_ref[:, 1, r, :] = (
            logistic(proj[3 * block :]) * proj[2 * block : 3 * block]
        ).astype(out_ref.dtype)


def pair_front(pairwise_input, triangle_projection_weight):
    tile_rows, columns, chans = pairwise_input.shape
    block = 32
    weight = triangle_projection_weight[:, : 4 * chans].T.reshape(4, chans, chans)
    return pl.pallas_call(
        front_kernel,
        out_shape=jax.ShapeDtypeStruct((chans, 2, tile_rows, columns), jnp.bfloat16),
        grid=(chans // block,),
        in_specs=[
            pl.BlockSpec((tile_rows, columns, chans), lambda g: (0, 0, 0)),
            pl.BlockSpec((4, block, chans), lambda g: (0, g, 0)),
        ],
        out_specs=pl.BlockSpec((block, 2, tile_rows, columns), lambda g: (g, 0, 0, 0)),
        scratch_shapes=[pltpu.VMEM((tile_rows, columns, chans), jnp.bfloat16)],
        cost_estimate=pl.CostEstimate(
            flops=2 * tile_rows * columns * chans * 4 * chans,
            transcendentals=2 * tile_rows * columns * chans,
            bytes_accessed=tile_rows * columns * chans * 6,
        ),
    )(pairwise_input, weight)


def product_kernel(moved_ref, out_ref):
    halves, span, columns = out_ref.shape
    n_src, _, tile_rows, _ = moved_ref.shape
    per_half = n_src // halves
    per_out = per_half // halves
    for h in range(halves):
        total = None
        for b in range(halves):
            left = moved_ref[b * per_half : (b + 1) * per_half, 0]
            first = b * per_half + h * per_out
            right = moved_ref[first : first + per_out, 1]
            part = lax.dot_general(
                left.reshape(per_half * tile_rows, columns),
                right.reshape(per_out * tile_rows, columns),
                (((1,), (1,)), ((), ())),
                preferred_element_type=jnp.float32,
            )
            total = part if total is None else total + part
        out_ref[h] = total.astype(out_ref.dtype)


def triangle_product(moved):
    n_src, _, tile_rows, columns = moved.shape
    halves = lax.axis_size("branch")
    product = pl.pallas_call(
        product_kernel,
        out_shape=jax.ShapeDtypeStruct((halves, n_src * tile_rows // halves, columns), jnp.bfloat16),
        in_specs=[pl.BlockSpec(memory_space=pltpu.VMEM)],
        out_specs=pl.BlockSpec(memory_space=pltpu.VMEM),
        cost_estimate=pl.CostEstimate(
            flops=2 * (n_src * tile_rows) ** 2 * columns // halves,
            transcendentals=0,
            bytes_accessed=moved.size * 2 + n_src * tile_rows * columns * 2,
        ),
    )(moved)
    return product.reshape(-1, tile_rows, columns)


def back_kernel(prod_ref, pair_ref, outer_ref, wo_ref, wg_ref, wu_ref, wd_ref, out_ref):
    rows, columns, chans = pair_ref.shape
    for r in range(rows):
        prod = prod_ref[:, r * columns : (r + 1) * columns].astype(jnp.float32)
        prod_norm = standardize_features(prod, 0).T.astype(jnp.bfloat16)
        tri_update = jnp.dot(prod_norm, wo_ref[...], preferred_element_type=jnp.float32)
        pair_float = pair_ref[r].astype(jnp.float32)
        pair_norm = standardize_features(pair_float, -1).astype(jnp.bfloat16)
        gate = logistic(
            jnp.dot(pair_norm, wg_ref[...], preferred_element_type=jnp.float32)
        )
        pair_mid = pair_float + gate * tri_update
        mid_norm = standardize_features(pair_mid, -1).astype(jnp.bfloat16)
        hidden = jnp.maximum(
            jnp.dot(mid_norm, wu_ref[...], preferred_element_type=jnp.float32), 0.0
        ).astype(jnp.bfloat16)
        down = jnp.dot(hidden, wd_ref[...], preferred_element_type=jnp.float32)
        out_ref[r] = (pair_mid + down + outer_ref[r]).astype(out_ref.dtype)


def pair_back(
    pairwise_input,
    product_tile,
    outer_update,
    triangle_projection_weight,
    triangle_output_weight,
    pairwise_up_weight,
    pairwise_down_weight,
):
    tile_rows, columns, chans = pairwise_input.shape
    step_rows = 4
    prod_flat = product_tile.reshape(chans, tile_rows * columns)
    gate_weight = triangle_projection_weight
    hidden = pairwise_up_weight.shape[1]
    row_block = lambda g: (g, 0, 0)
    fixed = lambda g: (0, 0)
    return pl.pallas_call(
        back_kernel,
        out_shape=jax.ShapeDtypeStruct((tile_rows, columns, chans), jnp.bfloat16),
        grid=(tile_rows // step_rows,),
        in_specs=[
            pl.BlockSpec((chans, step_rows * columns), lambda g: (0, g)),
            pl.BlockSpec((step_rows, columns, chans), row_block),
            pl.BlockSpec((step_rows, columns, chans), row_block),
            pl.BlockSpec((chans, chans), fixed),
            pl.BlockSpec((chans, chans), fixed),
            pl.BlockSpec((chans, hidden), fixed),
            pl.BlockSpec((hidden, chans), fixed),
        ],
        out_specs=pl.BlockSpec((step_rows, columns, chans), row_block),
        cost_estimate=pl.CostEstimate(
            flops=2 * tile_rows * columns * chans * (3 * chans + 2 * hidden) // 1,
            transcendentals=tile_rows * columns * chans,
            bytes_accessed=tile_rows * columns * chans * 10,
        ),
    )(
        prod_flat,
        pairwise_input,
        outer_update,
        triangle_output_weight,
        gate_weight,
        pairwise_up_weight,
        pairwise_down_weight,
    )


def outer_kernel(lt_ref, r_ref, wt_ref, out_ref, x_ref):
    n_factor = r_ref.shape[0]
    tile_rows = out_ref.shape[0]
    scale = 1.0 / r_ref.shape[1]

    def fill(d, carry):
        vals = jnp.dot(lt_ref[...], r_ref[d], preferred_element_type=jnp.float32)
        vals = (vals * scale).astype(jnp.bfloat16)
        start = pl.multiple_of(d * n_factor, n_factor)
        for i in range(tile_rows):
            x_ref[i, pl.ds(start, n_factor), :] = vals[i * n_factor : (i + 1) * n_factor, :]
        return carry

    lax.fori_loop(0, n_factor, fill, 0)

    def emit(i, carry):
        upd = jnp.dot(wt_ref[...], x_ref[i], preferred_element_type=jnp.float32)
        out_ref[i] = upd.T
        return carry

    lax.fori_loop(0, tile_rows, emit, 0)


def outer_operands(left_gathered, outer_output_weight):
    total_rows, tile_rows, channels = left_gathered.shape
    pair = outer_output_weight.shape[1]
    left_t = jnp.transpose(left_gathered, (1, 2, 0)).reshape(tile_rows * channels, total_rows)
    weight_t = jnp.transpose(
        outer_output_weight.reshape(channels, channels, pair), (1, 0, 2)
    ).reshape(channels * channels, pair).T
    return left_t, weight_t


def outer_product(left_t, right_gathered, weight_t, tile_rows):
    channels = left_t.shape[0] // tile_rows
    total_rows = left_t.shape[1]
    columns = right_gathered.shape[2]
    pair = weight_t.shape[0]
    flops = 4 * tile_rows * channels * channels * columns * (total_rows + pair) // 2
    return pl.pallas_call(
        outer_kernel,
        out_shape=jax.ShapeDtypeStruct((tile_rows, columns, pair), jnp.float32),
        in_specs=[pl.BlockSpec(memory_space=pltpu.VMEM)] * 3,
        out_specs=pl.BlockSpec(memory_space=pltpu.VMEM),
        scratch_shapes=[pltpu.VMEM((tile_rows, channels * channels, columns), jnp.bfloat16)],
        compiler_params=pltpu.CompilerParams(vmem_limit_bytes=56 * 1024 * 1024),
        cost_estimate=pl.CostEstimate(
            flops=flops, transcendentals=0, bytes_accessed=right_gathered.size * 2 + tile_rows * columns * pair * 4
        ),
    )(left_t, right_gathered, weight_t)


def on_device(
    homolog_features,
    pairwise_input,
    transition_expand_matrix,
    transition_contract_matrix,
    factor_pair_matrices,
    outer_output_weight,
    triangle_projection_weight,
    triangle_output_weight,
    pairwise_up_weight,
    pairwise_down_weight,
):
    refreshed_homolog_features, left_side, right_side = alignment_branch(
        homolog_features, transition_expand_matrix, transition_contract_matrix, factor_pair_matrices
    )
    left_gathered, right_gathered = gather_sides(left_side, right_side)
    pairwise_input, right_side = lax.optimization_barrier((pairwise_input, right_side))
    tri_stack = pair_front(pairwise_input, triangle_projection_weight)
    moved = send_whole(tri_stack)
    product = triangle_product(moved)
    left_t, weight_t = outer_operands(left_gathered, outer_output_weight)
    gate_weight = triangle_projection_weight[:, 4 * pairwise_input.shape[2] :]
    product, left_t, weight_t, gate_weight = lax.optimization_barrier(
        (product, left_t, weight_t, gate_weight)
    )
    product_tile = send_back(product)
    outer_update = outer_product(left_t, right_gathered, weight_t, pairwise_input.shape[0])
    product_tile, outer_update = lax.optimization_barrier((product_tile, outer_update))
    pairwise_output = pair_back(
        pairwise_input,
        product_tile,
        outer_update,
        gate_weight,
        triangle_output_weight,
        pairwise_up_weight,
        pairwise_down_weight,
    )
    return (refreshed_homolog_features, pairwise_output)


def solution(mesh):
    return jax.shard_map(
        on_device,
        mesh=mesh,
        in_specs=(
            P(("branch", "rows"), None, None),
            P("rows", "branch", None),
            P(),
            P(),
            P(),
            P(),
            P(),
            P(),
            P(),
            P(),
        ),
        out_specs=(P(("branch", "rows"), None, None), P("rows", "branch", None)),
        check_vma=False,
    )
```

```python
import jax
import jax.numpy as jnp
from jax import lax
from jax.experimental import pallas as pl
from jax.experimental.pallas import tpu as pltpu
from jax.sharding import PartitionSpec as P


def standardize_features(values, dimension):
    average = jnp.mean(values, axis=dimension, keepdims=True)
    centered = values - average
    variance = jnp.mean(centered * centered, axis=dimension, keepdims=True)
    return centered * lax.rsqrt(variance + 1e-05)


def alignment_branch(
    homolog_features, transition_expand_matrix, transition_contract_matrix, factor_pair_matrices
):
    local_rows, sequence_length, channel_width = homolog_features.shape
    homolog_real_matrix = homolog_features.astype(jnp.float32)
    standardized_homologs = (
        standardize_features(homolog_real_matrix, -1)
        .astype(jnp.bfloat16)
        .reshape(local_rows * sequence_length, channel_width)
    )
    expanded_activations = jax.nn.relu(
        jnp.dot(standardized_homologs, transition_expand_matrix, preferred_element_type=jnp.float32)
    ).astype(jnp.bfloat16)
    refreshed_homolog_features = (
        homolog_real_matrix
        + jnp.dot(
            expanded_activations, transition_contract_matrix, preferred_element_type=jnp.float32
        ).reshape(homolog_features.shape)
    ).astype(jnp.bfloat16)
    standardized_for_factors = (
        standardize_features(refreshed_homolog_features.astype(jnp.float32), -1)
        .astype(jnp.bfloat16)
        .reshape(local_rows * sequence_length, channel_width)
    )
    projected = jnp.dot(
        standardized_for_factors, factor_pair_matrices, preferred_element_type=jnp.float32
    ).reshape(local_rows, sequence_length, -1)
    channels = projected.shape[-1] // 2
    left_side = projected[..., :channels].astype(jnp.bfloat16)
    right_side = jnp.swapaxes(projected[..., channels:].astype(jnp.bfloat16), 1, 2)
    return (refreshed_homolog_features, left_side, right_side)


def branch_pair(mine, theirs):
    first = lax.axis_index("branch") == 0
    return jnp.where(first, jnp.concatenate([mine, theirs]), jnp.concatenate([theirs, mine]))


def gather_sides(left_side, right_side):
    swap = [(0, 1), (1, 0)]
    left_pair = branch_pair(left_side, lax.ppermute(left_side, "branch", swap))
    left_gathered = lax.all_to_all(left_pair, "rows", split_axis=1, concat_axis=0, tiled=True)
    half = right_side.shape[2] // 2
    me = lax.axis_index("branch")
    keep = lax.dynamic_slice_in_dim(right_side, me * half, half, axis=2)
    send = lax.dynamic_slice_in_dim(right_side, (1 - me) * half, half, axis=2)
    right_pair = branch_pair(keep, lax.ppermute(send, "branch", swap))
    right_gathered = lax.all_gather(jnp.swapaxes(right_pair, 0, 1), "rows", axis=1, tiled=True)
    return left_gathered, right_gathered


def send_whole(tri_stack):
    both = ("branch", "rows")
    moved = lax.all_to_all(tri_stack, both, split_axis=0, concat_axis=0, tiled=True)
    return moved


def send_back(product):
    return lax.all_to_all(product, ("branch", "rows"), split_axis=0, concat_axis=0, tiled=True)


def logistic(values):
    return 0.5 * jnp.tanh(0.5 * values) + 0.5


def front_kernel(pair_ref, w_ref, out_ref, norm_ref):
    tile_rows, columns, chans = pair_ref.shape
    block = out_ref.shape[0]

    @pl.when(pl.program_id(0) == 0)
    def _():
        for r in range(tile_rows):
            norm_ref[r] = standardize_features(pair_ref[r].astype(jnp.float32), -1).astype(
                norm_ref.dtype
            )

    weight = w_ref[...].reshape(4 * block, chans)
    for r in range(tile_rows):
        proj = lax.dot_general(
            weight, norm_ref[r], (((1,), (1,)), ((), ())), preferred_element_type=jnp.float32
        )
        out_ref[:, 0, r, :] = (
            logistic(proj[block : 2 * block]) * proj[:block]
        ).astype(out_ref.dtype)
        out_ref[:, 1, r, :] = (
            logistic(proj[3 * block :]) * proj[2 * block : 3 * block]
        ).astype(out_ref.dtype)


def pair_front(pairwise_input, triangle_projection_weight):
    tile_rows, columns, chans = pairwise_input.shape
    block = 32
    weight = triangle_projection_weight[:, : 4 * chans].T.reshape(4, chans, chans)
    return pl.pallas_call(
        front_kernel,
        out_shape=jax.ShapeDtypeStruct((chans, 2, tile_rows, columns), jnp.bfloat16),
        grid=(chans // block,),
        in_specs=[
            pl.BlockSpec((tile_rows, columns, chans), lambda g: (0, 0, 0)),
            pl.BlockSpec((4, block, chans), lambda g: (0, g, 0)),
        ],
        out_specs=pl.BlockSpec((block, 2, tile_rows, columns), lambda g: (g, 0, 0, 0)),
        scratch_shapes=[pltpu.VMEM((tile_rows, columns, chans), jnp.bfloat16)],
        cost_estimate=pl.CostEstimate(
            flops=2 * tile_rows * columns * chans * 4 * chans,
            transcendentals=2 * tile_rows * columns * chans,
            bytes_accessed=tile_rows * columns * chans * 6,
        ),
    )(pairwise_input, weight)


def product_kernel(moved_ref, out_ref):
    halves, span, columns = out_ref.shape
    n_src, _, tile_rows, _ = moved_ref.shape
    per_half = n_src // halves
    per_out = per_half // halves
    for h in range(halves):
        total = None
        for b in range(halves):
            left = moved_ref[b * per_half : (b + 1) * per_half, 0]
            first = b * per_half + h * per_out
            right = moved_ref[first : first + per_out, 1]
            part = lax.dot_general(
                left.reshape(per_half * tile_rows, columns),
                right.reshape(per_out * tile_rows, columns),
                (((1,), (1,)), ((), ())),
                preferred_element_type=jnp.float32,
            )
            total = part if total is None else total + part
        out_ref[h] = total.astype(out_ref.dtype)


def triangle_product(moved):
    n_src, _, tile_rows, columns = moved.shape
    halves = lax.axis_size("branch")
    product = pl.pallas_call(
        product_kernel,
        out_shape=jax.ShapeDtypeStruct((halves, n_src * tile_rows // halves, columns), jnp.bfloat16),
        in_specs=[pl.BlockSpec(memory_space=pltpu.VMEM)],
        out_specs=pl.BlockSpec(memory_space=pltpu.VMEM),
        cost_estimate=pl.CostEstimate(
            flops=2 * (n_src * tile_rows) ** 2 * columns // halves,
            transcendentals=0,
            bytes_accessed=moved.size * 2 + n_src * tile_rows * columns * 2,
        ),
    )(moved)
    return product.reshape(-1, tile_rows, columns)


def back_kernel(prod_ref, pair_ref, outer_ref, wo_ref, wg_ref, wu_ref, wd_ref, out_ref):
    rows, columns, chans = pair_ref.shape
    for r in range(rows):
        prod = prod_ref[:, r * columns : (r + 1) * columns].astype(jnp.float32)
        prod_norm = standardize_features(prod, 0).T.astype(jnp.bfloat16)
        tri_update = jnp.dot(prod_norm, wo_ref[...], preferred_element_type=jnp.float32)
        pair_float = pair_ref[r].astype(jnp.float32)
        pair_norm = standardize_features(pair_float, -1).astype(jnp.bfloat16)
        gate = logistic(
            jnp.dot(pair_norm, wg_ref[...], preferred_element_type=jnp.float32)
        )
        pair_mid = pair_float + gate * tri_update
        mid_norm = standardize_features(pair_mid, -1).astype(jnp.bfloat16)
        hidden = jnp.maximum(
            jnp.dot(mid_norm, wu_ref[...], preferred_element_type=jnp.float32), 0.0
        ).astype(jnp.bfloat16)
        down = jnp.dot(hidden, wd_ref[...], preferred_element_type=jnp.float32)
        out_ref[r] = (pair_mid + down + outer_ref[r]).astype(out_ref.dtype)


def pair_back(
    pairwise_input,
    product_tile,
    outer_update,
    triangle_projection_weight,
    triangle_output_weight,
    pairwise_up_weight,
    pairwise_down_weight,
):
    tile_rows, columns, chans = pairwise_input.shape
    step_rows = 8
    prod_flat = product_tile.reshape(chans, tile_rows * columns)
    gate_weight = triangle_projection_weight
    hidden = pairwise_up_weight.shape[1]
    row_block = lambda g: (g, 0, 0)
    fixed = lambda g: (0, 0)
    return pl.pallas_call(
        back_kernel,
        out_shape=jax.ShapeDtypeStruct((tile_rows, columns, chans), jnp.bfloat16),
        grid=(tile_rows // step_rows,),
        in_specs=[
            pl.BlockSpec((chans, step_rows * columns), lambda g: (0, g)),
            pl.BlockSpec((step_rows, columns, chans), row_block),
            pl.BlockSpec((step_rows, columns, chans), row_block),
            pl.BlockSpec((chans, chans), fixed),
            pl.BlockSpec((chans, chans), fixed),
            pl.BlockSpec((chans, hidden), fixed),
            pl.BlockSpec((hidden, chans), fixed),
        ],
        out_specs=pl.BlockSpec((step_rows, columns, chans), row_block),
        cost_estimate=pl.CostEstimate(
            flops=2 * tile_rows * columns * chans * (3 * chans + 2 * hidden) // 1,
            transcendentals=tile_rows * columns * chans,
            bytes_accessed=tile_rows * columns * chans * 10,
        ),
    )(
        prod_flat,
        pairwise_input,
        outer_update,
        triangle_output_weight,
        gate_weight,
        pairwise_up_weight,
        pairwise_down_weight,
    )


def outer_kernel(lt_ref, r_ref, wt_ref, out_ref, x_ref):
    n_factor = r_ref.shape[0]
    tile_rows = out_ref.shape[0]
    scale = 1.0 / r_ref.shape[1]

    def fill(d, carry):
        vals = jnp.dot(lt_ref[...], r_ref[d], preferred_element_type=jnp.float32)
        vals = (vals * scale).astype(jnp.bfloat16)
        start = pl.multiple_of(d * n_factor, n_factor)
        for i in range(tile_rows):
            x_ref[i, pl.ds(start, n_factor), :] = vals[i * n_factor : (i + 1) * n_factor, :]
        return carry

    lax.fori_loop(0, n_factor, fill, 0)

    def emit(i, carry):
        upd = jnp.dot(wt_ref[...], x_ref[i], preferred_element_type=jnp.float32)
        out_ref[i] = upd.T
        return carry

    lax.fori_loop(0, tile_rows, emit, 0)


def outer_operands(left_gathered, outer_output_weight):
    total_rows, tile_rows, channels = left_gathered.shape
    pair = outer_output_weight.shape[1]
    left_t = jnp.transpose(left_gathered, (1, 2, 0)).reshape(tile_rows * channels, total_rows)
    weight_t = jnp.transpose(
        outer_output_weight.reshape(channels, channels, pair), (1, 0, 2)
    ).reshape(channels * channels, pair).T
    return left_t, weight_t


def outer_product(left_t, right_gathered, weight_t, tile_rows):
    channels = left_t.shape[0] // tile_rows
    total_rows = left_t.shape[1]
    columns = right_gathered.shape[2]
    pair = weight_t.shape[0]
    flops = 4 * tile_rows * channels * channels * columns * (total_rows + pair) // 2
    return pl.pallas_call(
        outer_kernel,
        out_shape=jax.ShapeDtypeStruct((tile_rows, columns, pair), jnp.float32),
        in_specs=[pl.BlockSpec(memory_space=pltpu.VMEM)] * 3,
        out_specs=pl.BlockSpec(memory_space=pltpu.VMEM),
        scratch_shapes=[pltpu.VMEM((tile_rows, channels * channels, columns), jnp.bfloat16)],
        compiler_params=pltpu.CompilerParams(vmem_limit_bytes=56 * 1024 * 1024),
        cost_estimate=pl.CostEstimate(
            flops=flops, transcendentals=0, bytes_accessed=right_gathered.size * 2 + tile_rows * columns * pair * 4
        ),
    )(left_t, right_gathered, weight_t)


def on_device(
    homolog_features,
    pairwise_input,
    transition_expand_matrix,
    transition_contract_matrix,
    factor_pair_matrices,
    outer_output_weight,
    triangle_projection_weight,
    triangle_output_weight,
    pairwise_up_weight,
    pairwise_down_weight,
):
    refreshed_homolog_features, left_side, right_side = alignment_branch(
        homolog_features, transition_expand_matrix, transition_contract_matrix, factor_pair_matrices
    )
    left_gathered, right_gathered = gather_sides(left_side, right_side)
    pairwise_input, right_side = lax.optimization_barrier((pairwise_input, right_side))
    tri_stack = pair_front(pairwise_input, triangle_projection_weight)
    moved = send_whole(tri_stack)
    product = triangle_product(moved)
    left_t, weight_t = outer_operands(left_gathered, outer_output_weight)
    gate_weight = triangle_projection_weight[:, 4 * pairwise_input.shape[2] :]
    product, left_t, weight_t, gate_weight = lax.optimization_barrier(
        (product, left_t, weight_t, gate_weight)
    )
    product_tile = send_back(product)
    outer_update = outer_product(left_t, right_gathered, weight_t, pairwise_input.shape[0])
    product_tile, outer_update = lax.optimization_barrier((product_tile, outer_update))
    pairwise_output = pair_back(
        pairwise_input,
        product_tile,
        outer_update,
        gate_weight,
        triangle_output_weight,
        pairwise_up_weight,
        pairwise_down_weight,
    )
    return (refreshed_homolog_features, pairwise_output)


def solution(mesh):
    return jax.shard_map(
        on_device,
        mesh=mesh,
        in_specs=(
            P(("branch", "rows"), None, None),
            P("rows", "branch", None),
            P(),
            P(),
            P(),
            P(),
            P(),
            P(),
            P(),
            P(),
        ),
        out_specs=(P(("branch", "rows"), None, None), P("rows", "branch", None)),
        check_vma=False,
    )
```

```python
import jax
import jax.numpy as jnp
from jax import lax
from jax.experimental import pallas as pl
from jax.experimental.pallas import tpu as pltpu
from jax.sharding import PartitionSpec as P


def standardize_features(values, dimension):
    average = jnp.mean(values, axis=dimension, keepdims=True)
    centered = values - average
    variance = jnp.mean(centered * centered, axis=dimension, keepdims=True)
    return centered * lax.rsqrt(variance + 1e-05)


def alignment_branch(
    homolog_features, transition_expand_matrix, transition_contract_matrix, factor_pair_matrices
):
    local_rows, sequence_length, channel_width = homolog_features.shape
    homolog_real_matrix = homolog_features.astype(jnp.float32)
    standardized_homologs = (
        standardize_features(homolog_real_matrix, -1)
        .astype(jnp.bfloat16)
        .reshape(local_rows * sequence_length, channel_width)
    )
    expanded_activations = jax.nn.relu(
        jnp.dot(standardized_homologs, transition_expand_matrix, preferred_element_type=jnp.float32)
    ).astype(jnp.bfloat16)
    refreshed_homolog_features = (
        homolog_real_matrix
        + jnp.dot(
            expanded_activations, transition_contract_matrix, preferred_element_type=jnp.float32
        ).reshape(homolog_features.shape)
    ).astype(jnp.bfloat16)
    standardized_for_factors = (
        standardize_features(refreshed_homolog_features.astype(jnp.float32), -1)
        .astype(jnp.bfloat16)
        .reshape(local_rows * sequence_length, channel_width)
    )
    projected = jnp.dot(
        standardized_for_factors, factor_pair_matrices, preferred_element_type=jnp.float32
    ).reshape(local_rows, sequence_length, -1)
    channels = projected.shape[-1] // 2
    left_side = projected[..., :channels].astype(jnp.bfloat16)
    right_side = jnp.swapaxes(projected[..., channels:].astype(jnp.bfloat16), 1, 2)
    return (refreshed_homolog_features, left_side, right_side)


def branch_pair(mine, theirs):
    first = lax.axis_index("branch") == 0
    return jnp.where(first, jnp.concatenate([mine, theirs]), jnp.concatenate([theirs, mine]))


def gather_sides(left_side, right_side):
    swap = [(0, 1), (1, 0)]
    left_pair = branch_pair(left_side, lax.ppermute(left_side, "branch", swap))
    left_gathered = lax.all_to_all(left_pair, "rows", split_axis=1, concat_axis=0, tiled=True)
    half = right_side.shape[2] // 2
    me = lax.axis_index("branch")
    keep = lax.dynamic_slice_in_dim(right_side, me * half, half, axis=2)
    send = lax.dynamic_slice_in_dim(right_side, (1 - me) * half, half, axis=2)
    right_pair = branch_pair(keep, lax.ppermute(send, "branch", swap))
    right_gathered = lax.all_gather(jnp.swapaxes(right_pair, 0, 1), "rows", axis=1, tiled=True)
    return left_gathered, right_gathered


def send_whole(tri_stack):
    both = ("branch", "rows")
    moved = lax.all_to_all(tri_stack, both, split_axis=0, concat_axis=0, tiled=True)
    return moved


def send_back(product):
    return lax.all_to_all(product, ("branch", "rows"), split_axis=0, concat_axis=0, tiled=True)


def logistic(values):
    return 0.5 * jnp.tanh(0.5 * values) + 0.5


def front_kernel(pair_ref, w_ref, out_ref, norm_ref):
    tile_rows, columns, chans = pair_ref.shape
    block = out_ref.shape[0]

    @pl.when(pl.program_id(0) == 0)
    def _():
        for r in range(tile_rows):
            norm_ref[r] = standardize_features(pair_ref[r].astype(jnp.float32), -1).astype(
                norm_ref.dtype
            )

    weight = w_ref[...].reshape(4 * block, chans)
    for r in range(tile_rows):
        proj = lax.dot_general(
            weight, norm_ref[r], (((1,), (1,)), ((), ())), preferred_element_type=jnp.float32
        )
        out_ref[:, 0, r, :] = (
            logistic(proj[block : 2 * block]) * proj[:block]
        ).astype(out_ref.dtype)
        out_ref[:, 1, r, :] = (
            logistic(proj[3 * block :]) * proj[2 * block : 3 * block]
        ).astype(out_ref.dtype)


def pair_front(pairwise_input, triangle_projection_weight):
    tile_rows, columns, chans = pairwise_input.shape
    block = 32
    weight = triangle_projection_weight[:, : 4 * chans].T.reshape(4, chans, chans)
    return pl.pallas_call(
        front_kernel,
        out_shape=jax.ShapeDtypeStruct((chans, 2, tile_rows, columns), jnp.bfloat16),
        grid=(chans // block,),
        in_specs=[
            pl.BlockSpec((tile_rows, columns, chans), lambda g: (0, 0, 0)),
            pl.BlockSpec((4, block, chans), lambda g: (0, g, 0)),
        ],
        out_specs=pl.BlockSpec((block, 2, tile_rows, columns), lambda g: (g, 0, 0, 0)),
        scratch_shapes=[pltpu.VMEM((tile_rows, columns, chans), jnp.bfloat16)],
        cost_estimate=pl.CostEstimate(
            flops=2 * tile_rows * columns * chans * 4 * chans,
            transcendentals=2 * tile_rows * columns * chans,
            bytes_accessed=tile_rows * columns * chans * 6,
        ),
    )(pairwise_input, weight)


def product_kernel(moved_ref, out_ref):
    _, span, columns = out_ref.shape
    n_src, _, tile_rows, _ = moved_ref.shape
    halves = pl.num_programs(0)
    h = pl.program_id(0)
    per_half = n_src // 2
    per_out = per_half // 2
    if True:
        total = None
        for b in range(2):
            left = moved_ref[b * per_half : (b + 1) * per_half, 0]
            first = pl.multiple_of(b * per_half + h * per_out, per_out)
            right = moved_ref[pl.ds(first, per_out), 1]
            part = lax.dot_general(
                left.reshape(per_half * tile_rows, columns),
                right.reshape(per_out * tile_rows, columns),
                (((1,), (1,)), ((), ())),
                preferred_element_type=jnp.float32,
            )
            total = part if total is None else total + part
        out_ref[0] = total.astype(out_ref.dtype)


def triangle_product(moved):
    n_src, _, tile_rows, columns = moved.shape
    halves = lax.axis_size("branch")
    product = pl.pallas_call(
        product_kernel,
        out_shape=jax.ShapeDtypeStruct((halves, n_src * tile_rows // halves, columns), jnp.bfloat16),
        grid=(halves,),
        in_specs=[pl.BlockSpec(memory_space=pltpu.VMEM)],
        out_specs=pl.BlockSpec(
            (1, n_src * tile_rows // halves, columns), lambda h: (h, 0, 0)
        ),
        cost_estimate=pl.CostEstimate(
            flops=2 * (n_src * tile_rows) ** 2 * columns // halves,
            transcendentals=0,
            bytes_accessed=moved.size * 2 + n_src * tile_rows * columns * 2,
        ),
    )(moved)
    return product.reshape(-1, tile_rows, columns)


def back_kernel(prod_ref, pair_ref, outer_ref, wo_ref, wg_ref, wu_ref, wd_ref, out_ref):
    rows, columns, chans = pair_ref.shape
    for r in range(rows):
        prod = prod_ref[:, r * columns : (r + 1) * columns].astype(jnp.float32)
        prod_norm = standardize_features(prod, 0).T.astype(jnp.bfloat16)
        tri_update = jnp.dot(prod_norm, wo_ref[...], preferred_element_type=jnp.float32)
        pair_float = pair_ref[r].astype(jnp.float32)
        pair_norm = standardize_features(pair_float, -1).astype(jnp.bfloat16)
        gate = logistic(
            jnp.dot(pair_norm, wg_ref[...], preferred_element_type=jnp.float32)
        )
        pair_mid = pair_float + gate * tri_update
        mid_norm = standardize_features(pair_mid, -1).astype(jnp.bfloat16)
        hidden = jnp.maximum(
            jnp.dot(mid_norm, wu_ref[...], preferred_element_type=jnp.float32), 0.0
        ).astype(jnp.bfloat16)
        down = jnp.dot(hidden, wd_ref[...], preferred_element_type=jnp.float32)
        out_ref[r] = (pair_mid + down + outer_ref[r]).astype(out_ref.dtype)


def pair_back(
    pairwise_input,
    product_tile,
    outer_update,
    triangle_projection_weight,
    triangle_output_weight,
    pairwise_up_weight,
    pairwise_down_weight,
):
    tile_rows, columns, chans = pairwise_input.shape
    step_rows = 4
    prod_flat = product_tile.reshape(chans, tile_rows * columns)
    gate_weight = triangle_projection_weight
    hidden = pairwise_up_weight.shape[1]
    row_block = lambda g: (g, 0, 0)
    fixed = lambda g: (0, 0)
    return pl.pallas_call(
        back_kernel,
        out_shape=jax.ShapeDtypeStruct((tile_rows, columns, chans), jnp.bfloat16),
        grid=(tile_rows // step_rows,),
        in_specs=[
            pl.BlockSpec((chans, step_rows * columns), lambda g: (0, g)),
            pl.BlockSpec((step_rows, columns, chans), row_block),
            pl.BlockSpec((step_rows, columns, chans), row_block),
            pl.BlockSpec((chans, chans), fixed),
            pl.BlockSpec((chans, chans), fixed),
            pl.BlockSpec((chans, hidden), fixed),
            pl.BlockSpec((hidden, chans), fixed),
        ],
        out_specs=pl.BlockSpec((step_rows, columns, chans), row_block),
        cost_estimate=pl.CostEstimate(
            flops=2 * tile_rows * columns * chans * (3 * chans + 2 * hidden) // 1,
            transcendentals=tile_rows * columns * chans,
            bytes_accessed=tile_rows * columns * chans * 10,
        ),
    )(
        prod_flat,
        pairwise_input,
        outer_update,
        triangle_output_weight,
        gate_weight,
        pairwise_up_weight,
        pairwise_down_weight,
    )


def outer_kernel(lt_ref, r_ref, wt_ref, out_ref, x_ref):
    n_factor = r_ref.shape[0]
    tile_rows = out_ref.shape[0]
    scale = 1.0 / r_ref.shape[1]

    def fill(d, carry):
        vals = jnp.dot(lt_ref[...], r_ref[d], preferred_element_type=jnp.float32)
        vals = (vals * scale).astype(jnp.bfloat16)
        start = pl.multiple_of(d * n_factor, n_factor)
        for i in range(tile_rows):
            x_ref[i, pl.ds(start, n_factor), :] = vals[i * n_factor : (i + 1) * n_factor, :]
        return carry

    lax.fori_loop(0, n_factor, fill, 0)

    def emit(i, carry):
        upd = jnp.dot(wt_ref[...], x_ref[i], preferred_element_type=jnp.float32)
        out_ref[i] = upd.T
        return carry

    lax.fori_loop(0, tile_rows, emit, 0)


def outer_operands(left_gathered, outer_output_weight):
    total_rows, tile_rows, channels = left_gathered.shape
    pair = outer_output_weight.shape[1]
    left_t = jnp.transpose(left_gathered, (1, 2, 0)).reshape(tile_rows * channels, total_rows)
    weight_t = jnp.transpose(
        outer_output_weight.reshape(channels, channels, pair), (1, 0, 2)
    ).reshape(channels * channels, pair).T
    return left_t, weight_t


def outer_product(left_t, right_gathered, weight_t, tile_rows):
    channels = left_t.shape[0] // tile_rows
    total_rows = left_t.shape[1]
    columns = right_gathered.shape[2]
    pair = weight_t.shape[0]
    flops = 4 * tile_rows * channels * channels * columns * (total_rows + pair) // 2
    return pl.pallas_call(
        outer_kernel,
        out_shape=jax.ShapeDtypeStruct((tile_rows, columns, pair), jnp.float32),
        in_specs=[pl.BlockSpec(memory_space=pltpu.VMEM)] * 3,
        out_specs=pl.BlockSpec(memory_space=pltpu.VMEM),
        scratch_shapes=[pltpu.VMEM((tile_rows, channels * channels, columns), jnp.bfloat16)],
        compiler_params=pltpu.CompilerParams(vmem_limit_bytes=56 * 1024 * 1024),
        cost_estimate=pl.CostEstimate(
            flops=flops, transcendentals=0, bytes_accessed=right_gathered.size * 2 + tile_rows * columns * pair * 4
        ),
    )(left_t, right_gathered, weight_t)


def on_device(
    homolog_features,
    pairwise_input,
    transition_expand_matrix,
    transition_contract_matrix,
    factor_pair_matrices,
    outer_output_weight,
    triangle_projection_weight,
    triangle_output_weight,
    pairwise_up_weight,
    pairwise_down_weight,
):
    refreshed_homolog_features, left_side, right_side = alignment_branch(
        homolog_features, transition_expand_matrix, transition_contract_matrix, factor_pair_matrices
    )
    left_gathered, right_gathered = gather_sides(left_side, right_side)
    pairwise_input, right_side = lax.optimization_barrier((pairwise_input, right_side))
    tri_stack = pair_front(pairwise_input, triangle_projection_weight)
    moved = send_whole(tri_stack)
    product = triangle_product(moved)
    left_t, weight_t = outer_operands(left_gathered, outer_output_weight)
    gate_weight = triangle_projection_weight[:, 4 * pairwise_input.shape[2] :]
    product, left_t, weight_t, gate_weight = lax.optimization_barrier(
        (product, left_t, weight_t, gate_weight)
    )
    product_tile = send_back(product)
    outer_update = outer_product(left_t, right_gathered, weight_t, pairwise_input.shape[0])
    product_tile, outer_update = lax.optimization_barrier((product_tile, outer_update))
    pairwise_output = pair_back(
        pairwise_input,
        product_tile,
        outer_update,
        gate_weight,
        triangle_output_weight,
        pairwise_up_weight,
        pairwise_down_weight,
    )
    return (refreshed_homolog_features, pairwise_output)


def solution(mesh):
    return jax.shard_map(
        on_device,
        mesh=mesh,
        in_specs=(
            P(("branch", "rows"), None, None),
            P("rows", "branch", None),
            P(),
            P(),
            P(),
            P(),
            P(),
            P(),
            P(),
            P(),
        ),
        out_specs=(P(("branch", "rows"), None, None), P("rows", "branch", None)),
        check_vma=False,
    )
```
